32 devices in a mesh: group: 2 (over x), chan: 4 (over y, core), tensor: 4 (over z).
Axes of the slice: x: 2, y: 2, z: 4, core: 2. Of those that a mesh axis runs over, the one named last changes fastest.
Arguments:
- tokens: bfloat16 [100, 256, 4096], P('chan', 'group'), parts along dimension 1, may hold values from -6 to 6
- chan_table: int32 [100], replicated, may hold values from -1 to 90, as said below
- chan_valid: int32 [91], replicated, may hold values from 0 to 1, as said below
- chan_embed: bfloat16 [91, 4096], replicated, may hold values from -3 to 3
- query: float32 [4096], P('tensor')
- w_key: bfloat16 [4096, 4096], P('chan', 'tensor'), may hold values from -0.09375 to 0.09375
- w_value: bfloat16 [4096, 4096], P('chan', 'tensor'), may hold values from -0.09375 to 0.09375
- w_out: bfloat16 [4096, 4096], P('tensor', 'chan'), may hold values from -0.09375 to 0.09375
- ln_gain: float32 [4096], replicated, may hold values from 0.25 to 1.75
- w_up: bfloat16 [4096, 16384], P(None, ('chan', 'tensor')), may hold values from -0.09375 to 0.09375
- w_down: bfloat16 [16384, 4096], P(('chan', 'tensor')), may hold values from -0.046875 to 0.046875
Outputs:
- mixed: bfloat16 [256, 4096], P(('group', 'tensor'), 'chan'), parts along dimension 0
The draws below stay inside these ranges and needn't reach their ends.
There are 2 independent parts, one for each index of `group`. The reference program is written for one: setup_inputs(seed, part) draws one part's arguments, and reference() takes and returns one part's arrays. A program takes and returns all parts, laid end to end along the dimension named above; an argument that names none is the same for every part. Nothing has to cross between parts.
Inputs may be any that keep to these rules, and one draw needn't show every extreme that they name: `chan_table`: each of the 91 channels stands in exactly one slot, -1 marks an empty slot, and in every draw some index of chan has all 25 of its slots filled. `chan_valid`: at least one channel is valid.
All inputs are finite; a program needn't handle non-finite values.
Results may differ from the reference program's by a relative error of at most 0.02.
Values may be sent and summed in bfloat16 or wider, within the bound.
No kernel may reach another device: no remote copies, remote signals or barrier semaphores. Data moves between devices by JAX's collectives and lax.ppermute only.
A program may use at most 256 MiB of HBM per device.

```python
import jax
import jax.numpy as jnp
from jax import lax

D = 4096
HEADS = 32
HEAD_DIM = 128
HID = 16384
NCH = 91
PATCH = 128
SLOT_DEV = 25
SLOTS = 100
N_CHAN = 4


def draw_chan_table(key, part):
    slot_total = SLOT_DEV * N_CHAN
    order_key, level_key, full_key, label_key = jax.random.split(jax.random.fold_in(key, 11), 4)
    slot_order = jax.random.permutation(order_key, slot_total).astype(jnp.int32)
    levels = jax.random.randint(level_key, (N_CHAN,), 0, 3).astype(jnp.int32)
    full_device = jax.random.randint(full_key, (), 0, N_CHAN).astype(jnp.int32)
    levels = jnp.where(jnp.arange(N_CHAN, dtype=jnp.int32) == full_device, 4, levels).astype(jnp.int32)
    owners = jnp.arange(slot_total, dtype=jnp.int32) // SLOT_DEV
    priority = slot_order + slot_total * levels[owners]
    unused, chosen = lax.top_k(priority, NCH)
    labels = jax.random.permutation(label_key, NCH).astype(jnp.int32)
    return jnp.full((slot_total,), -1, jnp.int32).at[chosen].set(labels)


def draw_chan_valid(key, part):
    coin_key, keep_key = jax.random.split(jax.random.fold_in(key, 23))
    coins = jax.random.randint(coin_key, (NCH,), 0, 4)
    kept = jax.random.randint(keep_key, (), 0, NCH)
    chosen = (coins > 0) | (jnp.arange(NCH, dtype=jnp.int32) == kept)
    return jnp.where(chosen, 1, 0).astype(jnp.int32)


def draw_query(key, part):
    base_key = jax.random.fold_in(jax.random.fold_in(key, 37), 0)
    base = jnp.clip(jax.random.normal(base_key, (D,), jnp.float32), -5.0, 5.0)
    return base


def steps_of(own_key, shape, cuts, least, high):
    def one(position, shards_of):
        heights = jax.random.uniform(jax.random.fold_in(jax.random.fold_in(own_key, 6), position), (shards_of,), jnp.float32, least / len(cuts), high / len(cuts))
        return jnp.repeat(jnp.exp(heights), shape[position] // shards_of).reshape((-1,) + (1,) * (len(shape) - position - 1))

    loudness = one(*cuts[0])
    for cut in cuts[1:]:
        loudness = loudness * one(*cut)
    return loudness


def scatter_about(rng, shape, spread, reach, cuts=(), kind=jnp.bfloat16):
    array = jax.random.normal(rng, shape, jnp.float32) * spread
    if len(cuts) > 0:
        array = steps_of(rng, shape, cuts, -0.22, 0.18) * array
    return jnp.clip(array, min=-reach, max=reach).astype(kind)


def setup_inputs(seed: int = 0, part: int = 0) -> dict:
    key_of = jax.random.split(jax.random.key(seed), 12)
    part_splits = jax.random.split(jax.random.fold_in(key_of[11], part), 12)
    return {
        "tokens": scatter_about(part_splits[0], (SLOTS, PATCH, D), 1.0, 6.0, ((0, 4),)),
        "chan_table": draw_chan_table(jax.random.fold_in(key_of[11], 71), part),
        "chan_valid": draw_chan_valid(jax.random.fold_in(key_of[11], 71), part),
        "chan_embed": scatter_about(key_of[3], (NCH, D), 0.5, 3.0),
        "query": draw_query(jax.random.fold_in(key_of[11], 71), part),
        "w_key": scatter_about(key_of[5], (D, D), D ** -0.5, 0.09375, ((0, 4), (1, 4))),
        "w_value": scatter_about(key_of[6], (D, D), D ** -0.5, 0.09375, ((0, 4), (1, 4))),
        "w_out": scatter_about(key_of[7], (D, D), D ** -0.5, 0.09375, ((0, 4), (1, 4))),
        "ln_gain": jnp.clip(1.0 + 0.15 * jax.random.normal(key_of[8], (D,), jnp.float32), 0.25, 1.75),
        "w_up": scatter_about(key_of[9], (D, HID), D ** -0.5, 0.09375, ((1, 16),)),
        "w_down": scatter_about(key_of[10], (HID, D), HID ** -0.5, 0.046875, ((0, 16),)),
    }


def layer_norm(rows_in, ln_gain):
    row_mean = lax.optimization_barrier(jnp.mean(rows_in, axis=-1, keepdims=True))
    centered = rows_in - row_mean
    variance = lax.optimization_barrier(jnp.mean(centered * centered, axis=-1, keepdims=True))
    return (centered * lax.rsqrt(variance + 1e-05) * ln_gain).astype(jnp.bfloat16)

def reference(tokens, chan_table, chan_valid, chan_embed, query, w_key, w_value, w_out, ln_gain, w_up, w_down):
    present = chan_table >= 0
    safe_ids = jnp.where(present, chan_table, 0).astype(jnp.int32)
    live_slots = present & (chan_valid[safe_ids] == 1)
    added = jnp.where(present[:, None], chan_embed[safe_ids].astype(jnp.float32), jnp.float32(0.0))
    embedded = (tokens.astype(jnp.float32) + added[:, None, :]).astype(jnp.bfloat16)
    emb_wide = embedded.astype(jnp.float32)
    query_heads = query.astype(jnp.float32).reshape(HEADS, HEAD_DIM)
    key_cube = w_key.astype(jnp.float32).reshape(D, HEADS, HEAD_DIM)
    key_vectors = jnp.einsum('dhk,hk->dh', key_cube, query_heads, precision=lax.Precision.HIGHEST)
    key_vectors = key_vectors / jnp.sqrt(jnp.float32(HEAD_DIM))
    scores = jnp.einsum('spd,dh->sph', emb_wide, key_vectors, precision=lax.Precision.HIGHEST)
    masked = jnp.where(live_slots[:, None, None], scores, jnp.float32(-1e+30))
    top_score = lax.optimization_barrier(jnp.max(masked, axis=0))
    weights = jnp.where(live_slots[:, None, None], jnp.exp(masked - top_score[None]), jnp.float32(0.0))
    weight_sum = lax.optimization_barrier(jnp.sum(weights, axis=0))
    pooled = jnp.einsum('sph,spd->phd', weights, emb_wide, precision=lax.Precision.HIGHEST)
    value_cube = w_value.astype(jnp.float32).reshape(D, HEADS, HEAD_DIM)
    attended = jnp.einsum('phd,dhk->phk', pooled, value_cube, precision=lax.Precision.HIGHEST)
    attended = (attended / weight_sum[:, :, None]).reshape(PATCH, D).astype(jnp.bfloat16)
    projected = jnp.dot(attended, w_out, preferred_element_type=jnp.float32)
    normed = layer_norm(projected, ln_gain)
    hidden = jax.nn.gelu(jnp.dot(normed, w_up, preferred_element_type=jnp.float32)).astype(jnp.bfloat16)
    return (projected + jnp.dot(hidden, w_down, preferred_element_type=jnp.float32)).astype(jnp.bfloat16)
```

```python
import functools

import jax
import jax.numpy as jnp
from jax import lax
from jax.experimental import pallas as pl
from jax.experimental.pallas import tpu as pltpu
from jax.sharding import Mesh, PartitionSpec as P

HEAD_DIM = 128
BLOCK = 16
LANES = 128
NEG = -1e30
F32 = jnp.float32
BF16 = jnp.bfloat16
NT = (((1,), (1,)), ((), ()))
MIB = 1 << 20


def swap(x, axis, bit=1):
    size = lax.axis_size(axis)
    return lax.ppermute(x, axis, [(i, i ^ bit) for i in range(size)])


def bits_of(axis):
    size, bit, found = lax.axis_size(axis), 1, []
    while bit < size:
        found.append(bit)
        bit *= 2
    return found


def chan_swap(x, bit):
    return swap(x, "core", 1) if bit == 1 else swap(x, "y", bit // 2)


def split_parts(x, parts):
    out, rest = [], x
    for _ in range(parts):
        piece = rest.astype(BF16)
        out.append(piece)
        rest = rest - piece.astype(F32)
    return out


def pool_kernel(
    heads, chan_count, place, tokens, added, live, *rest
):
    key_refs = rest[:chan_count]
    pooled, top_out, sum_out, keys, add_scores, scores = rest[chan_count:]
    slots, block, width = tokens.shape
    rows = slots * block
    lanes = scores.shape[1]
    padded = added.shape[0]
    lane = lax.broadcasted_iota(jnp.int32, (padded, lanes), 1)
    slot = lax.broadcasted_iota(jnp.int32, (padded, lanes), 0)

    @pl.when(pl.program_id(0) == 0)
    def _():
        piece = width // chan_count
        for j in range(chan_count):
            at = pl.multiple_of(place[1 + j] * piece, piece)
            high, low = split_parts(key_refs[j][...], 2)
            keys[:, pl.ds(at, piece)] = jnp.concatenate([high, low], axis=0)
        raw = lax.dot_general(keys[...], added[...], NT, preferred_element_type=F32)
        raw = raw[:heads] + raw[heads:]
        spread = jnp.where(lane // block == slot, 1.0, 0.0).astype(BF16)
        total = jnp.zeros((heads, lanes), F32)
        for part in split_parts(raw, 3):
            total = total + jnp.dot(part, spread, preferred_element_type=F32)
        add_scores[...] = total
        scores[...] = jnp.zeros_like(scores)

    flat = tokens[...].reshape(rows, width)
    raw = lax.dot_general(keys[...], flat, NT, preferred_element_type=F32)
    scores[:, :rows] = raw[:heads] + raw[heads:]
    alive = live[...] > 0.0
    masked = jnp.where(alive, scores[...] + add_scores[...], NEG)
    groups = lanes // LANES
    top = masked[:, :LANES]
    for g in range(1, groups):
        top = jnp.maximum(top, masked[:, g * LANES : (g + 1) * LANES])
    shift = LANES // 2
    while shift >= block:
        top = jnp.maximum(top, pltpu.roll(top, shift, 1))
        shift //= 2
    wide_top = jnp.concatenate([top] * groups, axis=1)
    weights = jnp.where(alive, jnp.exp(masked - wide_top), 0.0)
    weights = weights.astype(BF16).astype(F32)
    total = weights[:, :LANES]
    for g in range(1, groups):
        total = total + weights[:, g * LANES : (g + 1) * LANES]
    shift = LANES // 2
    while shift >= block:
        total = total + pltpu.roll(total, shift, 1)
        shift //= 2
    top_out[0] = top
    sum_out[0] = total

    patch = lax.broadcasted_iota(jnp.int32, (heads, block, lanes), 1)
    column = lax.broadcasted_iota(jnp.int32, (heads, block, lanes), 2)
    spread = jnp.where(
        column % block == patch, jnp.broadcast_to(weights[:, None, :], patch.shape), 0.0
    )
    spread = spread.reshape(heads * block, lanes).astype(BF16)
    pick = jnp.where(
        lax.broadcasted_iota(jnp.int32, (lanes, padded), 0) // block
        == lax.broadcasted_iota(jnp.int32, (lanes, padded), 1),
        1.0,
        0.0,
    ).astype(BF16)
    by_slot = jnp.dot(spread, pick, preferred_element_type=F32).astype(BF16)
    step = min(width, 1024)
    for at in range(0, width, step):
        part = tokens[:, :, at : at + step].reshape(rows, step)
        got = jnp.dot(spread[:, :rows], part, preferred_element_type=F32)
        got = got + jnp.dot(by_slot, added[:, at : at + step], preferred_element_type=F32)
        pooled[:, :, at : at + step] = got.reshape(heads, block, step).astype(BF16)


def pool_tokens(tokens, added, live, key_parts, place, heads, rows_own):
    slots, patches, width = tokens.shape
    chan_count = len(key_parts)
    per_owner = max(rows_own // BLOCK, 1)
    lanes = live.shape[1]
    blocks = patches // BLOCK

    def block_at(i, place):
        return (0, ((i // per_owner) ^ place[0]) * per_owner + i % per_owner, 0)

    whole = lambda i, place: (0, 0)
    return pl.pallas_call(
        functools.partial(pool_kernel, heads, chan_count),
        out_shape=(
            jax.ShapeDtypeStruct((heads, patches, width), BF16),
            jax.ShapeDtypeStruct((blocks, heads, LANES), F32),
            jax.ShapeDtypeStruct((blocks, heads, LANES), F32),
        ),
        grid_spec=pltpu.PrefetchScalarGridSpec(
            num_scalar_prefetch=1,
            grid=(blocks,),
            in_specs=[
                pl.BlockSpec((slots, BLOCK, width), block_at),
                pl.BlockSpec(added.shape, whole),
                pl.BlockSpec(live.shape, whole),
            ]
            + [pl.BlockSpec(k.shape, whole) for k in key_parts],
            out_specs=(
                pl.BlockSpec((heads, BLOCK, width), lambda i, place: (0, i, 0)),
                pl.BlockSpec((1, heads, LANES), lambda i, place: (i, 0, 0)),
                pl.BlockSpec((1, heads, LANES), lambda i, place: (i, 0, 0)),
            ),
            scratch_shapes=[
                pltpu.VMEM((2 * heads, width), BF16),
                pltpu.VMEM((heads, lanes), F32),
                pltpu.VMEM((heads, lanes), F32),
            ],
        ),
        compiler_params=pltpu.CompilerParams(vmem_limit_bytes=40 * MIB),
        name="pool_tokens",
    )(place, tokens, added, live, *key_parts)


def value_kernel(piece_count, has_start, has_factor, offsets, pooled, *rest):
    pieces = rest[:piece_count]
    rest = rest[piece_count:]
    total = None
    for n, piece in enumerate(pieces):
        depth = piece.shape[0]
        at = pl.multiple_of(offsets[n] * depth, depth)
        got = jnp.dot(pooled[0, :, pl.ds(at, depth)], piece[...], preferred_element_type=F32)
        total = got if total is None else total + got
    if has_start:
        total = total + rest[0][...]
        rest = rest[1:]
    if has_factor:
        total = total * rest[0][0]
        rest = rest[1:]
    rest[0][...] = total.astype(rest[0].dtype)


def value_products(pooled, pieces, offsets, first_head, head_count, start, factor, kind):
    heads, patches, width = pooled.shape
    operands, specs = [pooled], [
        pl.BlockSpec((1, patches, width), lambda h, o: (first_head + h, 0, 0))
    ]
    for piece, from_head in pieces:
        specs.append(
            pl.BlockSpec(
                (piece.shape[0], HEAD_DIM), lambda h, o, from_head=from_head: (0, from_head + h)
            )
        )
        operands.append(piece)
    if start is not None:
        specs.append(pl.BlockSpec((patches, HEAD_DIM), lambda h, o: (0, first_head + h)))
        operands.append(start)
    if factor is not None:
        specs.append(pl.BlockSpec((1, patches, HEAD_DIM), lambda h, o: (first_head + h, 0, 0)))
        operands.append(factor)
    return pl.pallas_call(
        functools.partial(value_kernel, len(pieces), start is not None, factor is not None),
        out_shape=jax.ShapeDtypeStruct((patches, head_count * HEAD_DIM), kind),
        grid_spec=pltpu.PrefetchScalarGridSpec(
            num_scalar_prefetch=1,
            grid=(head_count,),
            in_specs=specs,
            out_specs=pl.BlockSpec((patches, HEAD_DIM), lambda h, o: (0, h)),
        ),
        compiler_params=pltpu.CompilerParams(vmem_limit_bytes=40 * MIB),
        name="value_products",
    )(offsets, *operands)


def mlp_kernel(count, order, x, gain, w_up, w_down, out, normed, total, hidden):
    i = pl.program_id(0)
    patches, piece = x.shape[1:]
    width = count * piece

    @pl.when(i == 0)
    def _():
        mean = jnp.zeros((patches, 1), F32)
        for j in range(count):
            mean = mean + jnp.sum(x[j].astype(F32), axis=1, keepdims=True)
        mean = mean / width
        variance = jnp.zeros((patches, 1), F32)
        for j in range(count):
            centered = x[j].astype(F32) - mean
            variance = variance + jnp.sum(centered * centered, axis=1, keepdims=True)
        scale = lax.rsqrt(variance / width + 1e-05)
        for j in range(count):
            rows_gain = gain[order[j]]
            normed[j] = ((x[j].astype(F32) - mean) * scale * rows_gain).astype(BF16)
        total[...] = jnp.zeros_like(total)

    @pl.when(i < count)
    def _():
        total[...] += jnp.dot(normed[i], w_up[...], preferred_element_type=F32)

    @pl.when(i == count - 1)
    def _():
        hidden[...] = jax.nn.gelu(total[...]).astype(BF16)

    @pl.when(i >= count)
    def _():
        out[0] = jnp.dot(hidden[...], w_down[...], preferred_element_type=F32).astype(BF16)


def mlp(x, order, ln_gain, w_up, w_down):
    count, patches, piece = x.shape
    units = w_up.shape[1]
    last = count - 1
    return pl.pallas_call(
        functools.partial(mlp_kernel, count),
        out_shape=jax.ShapeDtypeStruct((count, patches, piece), BF16),
        grid_spec=pltpu.PrefetchScalarGridSpec(
            num_scalar_prefetch=1,
            grid=(2 * count,),
            in_specs=[
                pl.BlockSpec(x.shape, lambda i, o: (0, 0, 0)),
                pl.BlockSpec((count, 1, piece), lambda i, o: (0, 0, 0)),
                pl.BlockSpec((piece, units), lambda i, o: (o[jnp.minimum(i, last)], 0)),
                pl.BlockSpec((units, piece), lambda i, o: (0, o[jnp.maximum(i - count, 0)])),
            ],
            out_specs=pl.BlockSpec(
                (1, patches, piece), lambda i, o: (jnp.maximum(i - count, 0), 0, 0)
            ),
            scratch_shapes=[
                pltpu.VMEM((count, patches, piece), BF16),
                pltpu.VMEM((patches, units), F32),
                pltpu.VMEM((patches, units), BF16),
            ],
        ),
        compiler_params=pltpu.CompilerParams(vmem_limit_bytes=40 * MIB),
        name="norm_mlp",
    )(order, x, ln_gain.reshape(count, 1, piece), w_up, w_down)


def key_vectors(query, w_key, heads):
    columns = query.shape[0]
    mine = jnp.arange(columns)[None, :] // HEAD_DIM == jnp.arange(heads)[:, None]
    rows = [jnp.where(mine, part[None, :], 0) for part in split_parts(query, 3)]
    stacked = jnp.concatenate(rows, axis=0).astype(BF16)
    got = lax.dot_general(stacked, w_key, NT, preferred_element_type=F32)
    scale = 1.0 / jnp.sqrt(F32(HEAD_DIM))
    return (got.reshape(3, heads, -1).sum(axis=0)) * scale


def add_up(*terms):
    total = terms[0].astype(F32)
    for term in terms[1:]:
        total = total + term.astype(F32)
    return total


def local(
    tokens, chan_table, chan_valid, chan_embed, query, w_key, w_value, w_out, ln_gain, w_up, w_down
):
    slots, patches, width = tokens.shape
    columns = query.shape[0]
    heads = columns // HEAD_DIM
    group, tensor = lax.axis_index("group"), lax.axis_index("tensor")
    tensors = lax.axis_size("tensor")
    chan = lax.axis_index(("y", "core"))
    chans = lax.axis_size("y") * lax.axis_size("core")
    chan_bits = [1] + [2 * b for b in bits_of("y")]
    tensor_bits = bits_of("tensor")
    rows_own = patches // tensors

    key_parts = key_vectors(query, w_key, heads)[None]
    key_order = [0]
    for bit in chan_bits:
        key_parts = jnp.concatenate([key_parts, chan_swap(key_parts, bit)], axis=0)
        key_order = key_order + [j ^ bit for j in key_order]
    key_place = chan ^ jnp.array(key_order, jnp.int32)
    place = jnp.concatenate([jnp.reshape(tensor, (1,)).astype(jnp.int32), key_place])

    piece_rows = w_value.shape[0]
    spread_groups = lax.axis_size("y") == 2 and lax.axis_size("group") == 2
    if spread_groups:
        half = piece_rows // 2
        mine = lax.dynamic_slice_in_dim(w_value, group * half, half, 0)
        chunks = 2
        chunk_cols = columns // chunks
        partner = swap(w_value, "core")
        late = []
        for k in range(chunks):
            first = swap(mine[:, k * chunk_cols : (k + 1) * chunk_cols], "y")
            second = swap(first, "group")
            both = jnp.stack([first, second])
            late.append((first, second, swap(first, "core"), swap(second, "core")))
        early = [(w_value, 0), (partner, 0)]
        early_offsets = jnp.stack([chan, chan ^ 1]).astype(jnp.int32)
        late_offsets = jnp.stack(
            [
                (chan ^ 2) * 2 + group,
                (chan ^ 2) * 2 + (1 - group),
                (chan ^ 3) * 2 + group,
                (chan ^ 3) * 2 + (1 - group),
            ]
        ).astype(jnp.int32)
    else:
        full = lax.all_gather(w_value, ("y", "core"), axis=0, tiled=True)

    padded = -(-slots // 16) * 16
    lanes = -(-(slots * BLOCK) // LANES) * LANES
    slot_ids = lax.dynamic_slice_in_dim(chan_table, chan * slots, slots)
    slot_ids = jnp.pad(slot_ids, (0, padded - slots), constant_values=-1)
    matches = slot_ids[:, None] == jnp.arange(chan_embed.shape[0], dtype=jnp.int32)[None, :]
    added = jnp.dot(matches.astype(BF16), chan_embed, preferred_element_type=F32).astype(BF16)
    live_slots = jnp.sum(matches.astype(jnp.int32) * chan_valid[None, :], axis=1) > 0
    live = jnp.repeat(live_slots.astype(F32), BLOCK)
    live = jnp.pad(live, (0, max(lanes - live.shape[0], 0)))[:lanes][None]

    pooled, tops, sums = pool_tokens(
        tokens, added, live, [key_parts[j] for j in range(chans)], place, heads, rows_own
    )
    top = tops[:, :, :BLOCK].transpose(1, 0, 2).reshape(heads, patches)
    weight_sum = sums[:, :, :BLOCK].transpose(1, 0, 2).reshape(heads, patches)
    stats = jnp.stack([top, weight_sum])[None]
    for bit in chan_bits:
        stats = jnp.concatenate([stats, chan_swap(stats, bit)], axis=0)
    best = jnp.max(stats[:, 0], axis=0)
    total = jnp.sum(stats[:, 1] * jnp.exp(stats[:, 0] - best[None]), axis=0)
    factor = jnp.exp(top - best) / total
    factor = jnp.broadcast_to(factor[:, :, None], (heads, patches, HEAD_DIM))

    if spread_groups:
        start = value_products(pooled, early, early_offsets, 0, heads, None, None, F32)
        parts = []
        for k in range(chunks):
            count = heads // chunks
            parts.append(
                value_products(
                    pooled,
                    [(piece, 0) for piece in late[k]],
                    late_offsets,
                    k * count,
                    count,
                    start,
                    factor,
                    BF16,
                )
            )
    else:
        parts = [
            value_products(
                pooled, [(full, 0)], jnp.zeros((1,), jnp.int32), 0, heads, None, factor, BF16
            )
        ]

    partial_value = None
    at = 0
    for part in parts:
        for bit in chan_bits:
            part = add_up(part, chan_swap(part, bit)).astype(BF16)
        got = jnp.dot(part, w_out[at : at + part.shape[1]], preferred_element_type=F32)
        at += part.shape[1]
        partial_value = got if partial_value is None else partial_value + got

    sent = partial_value.astype(BF16).reshape(tensors, rows_own, -1)
    projected = add_up(
        partial_value[:rows_own], *[swap(sent[k], "tensor", k) for k in range(1, tensors)]
    )
    own = projected.astype(BF16)
    rows = jnp.concatenate([own] + [swap(own, "tensor", k) for k in range(1, tensors)], axis=0)

    gathered, order = rows[None], [0]
    for bit in chan_bits[1:] + chan_bits[:1]:
        gathered = jnp.concatenate([gathered, chan_swap(gathered, bit)], axis=0)
        order = order + [j ^ bit for j in order]
    partial_out = mlp(gathered, chan ^ jnp.array(order, jnp.int32), ln_gain, w_up, w_down)

    held = {j: partial_out[n] for n, j in enumerate(order)}
    for bit in chan_bits:
        keep = sorted(j for j in held if not j & bit)
        send = jnp.stack([held[j ^ bit] for j in keep]).astype(BF16)
        got = chan_swap(send, bit)
        held = {j: add_up(held[j], got[n]).astype(BF16) for n, j in enumerate(keep)}
    sent = held[0].reshape(tensors, rows_own, -1)
    mixed = add_up(
        projected, sent[0], *[swap(sent[k], "tensor", k) for k in range(1, tensors)]
    )
    return mixed.astype(BF16)


def solution(mesh):
    groups, chans, tensors = (mesh.shape[a] for a in ("group", "chan", "tensor"))
    split = Mesh(
        mesh.devices.reshape(groups, chans // 2, 2, tensors), ("group", "y", "core", "tensor")
    )
    chan = ("y", "core")
    in_specs = (
        P(chan, "group", None),
        P(),
        P(),
        P(),
        P("tensor"),
        P(chan, "tensor"),
        P(chan, "tensor"),
        P("tensor", chan),
        P(),
        P(None, (*chan, "tensor")),
        P((*chan, "tensor"), None),
    )
    out_specs = P(("group", "tensor"), chan)
    return jax.shard_map(
        local, mesh=split, in_specs=in_specs, out_specs=out_specs, check_vma=False
    )
```

```python
import functools

import jax
import jax.numpy as jnp
from jax import lax
from jax.experimental import pallas as pl
from jax.experimental.pallas import tpu as pltpu
from jax.sharding import Mesh, PartitionSpec as P

HEAD_DIM = 128
BLOCK = 16
LANES = 128
NEG = -1e30
F32 = jnp.float32
BF16 = jnp.bfloat16
NT = (((1,), (1,)), ((), ()))
MIB = 1 << 20


def swap(x, axis, bit=1):
    size = lax.axis_size(axis)
    return lax.ppermute(x, axis, [(i, i ^ bit) for i in range(size)])


def bits_of(axis):
    size, bit, found = lax.axis_size(axis), 1, []
    while bit < size:
        found.append(bit)
        bit *= 2
    return found


def chan_swap(x, bit):
    return swap(x, "core", 1) if bit == 1 else swap(x, "y", bit // 2)


def split_parts(x, parts):
    out, rest = [], x
    for _ in range(parts):
        piece = rest.astype(BF16)
        out.append(piece)
        rest = rest - piece.astype(F32)
    return out


def pool_kernel(heads, chan_count, first, count, per_owner, place, tokens, added, live, *rest):
    key_refs = rest[:chan_count]
    pooled, top_out, sum_out = rest[chan_count : chan_count + 3]
    held, arrived, keys, add_scores, scores, spreads = rest[chan_count + 3 :]
    slots, _, width = tokens.shape
    block = held.shape[2]
    rows = slots * block
    lanes = scores.shape[1]
    groups = lanes // LANES
    padded = added.shape[0]

    def fetch(i):
        at = first + i
        row = (((at // per_owner) ^ place[0]) * per_owner + at % per_owner) * block
        return pltpu.make_async_copy(
            tokens.at[:, pl.ds(pl.multiple_of(row, block), block), :],
            held.at[i],
            arrived.at[i],
        )

    fetch(0).start()
    if count > 1:
        fetch(1).start()

    piece = width // chan_count
    for j in range(chan_count):
        at = pl.multiple_of(place[1 + j] * piece, piece)
        high, low = split_parts(key_refs[j][...], 2)
        keys[:, pl.ds(at, piece)] = jnp.concatenate([high, low], axis=0)
    raw = lax.dot_general(keys[...], added[...], NT, preferred_element_type=F32)
    raw = raw[:heads] + raw[heads:]
    lane = lax.broadcasted_iota(jnp.int32, (padded, lanes), 1)
    slot = lax.broadcasted_iota(jnp.int32, (padded, lanes), 0)
    expand = jnp.where(lane // block == slot, 1.0, 0.0).astype(BF16)
    total = jnp.zeros((heads, lanes), F32)
    for part in split_parts(raw, 3):
        total = total + jnp.dot(part, expand, preferred_element_type=F32)
    add_scores[...] = total
    scores[...] = jnp.zeros_like(scores)

    def fold(x, combine):
        out = x[:, :LANES]
        for g in range(1, groups):
            out = combine(out, x[:, g * LANES : (g + 1) * LANES])
        shift = LANES // 2
        while shift >= block:
            out = combine(out, pltpu.roll(out, shift, 1))
            shift //= 2
        return out

    step = min(width, 512)
    by_slot = None
    for i in range(count + 1):
        if i < count:
            fetch(i).wait()
            if i + 2 < count:
                fetch(i + 2).start()
        raw = None
        for at in range(0, width, step):
            if i < count:
                part = held[i, :, :, at : at + step].reshape(rows, step)
                got = lax.dot_general(
                    keys[:, at : at + step], part, NT, preferred_element_type=F32
                )
                raw = got if raw is None else raw + got
            if i > 0:
                part = held[i - 1, :, :, at : at + step].reshape(rows, step)
                got = jnp.dot(spreads[:, :rows], part, preferred_element_type=F32)
                got = got + jnp.dot(
                    by_slot, added[:, at : at + step], preferred_element_type=F32
                )
                pooled[:, (i - 1) * block : i * block, at : at + step] = got.reshape(
                    heads, block, step
                ).astype(BF16)
        if i == count:
            break
        scores[:, :rows] = raw[:heads] + raw[heads:]
        alive = live[...] > 0.0
        masked = jnp.where(alive, scores[...] + add_scores[...], NEG)
        top = fold(masked, jnp.maximum)
        wide_top = jnp.concatenate([top] * groups, axis=1)
        weights = jnp.where(alive, jnp.exp(masked - wide_top), 0.0)
        weights = weights.astype(BF16).astype(F32)
        top_out[i] = top
        sum_out[i] = fold(weights, jnp.add)
        patch = lax.broadcasted_iota(jnp.int32, (heads, block, lanes), 1)
        column = lax.broadcasted_iota(jnp.int32, (heads, block, lanes), 2)
        spread = jnp.where(
            column % block == patch, jnp.broadcast_to(weights[:, None, :], patch.shape), 0.0
        )
        spread = spread.reshape(heads * block, lanes).astype(BF16)
        spreads[...] = spread
        pick = jnp.where(
            lax.broadcasted_iota(jnp.int32, (lanes, padded), 0) // block
            == lax.broadcasted_iota(jnp.int32, (lanes, padded), 1),
            1.0,
            0.0,
        ).astype(BF16)
        by_slot = jnp.dot(spread, pick, preferred_element_type=F32).astype(BF16)


def pool_tokens(tokens, added, live, key_parts, place, heads, rows_own, first, count):
    slots, _, width = tokens.shape
    lanes = live.shape[1]
    vmem = pl.BlockSpec(memory_space=pltpu.VMEM)
    return pl.pallas_call(
        functools.partial(
            pool_kernel, heads, len(key_parts), first, count, max(rows_own // BLOCK, 1)
        ),
        out_shape=(
            pltpu.VMEM((heads, count * BLOCK, width), BF16),
            jax.ShapeDtypeStruct((count, heads, LANES), F32),
            jax.ShapeDtypeStruct((count, heads, LANES), F32),
        ),
        in_specs=[
            pl.BlockSpec(memory_space=pltpu.SMEM),
            pl.BlockSpec(memory_space=pl.ANY),
            vmem,
            vmem,
        ]
        + [vmem] * len(key_parts),
        out_specs=(vmem, vmem, vmem),
        scratch_shapes=[
            pltpu.VMEM((count, slots, BLOCK, width), BF16),
            pltpu.SemaphoreType.DMA((count,)),
            pltpu.VMEM((2 * heads, width), BF16),
            pltpu.VMEM((heads, lanes), F32),
            pltpu.VMEM((heads, lanes), F32),
            pltpu.VMEM((heads * BLOCK, lanes), BF16),
        ],
        compiler_params=pltpu.CompilerParams(vmem_limit_bytes=28 * MIB),
        name="pool_tokens",
    )(place, tokens, added, live, *key_parts)


def value_kernel(first, together, pool_count, piece_count, has_start, has_factor, offsets, *rest):
    pooled, rest = rest[:pool_count], rest[pool_count:]
    pieces, rest = rest[:piece_count], rest[piece_count:]
    head = (first + pl.program_id(0)) * together
    total = None
    for n, piece in enumerate(pieces):
        depth = piece.shape[0]
        at = pl.multiple_of(offsets[n], LANES)
        stacked = jnp.concatenate(
            [part[head + h, :, pl.ds(at, depth)] for h in range(together) for part in pooled],
            axis=0,
        )
        got = jnp.dot(stacked, piece[...], preferred_element_type=F32)
        total = got if total is None else total + got
    patches = total.shape[0] // together
    out = rest[-1]
    for h in range(together):
        columns = slice(h * HEAD_DIM, (h + 1) * HEAD_DIM)
        got = total[h * patches : (h + 1) * patches, columns]
        if has_start:
            got = got + rest[0][:, columns]
        if has_factor:
            got = got * rest[-2][h]
        out[:, columns] = got.astype(out.dtype)


def value_products(pooled, pieces, offsets, first_head, head_count, start, factor, kind):
    patches = sum(part.shape[1] for part in pooled)
    together = 2 if head_count % 2 == 0 else 1
    wide = together * HEAD_DIM
    first = first_head // together
    specs = [pl.BlockSpec(memory_space=pltpu.VMEM)] * len(pooled)
    operands = [pltpu.with_memory_space_constraint(part, pltpu.VMEM) for part in pooled]
    for piece in pieces:
        specs.append(pl.BlockSpec((piece.shape[0], wide), lambda h, o: (0, first + h)))
        operands.append(piece)
    if start is not None:
        specs.append(pl.BlockSpec((patches, wide), lambda h, o: (0, first + h)))
        operands.append(start)
    if factor is not None:
        specs.append(pl.BlockSpec((together, patches, HEAD_DIM), lambda h, o: (first + h, 0, 0)))
        operands.append(factor)
    return pl.pallas_call(
        functools.partial(
            value_kernel,
            first,
            together,
            len(pooled),
            len(pieces),
            start is not None,
            factor is not None,
        ),
        out_shape=jax.ShapeDtypeStruct((patches, head_count * HEAD_DIM), kind),
        grid_spec=pltpu.PrefetchScalarGridSpec(
            num_scalar_prefetch=1,
            grid=(head_count // together,),
            in_specs=specs,
            out_specs=pl.BlockSpec((patches, wide), lambda h, o: (0, h)),
        ),
        compiler_params=pltpu.CompilerParams(vmem_limit_bytes=16 * MIB),
        name="value_products",
    )(offsets, *operands)


def load_kernel(*refs):
    half = len(refs) // 2
    arrived = refs[-1]
    copies = [
        pltpu.make_async_copy(refs[i], refs[half + i], arrived.at[i]) for i in range(half)
    ]
    for copy in copies:
        copy.start()
    for copy in copies:
        copy.wait()


def load_weights(*weights):
    return pl.pallas_call(
        load_kernel,
        out_shape=[pltpu.VMEM(w.shape, w.dtype) for w in weights],
        in_specs=[pl.BlockSpec(memory_space=pl.ANY)] * len(weights),
        out_specs=[pl.BlockSpec(memory_space=pltpu.VMEM)] * len(weights),
        scratch_shapes=[pltpu.SemaphoreType.DMA((len(weights),))],
        cost_estimate=pl.CostEstimate(
            flops=0, transcendentals=0, bytes_accessed=sum(w.size * 2 for w in weights)
        ),
        compiler_params=pltpu.CompilerParams(vmem_limit_bytes=MIB),
        name="load_weights",
    )(*[pltpu.with_memory_space_constraint(w, pltpu.HBM) for w in weights])


def mlp_kernel(count, order, x, gain, w_up, w_down, out, normed):
    patches, piece = x.shape[1:]
    width = count * piece
    mean = jnp.zeros((patches, 1), F32)
    for j in range(count):
        mean = mean + jnp.sum(x[j].astype(F32), axis=1, keepdims=True)
    mean = mean / width
    variance = jnp.zeros((patches, 1), F32)
    for j in range(count):
        centered = x[j].astype(F32) - mean
        variance = variance + jnp.sum(centered * centered, axis=1, keepdims=True)
    scale = lax.rsqrt(variance / width + 1e-05)
    for j in range(count):
        normed[j] = ((x[j].astype(F32) - mean) * scale * gain[order[j]]).astype(BF16)
    total = None
    for j in range(count):
        at = pl.multiple_of(order[j] * piece, piece)
        got = jnp.dot(normed[j], w_up[pl.ds(at, piece), :], preferred_element_type=F32)
        total = got if total is None else total + got
    hidden = jax.nn.gelu(total).astype(BF16)
    for j in range(count):
        at = pl.multiple_of(order[j] * piece, piece)
        got = jnp.dot(hidden, w_down[:, pl.ds(at, piece)], preferred_element_type=F32)
        out[j] = got.astype(BF16)


def mlp(x, order, ln_gain, w_up, w_down):
    count, patches, piece = x.shape
    vmem = pl.BlockSpec(memory_space=pltpu.VMEM)
    w_up, w_down = (pltpu.with_memory_space_constraint(w, pltpu.VMEM) for w in (w_up, w_down))
    return pl.pallas_call(
        functools.partial(mlp_kernel, count),
        out_shape=jax.ShapeDtypeStruct((count, patches, piece), BF16),
        in_specs=[pl.BlockSpec(memory_space=pltpu.SMEM)] + [vmem] * 4,
        out_specs=vmem,
        scratch_shapes=[pltpu.VMEM((count, patches, piece), BF16)],
        compiler_params=pltpu.CompilerParams(vmem_limit_bytes=18 * MIB),
        name="norm_mlp",
    )(order, x, ln_gain.reshape(count, 1, piece), w_up, w_down)


def key_vectors(query, w_key, heads):
    columns = query.shape[0]
    mine = jnp.arange(columns)[None, :] // HEAD_DIM == jnp.arange(heads)[:, None]
    rows = [jnp.where(mine, part[None, :], 0) for part in split_parts(query, 3)]
    stacked = jnp.concatenate(rows, axis=0).astype(BF16)
    got = lax.dot_general(stacked, w_key, NT, preferred_element_type=F32)
    scale = 1.0 / jnp.sqrt(F32(HEAD_DIM))
    return (got.reshape(3, heads, -1).sum(axis=0)) * scale


def add_up(*terms):
    total = terms[0].astype(F32)
    for term in terms[1:]:
        total = total + term.astype(F32)
    return total


def local(
    tokens, chan_table, chan_valid, chan_embed, query, w_key, w_value, w_out, ln_gain, w_up, w_down
):
    slots, patches, width = tokens.shape
    columns = query.shape[0]
    heads = columns // HEAD_DIM
    group, tensor = lax.axis_index("group"), lax.axis_index("tensor")
    tensors = lax.axis_size("tensor")
    chan = lax.axis_index(("y", "core"))
    chans = lax.axis_size("y") * lax.axis_size("core")
    chan_bits = [1] + [2 * b for b in bits_of("y")]
    tensor_bits = bits_of("tensor")
    rows_own = patches // tensors

    key_parts = key_vectors(query, w_key, heads)[None]
    key_order = [0]
    for bit in chan_bits:
        key_parts = jnp.concatenate([key_parts, chan_swap(key_parts, bit)], axis=0)
        key_order = key_order + [j ^ bit for j in key_order]
    key_place = chan ^ jnp.array(key_order, jnp.int32)
    place = jnp.concatenate([jnp.reshape(tensor, (1,)).astype(jnp.int32), key_place])

    padded = -(-slots // 16) * 16
    lanes = -(-(slots * BLOCK) // LANES) * LANES
    slot_ids = lax.dynamic_slice_in_dim(chan_table, chan * slots, slots)
    slot_ids = jnp.pad(slot_ids, (0, padded - slots), constant_values=-1)
    matches = slot_ids[:, None] == jnp.arange(chan_embed.shape[0], dtype=jnp.int32)[None, :]
    added = jnp.dot(matches.astype(BF16), chan_embed, preferred_element_type=F32).astype(BF16)
    live_slots = jnp.sum(matches.astype(jnp.int32) * chan_valid[None, :], axis=1) > 0
    live = jnp.repeat(live_slots.astype(F32), BLOCK)
    live = jnp.pad(live, (0, max(lanes - live.shape[0], 0)))[:lanes][None]

    blocks = patches // BLOCK
    spread_groups = lax.axis_size("y") == 2 and lax.axis_size("group") == 2
    cut = 5 * blocks // 8

    def pool(keys, where, first, count):
        keys = [keys[j] for j in range(chans)]
        return pool_tokens(tokens, added, live, keys, where, heads, rows_own, first, count)

    if spread_groups:
        rows = w_value.shape[0]
        share = 3 * rows // 8
        mine = lax.dynamic_slice_in_dim(w_value, group * share, share, 0)
        key_parts, mine, straight = lax.optimization_barrier(
            (key_parts, mine, w_value[2 * share :])
        )
        one = swap(mine, "y")
        near = swap(w_value, "core")
        first_pool = pool(key_parts, place, 0, cut)
        one, first_pool, late_place, straight = lax.optimization_barrier(
            (one, first_pool, place, straight)
        )
        two = swap(one, "group")
        three = swap(straight, "y")
        second_pool = pool(key_parts, late_place, cut, blocks - cut)
        found = (first_pool, second_pool)
    else:
        full = lax.all_gather(w_value, ("y", "core"), axis=0, tiled=True)
        found = (pool(key_parts, place, 0, cut), pool(key_parts, place, cut, blocks - cut))

    pooled = [part[0] for part in found]
    tops = jnp.concatenate([part[1] for part in found])
    sums = jnp.concatenate([part[2] for part in found])
    top = tops[:, :, :BLOCK].transpose(1, 0, 2).reshape(heads, patches)
    weight_sum = sums[:, :, :BLOCK].transpose(1, 0, 2).reshape(heads, patches)
    stats = jnp.stack([top, weight_sum])[None]
    for bit in chan_bits:
        stats = jnp.concatenate([stats, chan_swap(stats, bit)], axis=0)
    best = jnp.max(stats[:, 0], axis=0)
    total = jnp.sum(stats[:, 1] * jnp.exp(stats[:, 0] - best[None]), axis=0)
    factor = jnp.exp(top - best) / total
    factor = jnp.broadcast_to(factor[:, :, None], (heads, patches, HEAD_DIM))

    if spread_groups:
        start = value_products(
            pooled, [w_value, near], jnp.stack([chan, chan ^ 1]) * rows, 0, heads, None, None, F32
        )
        pieces = [one, two, three]
        pieces += [swap(piece, "core") for piece in pieces]
        places = []
        for base in ((chan ^ 2) * rows, (chan ^ 3) * rows):
            places += [base + group * share, base + (1 - group) * share, base + 2 * share]
        places, count = jnp.stack(places), heads // 2
        parts = [
            value_products(pooled, pieces, places, h, count, start, factor, BF16)
            for h in (0, count)
        ]
    else:
        parts = [
            value_products(
                pooled, [full], jnp.zeros((1,), jnp.int32), 0, heads, None, factor, BF16
            )
        ]

    partial_value = None
    at = 0
    for part in parts:
        for bit in chan_bits:
            part = add_up(part, chan_swap(part, bit)).astype(BF16)
        got = jnp.dot(part, w_out[at : at + part.shape[1]], preferred_element_type=F32)
        at += part.shape[1]
        partial_value = got if partial_value is None else partial_value + got

    sent = partial_value.astype(BF16).reshape(tensors, rows_own, -1)
    projected = add_up(
        partial_value[:rows_own], *[swap(sent[k], "tensor", k) for k in range(1, tensors)]
    )
    own, w_up, w_down = lax.optimization_barrier((projected.astype(BF16), w_up, w_down))
    pieces = [swap(own, "tensor", k) for k in range(1, tensors)]
    pieces, w_up, w_down = lax.optimization_barrier((pieces, *load_weights(w_up, w_down)))
    rows = jnp.concatenate([own] + pieces, axis=0)

    gathered, order = rows[None], [0]
    for bit in chan_bits[1:] + chan_bits[:1]:
        gathered = jnp.concatenate([gathered, chan_swap(gathered, bit)], axis=0)
        order = order + [j ^ bit for j in order]
    partial_out = mlp(gathered, chan ^ jnp.array(order, jnp.int32), ln_gain, w_up, w_down)

    held = {j: partial_out[n] for n, j in enumerate(order)}
    for bit in chan_bits:
        keep = sorted(j for j in held if not j & bit)
        send = jnp.stack([held[j ^ bit] for j in keep]).astype(BF16)
        got = chan_swap(send, bit)
        held = {j: add_up(held[j], got[n]).astype(BF16) for n, j in enumerate(keep)}
    sent = held[0].reshape(tensors, rows_own, -1)
    mixed = add_up(
        projected, sent[0], *[swap(sent[k], "tensor", k) for k in range(1, tensors)]
    )
    return mixed.astype(BF16)


def solution(mesh):
    groups, chans, tensors = (mesh.shape[a] for a in ("group", "chan", "tensor"))
    split = Mesh(
        mesh.devices.reshape(groups, chans // 2, 2, tensors), ("group", "y", "core", "tensor")
    )
    chan = ("y", "core")
    in_specs = (
        P(chan, "group", None),
        P(),
        P(),
        P(),
        P("tensor"),
        P(chan, "tensor"),
        P(chan, "tensor"),
        P("tensor", chan),
        P(),
        P(None, (*chan, "tensor")),
        P((*chan, "tensor"), None),
    )
    out_specs = P(("group", "tensor"), chan)
    return jax.shard_map(
        local, mesh=split, in_specs=in_specs, out_specs=out_specs, check_vma=False
    )
```

```python
import functools

import jax
import jax.numpy as jnp
from jax import lax
from jax.experimental import pallas as pl
from jax.experimental.pallas import tpu as pltpu
from jax.sharding import Mesh, PartitionSpec as P

HEAD_DIM = 128
BLOCK = 16
LANES = 128
NEG = -1e30
F32 = jnp.float32
BF16 = jnp.bfloat16
NT = (((1,), (1,)), ((), ()))
MIB = 1 << 20


def swap(x, axis, bit=1):
    size = lax.axis_size(axis)
    return lax.ppermute(x, axis, [(i, i ^ bit) for i in range(size)])


def bits_of(axis):
    size, bit, found = lax.axis_size(axis), 1, []
    while bit < size:
        found.append(bit)
        bit *= 2
    return found


def chan_swap(x, bit):
    return swap(x, "core", 1) if bit == 1 else swap(x, "y", bit // 2)


def split_parts(x, parts):
    out, rest = [], x
    for _ in range(parts):
        piece = rest.astype(BF16)
        out.append(piece)
        rest = rest - piece.astype(F32)
    return out


def pool_kernel(heads, chan_count, first, count, per_owner, taken, place, tokens, *rest):
    if taken is not None:
        whole, rest = rest[0], rest[1:]
    added, live, rest = rest[0], rest[1], rest[2:]
    key_refs = rest[:chan_count]
    pooled_out, top_out, sum_out = rest[chan_count : chan_count + 3]
    rest = rest[chan_count + 3 :]
    if taken is not None:
        out_rows, rest = rest[0], rest[1:]
    held, arrived, pooled, stored, keys, add_scores, scores, spreads = rest[:8]
    if taken is not None:
        held_rows, rows_in, rows_out = rest[8:]
        copy_in = pltpu.make_async_copy(
            whole.at[pl.ds(taken, out_rows.shape[0]), :], held_rows, rows_in
        )
        copy_out = pltpu.make_async_copy(held_rows, out_rows, rows_out)
    slots, _, width = tokens.shape
    block = held.shape[2]
    rows = slots * block
    lanes = scores.shape[1]
    groups = lanes // LANES
    padded = added.shape[0]

    def fetch(i):
        at = first + i
        row = (((at // per_owner) ^ place[0]) * per_owner + at % per_owner) * block
        return pltpu.make_async_copy(
            tokens.at[:, pl.ds(pl.multiple_of(row, block), block), :],
            held.at[i],
            arrived.at[i],
        )

    fetch(0).start()
    if count > 1:
        fetch(1).start()

    piece = width // chan_count
    for j in range(chan_count):
        at = pl.multiple_of(place[1 + j] * piece, piece)
        high, low = split_parts(key_refs[j][...], 2)
        keys[:, pl.ds(at, piece)] = jnp.concatenate([high, low], axis=0)
    raw = lax.dot_general(keys[...], added[...], NT, preferred_element_type=F32)
    raw = raw[:heads] + raw[heads:]
    lane = lax.broadcasted_iota(jnp.int32, (padded, lanes), 1)
    slot = lax.broadcasted_iota(jnp.int32, (padded, lanes), 0)
    expand = jnp.where(lane // block == slot, 1.0, 0.0).astype(BF16)
    total = jnp.zeros((heads, lanes), F32)
    for part in split_parts(raw, 3):
        total = total + jnp.dot(part, expand, preferred_element_type=F32)
    add_scores[...] = total
    scores[...] = jnp.zeros_like(scores)

    def fold(x, combine):
        out = x[:, :LANES]
        for g in range(1, groups):
            out = combine(out, x[:, g * LANES : (g + 1) * LANES])
        shift = LANES // 2
        while shift >= block:
            out = combine(out, pltpu.roll(out, shift, 1))
            shift //= 2
        return out

    def store(i):
        return pltpu.make_async_copy(
            pooled.at[i], pooled_out.at[:, pl.ds(i * block, block), :], stored.at[i]
        )

    step = min(width, 512)
    by_slot = None
    for i in range(count + 1):
        if i < count:
            fetch(i).wait()
            if i + 2 < count:
                fetch(i + 2).start()
        raw = None
        for at in range(0, width, step):
            if i < count:
                part = held[i, :, :, at : at + step].reshape(rows, step)
                got = lax.dot_general(
                    keys[:, at : at + step], part, NT, preferred_element_type=F32
                )
                raw = got if raw is None else raw + got
            if i > 0:
                part = held[i - 1, :, :, at : at + step].reshape(rows, step)
                got = jnp.dot(spreads[:, :rows], part, preferred_element_type=F32)
                got = got + jnp.dot(
                    by_slot, added[:, at : at + step], preferred_element_type=F32
                )
                pooled[i - 1, :, :, at : at + step] = got.reshape(heads, block, step).astype(BF16)
        if i > 0:
            store(i - 1).start()
        if i == 1 and taken is not None:
            copy_in.start()
        if i == count - 1 and taken is not None:
            copy_in.wait()
            copy_out.start()
        if i == count:
            break
        scores[:, :rows] = raw[:heads] + raw[heads:]
        alive = live[...] > 0.0
        masked = jnp.where(alive, scores[...] + add_scores[...], NEG)
        top = fold(masked, jnp.maximum)
        wide_top = jnp.concatenate([top] * groups, axis=1)
        weights = jnp.where(alive, jnp.exp(masked - wide_top), 0.0)
        weights = weights.astype(BF16).astype(F32)
        top_out[i] = top
        sum_out[i] = fold(weights, jnp.add)
        patch = lax.broadcasted_iota(jnp.int32, (heads, block, lanes), 1)
        column = lax.broadcasted_iota(jnp.int32, (heads, block, lanes), 2)
        spread = jnp.where(
            column % block == patch, jnp.broadcast_to(weights[:, None, :], patch.shape), 0.0
        )
        spread = spread.reshape(heads * block, lanes).astype(BF16)
        spreads[...] = spread
        pick = jnp.where(
            lax.broadcasted_iota(jnp.int32, (lanes, padded), 0) // block
            == lax.broadcasted_iota(jnp.int32, (lanes, padded), 1),
            1.0,
            0.0,
        ).astype(BF16)
        by_slot = jnp.dot(spread, pick, preferred_element_type=F32).astype(BF16)
    for i in range(count):
        store(i).wait()
    if taken is not None:
        copy_out.wait()


def pool_tokens(tokens, added, live, key_parts, place, heads, rows_own, first, count, take=None):
    slots, _, width = tokens.shape
    lanes = live.shape[1]
    vmem, hbm = (pl.BlockSpec(memory_space=m) for m in (pltpu.VMEM, pltpu.HBM))
    extra_in, extra_out, extra_scratch, taken = [], [], [], None
    if take is not None:
        whole, taken = take
        extra_in = [pltpu.with_memory_space_constraint(whole, pltpu.HBM)]
        extra = (whole.shape[0] - taken, whole.shape[1])
        extra_out = [pltpu.HBM(extra, whole.dtype)]
        extra_scratch = [pltpu.VMEM(extra, whole.dtype)] + [pltpu.SemaphoreType.DMA] * 2
    return pl.pallas_call(
        functools.partial(
            pool_kernel, heads, len(key_parts), first, count, max(rows_own // BLOCK, 1), taken
        ),
        out_shape=[
            pltpu.HBM((heads, count * BLOCK, width), BF16),
            jax.ShapeDtypeStruct((count, heads, LANES), F32),
            jax.ShapeDtypeStruct((count, heads, LANES), F32),
        ]
        + extra_out,
        in_specs=[pl.BlockSpec(memory_space=pltpu.SMEM), hbm]
        + [hbm] * len(extra_in)
        + [vmem] * (2 + len(key_parts)),
        out_specs=[hbm, vmem, vmem] + [hbm] * len(extra_out),
        scratch_shapes=[
            pltpu.VMEM((count, slots, BLOCK, width), BF16),
            pltpu.SemaphoreType.DMA((count,)),
            pltpu.VMEM((count, heads, BLOCK, width), BF16),
            pltpu.SemaphoreType.DMA((count,)),
            pltpu.VMEM((2 * heads, width), BF16),
            pltpu.VMEM((heads, lanes), F32),
            pltpu.VMEM((heads, lanes), F32),
            pltpu.VMEM((heads * BLOCK, lanes), BF16),
        ]
        + extra_scratch,
        compiler_params=pltpu.CompilerParams(
            vmem_limit_bytes=3 * MIB + count * (slots + heads) * BLOCK * width * 2
        ),
        name="pool_tokens",
    )(
        place,
        pltpu.with_memory_space_constraint(tokens, pltpu.HBM),
        *extra_in,
        added,
        live,
        *key_parts,
    )


def value_kernel(together, pool_count, piece_count, has_start, has_factor, offsets, *rest):
    pooled, rest = rest[:pool_count], rest[pool_count:]
    pieces, rest = rest[:piece_count], rest[piece_count:]
    total = None
    for n, piece in enumerate(pieces):
        depth = piece.shape[0]
        at = pl.multiple_of(offsets[1 + n], LANES)
        stacked = jnp.concatenate(
            [part[h, :, pl.ds(at, depth)] for h in range(together) for part in pooled],
            axis=0,
        )
        got = jnp.dot(stacked, piece[...], preferred_element_type=F32)
        total = got if total is None else total + got
    patches = total.shape[0] // together
    out = rest[-1]
    for h in range(together):
        columns = slice(h * HEAD_DIM, (h + 1) * HEAD_DIM)
        got = total[h * patches : (h + 1) * patches, columns]
        if has_start:
            got = got + rest[0][:, columns]
        if has_factor:
            got = got * rest[-2][h]
        out[:, columns] = got.astype(out.dtype)


def value_products(pooled, window, pieces, offsets, first_head, head_count, start, factor, kind):
    patches = sum(part.shape[1] for part in pooled)
    together = 2 if head_count % 2 == 0 else 1
    wide = together * HEAD_DIM
    first = first_head // together
    specs = [
        pl.BlockSpec((together, part.shape[1], window), lambda h, o: (first + h, 0, o[0]))
        for part in pooled
    ]
    operands = [pltpu.with_memory_space_constraint(part, pltpu.HBM) for part in pooled]
    for piece in pieces:
        specs.append(pl.BlockSpec((piece.shape[0], wide), lambda h, o: (0, first + h)))
        operands.append(piece)
    if start is not None:
        specs.append(pl.BlockSpec((patches, wide), lambda h, o: (0, first + h)))
        operands.append(start)
    if factor is not None:
        specs.append(pl.BlockSpec((together, patches, HEAD_DIM), lambda h, o: (first + h, 0, 0)))
        operands.append(factor)
    return pl.pallas_call(
        functools.partial(
            value_kernel,
            together,
            len(pooled),
            len(pieces),
            start is not None,
            factor is not None,
        ),
        out_shape=jax.ShapeDtypeStruct((patches, head_count * HEAD_DIM), kind),
        grid_spec=pltpu.PrefetchScalarGridSpec(
            num_scalar_prefetch=1,
            grid=(head_count // together,),
            in_specs=specs,
            out_specs=pl.BlockSpec((patches, wide), lambda h, o: (0, h)),
        ),
        compiler_params=pltpu.CompilerParams(vmem_limit_bytes=14 * MIB),
        name="value_products",
    )(offsets, *operands)


def take_kernel(at, whole, out, held, arrived, left):
    rows = pl.ds(pl.multiple_of(at[0], 16), out.shape[0])
    copy = pltpu.make_async_copy(whole.at[rows, :], held, arrived)
    copy.start()
    copy.wait()
    copy = pltpu.make_async_copy(held, out, left)
    copy.start()
    copy.wait()


def take_rows(whole, at, count):
    return pl.pallas_call(
        take_kernel,
        out_shape=pltpu.HBM((count, whole.shape[1]), whole.dtype),
        in_specs=[pl.BlockSpec(memory_space=pltpu.SMEM), pl.BlockSpec(memory_space=pltpu.HBM)],
        out_specs=pl.BlockSpec(memory_space=pltpu.HBM),
        scratch_shapes=[
            pltpu.VMEM((count, whole.shape[1]), whole.dtype),
            pltpu.SemaphoreType.DMA,
            pltpu.SemaphoreType.DMA,
        ],
        compiler_params=pltpu.CompilerParams(vmem_limit_bytes=2 * MIB),
        name="take_rows",
    )(jnp.reshape(at, (1,)), pltpu.with_memory_space_constraint(whole, pltpu.HBM))


def load_kernel(*refs):
    half = len(refs) // 2
    arrived = refs[-1]
    copies = [
        pltpu.make_async_copy(refs[i], refs[half + i], arrived.at[i]) for i in range(half)
    ]
    for copy in copies:
        copy.start()
    for copy in copies:
        copy.wait()


def load_weights(*weights):
    return pl.pallas_call(
        load_kernel,
        out_shape=[pltpu.VMEM(w.shape, w.dtype) for w in weights],
        in_specs=[pl.BlockSpec(memory_space=pl.ANY)] * len(weights),
        out_specs=[pl.BlockSpec(memory_space=pltpu.VMEM)] * len(weights),
        scratch_shapes=[pltpu.SemaphoreType.DMA((len(weights),))],
        cost_estimate=pl.CostEstimate(
            flops=0, transcendentals=0, bytes_accessed=sum(w.size * 2 for w in weights)
        ),
        compiler_params=pltpu.CompilerParams(vmem_limit_bytes=MIB),
        name="load_weights",
    )(*[pltpu.with_memory_space_constraint(w, pltpu.HBM) for w in weights])


def mlp_kernel(count, chunks, order, *refs):
    xs = refs[:chunks]
    gain, w_up, w_down, out, normed = refs[chunks:]
    piece = xs[0].shape[2]
    width = count * piece
    at_row = 0
    for x in xs:
        rows = x.shape[1]
        mean = jnp.zeros((rows, 1), F32)
        for j in range(count):
            mean = mean + jnp.sum(x[j].astype(F32), axis=1, keepdims=True)
        mean = mean / width
        variance = jnp.zeros((rows, 1), F32)
        for j in range(count):
            centered = x[j].astype(F32) - mean
            variance = variance + jnp.sum(centered * centered, axis=1, keepdims=True)
        scale = lax.rsqrt(variance / width + 1e-05)
        for j in range(count):
            got = ((x[j].astype(F32) - mean) * scale * gain[order[j]]).astype(BF16)
            normed[j, at_row : at_row + rows, :] = got
        at_row += rows
    total = None
    for j in range(count):
        at = pl.multiple_of(order[j] * piece, piece)
        got = jnp.dot(normed[j], w_up[pl.ds(at, piece), :], preferred_element_type=F32)
        total = got if total is None else total + got
    hidden = jax.nn.gelu(total).astype(BF16)
    for j in range(count):
        at = pl.multiple_of(order[j] * piece, piece)
        got = jnp.dot(hidden, w_down[:, pl.ds(at, piece)], preferred_element_type=F32)
        out[j] = got.astype(BF16)


def mlp(xs, order, ln_gain, w_up, w_down):
    count, _, piece = xs[0].shape
    patches = sum(x.shape[1] for x in xs)
    vmem = pl.BlockSpec(memory_space=pltpu.VMEM)
    w_up, w_down = (pltpu.with_memory_space_constraint(w, pltpu.VMEM) for w in (w_up, w_down))
    return pl.pallas_call(
        functools.partial(mlp_kernel, count, len(xs)),
        out_shape=jax.ShapeDtypeStruct((count, patches, piece), BF16),
        in_specs=[pl.BlockSpec(memory_space=pltpu.SMEM)] + [vmem] * (len(xs) + 3),
        out_specs=vmem,
        scratch_shapes=[pltpu.VMEM((count, patches, piece), BF16)],
        compiler_params=pltpu.CompilerParams(vmem_limit_bytes=8 * MIB),
        name="norm_mlp",
    )(order, *xs, ln_gain.reshape(count, 1, piece), w_up, w_down)


def key_vectors(query, w_key, heads):
    columns = query.shape[0]
    mine = jnp.arange(columns)[None, :] // HEAD_DIM == jnp.arange(heads)[:, None]
    rows = [jnp.where(mine, part[None, :], 0) for part in split_parts(query, 3)]
    stacked = jnp.concatenate(rows, axis=0).astype(BF16)
    got = lax.dot_general(stacked, w_key, NT, preferred_element_type=F32)
    scale = 1.0 / jnp.sqrt(F32(HEAD_DIM))
    return (got.reshape(3, heads, -1).sum(axis=0)) * scale


def add_up(*terms):
    total = terms[0].astype(F32)
    for term in terms[1:]:
        total = total + term.astype(F32)
    return total


def local(
    tokens, chan_table, chan_valid, chan_embed, query, w_key, w_value, w_out, ln_gain, w_up, w_down
):
    slots, patches, width = tokens.shape
    columns = query.shape[0]
    heads = columns // HEAD_DIM
    group, tensor = lax.axis_index("group"), lax.axis_index("tensor")
    tensors = lax.axis_size("tensor")
    chan = lax.axis_index(("y", "core"))
    chans = lax.axis_size("y") * lax.axis_size("core")
    chan_bits = [1] + [2 * b for b in bits_of("y")]
    tensor_bits = bits_of("tensor")
    rows_own = patches // tensors

    key_parts = key_vectors(query, w_key, heads)[None]
    key_order = [0]
    weights = w_value
    for bit in chan_bits:
        key_parts = jnp.concatenate([key_parts, chan_swap(key_parts, bit)], axis=0)
        key_order = key_order + [j ^ bit for j in key_order]
        if bit == 1:
            key_parts, weights = lax.optimization_barrier((key_parts, weights))
    key_place = chan ^ jnp.array(key_order, jnp.int32)
    place = jnp.concatenate([jnp.reshape(tensor, (1,)).astype(jnp.int32), key_place])

    padded = -(-slots // 16) * 16
    lanes = -(-(slots * BLOCK) // LANES) * LANES
    slot_ids = lax.dynamic_slice_in_dim(chan_table, chan * slots, slots)
    slot_ids = jnp.pad(slot_ids, (0, padded - slots), constant_values=-1)
    matches = slot_ids[:, None] == jnp.arange(chan_embed.shape[0], dtype=jnp.int32)[None, :]
    added = jnp.dot(matches.astype(BF16), chan_embed, preferred_element_type=F32).astype(BF16)
    live_slots = jnp.sum(matches.astype(jnp.int32) * chan_valid[None, :], axis=1) > 0
    live = jnp.repeat(live_slots.astype(F32), BLOCK)
    live = jnp.pad(live, (0, max(lanes - live.shape[0], 0)))[:lanes][None]

    blocks = patches // BLOCK
    spread_groups = lax.axis_size("y") == 2 and lax.axis_size("group") == 2
    cut = 5 * blocks // 8

    def pool(keys, added, where, first, count, take=None):
        keys = [keys[j] for j in range(chans)]
        return pool_tokens(
            tokens, added, live, keys, where, heads, rows_own, first, count, take
        )

    if spread_groups:
        rows = w_value.shape[0]
        share = 3 * rows // 8
        mine = take_rows(weights, group * share, share)
        key_parts, mine, added, live = lax.optimization_barrier((key_parts, mine, added, live))
        one = swap(mine, "y")
        near = swap(w_value, "core")
        *first_pool, straight = pool(key_parts, added, place, 0, cut, (weights, 2 * share))
        one, first_pool, late_place, straight = lax.optimization_barrier(
            (one, first_pool, place, straight)
        )
        two = swap(one, "group")
        three = swap(straight, "y")
        one_across = swap(one, "core")
        second_pool = pool(key_parts, added, late_place, cut, blocks - cut)
        found = (first_pool, second_pool)
    else:
        full = lax.all_gather(w_value, ("y", "core"), axis=0, tiled=True)
        found = [
            pool(key_parts, added, place, at, n) for at, n in ((0, cut), (cut, blocks - cut))
        ]

    pooled = [part[0] for part in found]
    tops = jnp.concatenate([part[1] for part in found])
    sums = jnp.concatenate([part[2] for part in found])
    top = tops[:, :, :BLOCK].transpose(1, 0, 2).reshape(heads, patches)
    weight_sum = sums[:, :, :BLOCK].transpose(1, 0, 2).reshape(heads, patches)
    stats = jnp.stack([top, weight_sum])[None]
    for bit in chan_bits:
        stats = jnp.concatenate([stats, chan_swap(stats, bit)], axis=0)
        if bit == 1:
            stats, pooled = lax.optimization_barrier((stats, pooled))
    best = jnp.max(stats[:, 0], axis=0)
    total = jnp.sum(stats[:, 1] * jnp.exp(stats[:, 0] - best[None]), axis=0)
    factor = jnp.exp(top - best) / total
    factor = jnp.broadcast_to(factor[:, :, None], (heads, patches, HEAD_DIM))

    if spread_groups:
        own_at, near_at, far, across = (jnp.int32(chan ^ j) * rows for j in range(4))
        starts = [jnp.int32(0), own_at, near_at, far + group * share, across + group * share]
        pieces = [w_value, near, one, one_across]
        start = value_products(
            pooled, width, pieces, jnp.stack(starts), 0, heads, None, None, F32
        )
        two, three, start = lax.optimization_barrier((two, three, start))
        pieces = [two, three, swap(two, "core"), swap(three, "core")]
        window, side = 2 * rows, jnp.int32(1 - chan // 2)
        starts = [side]
        for base in (far - side * window, across - side * window):
            starts += [base + (1 - group) * share, base + 2 * share]
        value = value_products(
            pooled, window, pieces, jnp.stack(starts), 0, heads, start, factor, BF16
        )
    else:
        value = value_products(
            pooled, width, [full], jnp.zeros((2,), jnp.int32), 0, heads, None, factor, BF16
        )

    low = tensors // 2
    chunks = [list(range(low, tensors)), list(range(low))]
    split = lambda x: [x[ks[0] * rows_own : (ks[-1] + 1) * rows_own] for ks in chunks]
    value = add_up(value, swap(value, "core")).astype(BF16)
    value, w_out = lax.optimization_barrier((value, w_out))
    values = split(value)
    for bit in chan_bits[1:]:
        values = [(v, chan_swap(v, bit)) for v in values]
        (far_own, far_got), (low_own, low_got) = values
        if bit == chan_bits[-1]:
            far_got, w_out = lax.optimization_barrier((far_got, *load_weights(w_out)))
        far = add_up(far_own, far_got).astype(BF16)
        if bit == chan_bits[-1]:
            far_out = jnp.dot(far, w_out, preferred_element_type=F32).astype(BF16)
        values = [far, add_up(low_own, low_got).astype(BF16)]
    low_out = jnp.dot(values[1], w_out, preferred_element_type=F32)
    sent = list(low_out.astype(BF16).reshape(low, rows_own, -1))
    sent += list(far_out.reshape(tensors - low, rows_own, -1))
    got = [swap(sent[k], "tensor", k) for k in range(low, tensors)]
    low_out, w_up, w_down = lax.optimization_barrier((low_out, w_up, w_down))
    got += [swap(sent[k], "tensor", k) for k in range(1, low)]
    got, w_up, w_down = lax.optimization_barrier((got, *load_weights(w_up, w_down)))
    projected = add_up(low_out[:rows_own], *got)
    own = projected.astype(BF16)

    arrived = [own] + [swap(own, "tensor", k) for k in range(1, tensors)]
    gathered = []
    for ks in reversed(chunks):
        rows, order = jnp.concatenate([arrived[k] for k in ks], axis=0)[None], [0]
        for bit in chan_bits[1:] + chan_bits[:1]:
            rows = jnp.concatenate([rows, chan_swap(rows, bit)], axis=0)
            order = order + [j ^ bit for j in order]
        gathered.append(rows)
    partial_out = mlp(gathered, chan ^ jnp.array(order, jnp.int32), ln_gain, w_up, w_down)

    held = {j: partial_out[n] for n, j in enumerate(order)}
    keep = [j for j in held if not j & 1]
    passed = swap(jnp.stack([held[j ^ 1] for j in keep]), "core")
    held = {j: add_up(held[j], passed[n]).astype(BF16) for n, j in enumerate(keep)}
    parts = {j: split(x) for j, x in held.items()}
    for bit in chan_bits[1:]:
        keep = sorted(j for j in parts if not j & bit)
        passed = [chan_swap(jnp.stack([parts[j ^ bit][n] for j in keep]), bit) for n in (0, 1)]
        far = {j: add_up(parts[j][0], passed[0][n]).astype(BF16) for n, j in enumerate(keep)}
        far, passed = lax.optimization_barrier((far, passed))
        near = {j: add_up(parts[j][1], passed[1][n]) for n, j in enumerate(keep)}
        parts = {j: [far[j], near[j].astype(BF16)] for j in keep}
    got = [
        swap(x, "tensor", k) for k, x in zip(chunks[0], parts[0][0].reshape(low, rows_own, -1))
    ]
    sent = parts[0][1].reshape(low, rows_own, -1)
    got += [swap(sent[k], "tensor", k) for k in range(1, low)]
    return add_up(projected, sent[0], *got).astype(BF16)


def solution(mesh):
    groups, chans, tensors = (mesh.shape[a] for a in ("group", "chan", "tensor"))
    split = Mesh(
        mesh.devices.reshape(groups, chans // 2, 2, tensors), ("group", "y", "core", "tensor")
    )
    chan = ("y", "core")
    in_specs = (
        P(chan, "group", None),
        P(),
        P(),
        P(),
        P("tensor"),
        P(chan, "tensor"),
        P(chan, "tensor"),
        P("tensor", chan),
        P(),
        P(None, (*chan, "tensor")),
        P((*chan, "tensor"), None),
    )
    out_specs = P(("group", "tensor"), chan)
    return jax.shard_map(
        local, mesh=split, in_specs=in_specs, out_specs=out_specs, check_vma=False
    )
```

```python
import functools

import jax
import jax.numpy as jnp
from jax import lax
from jax.experimental import pallas as pl
from jax.experimental.pallas import tpu as pltpu
from jax.sharding import Mesh, PartitionSpec as P

HEAD_DIM = 128
BLOCK = 16
LANES = 128
NEG = -1e30
F32 = jnp.float32
BF16 = jnp.bfloat16
NT = (((1,), (1,)), ((), ()))
MIB = 1 << 20
LONG = 1e10


def swap(x, axis, bit=1):
    size = lax.axis_size(axis)
    return lax.ppermute(x, axis, [(i, i ^ bit) for i in range(size)])


def cost(flops, size):
    return pl.CostEstimate(flops=int(flops), transcendentals=0, bytes_accessed=int(size))


def bits_of(axis):
    size, bit, found = lax.axis_size(axis), 1, []
    while bit < size:
        found.append(bit)
        bit *= 2
    return found


def chan_swap(x, bit):
    return swap(x, "core", 1) if bit == 1 else swap(x, "y", bit // 2)


def split_parts(x, parts):
    out, rest = [], x
    for _ in range(parts):
        piece = rest.astype(BF16)
        out.append(piece)
        rest = rest - piece.astype(F32)
    return out


def pool_kernel(heads, chan_count, first, count, per_owner, taken, place, tokens, *rest):
    if taken is not None:
        whole, rest = rest[0], rest[1:]
    added, live, rest = rest[0], rest[1], rest[2:]
    key_refs = rest[:chan_count]
    pooled_out, top_out, sum_out = rest[chan_count : chan_count + 3]
    rest = rest[chan_count + 3 :]
    if taken is not None:
        out_rows, rest = rest[0], rest[1:]
    held, arrived, pooled, stored, keys, add_scores, scores, spreads = rest[:8]
    if taken is not None:
        held_rows, rows_in, rows_out = rest[8:]
        copy_in = pltpu.make_async_copy(
            whole.at[pl.ds(taken, out_rows.shape[0]), :], held_rows, rows_in
        )
        copy_out = pltpu.make_async_copy(held_rows, out_rows, rows_out)
    slots, _, width = tokens.shape
    block = held.shape[2]
    rows = slots * block
    lanes = scores.shape[1]
    groups = lanes // LANES
    padded = added.shape[0]

    def fetch(i):
        at = first + i
        row = (((at // per_owner) ^ place[0]) * per_owner + at % per_owner) * block
        return pltpu.make_async_copy(
            tokens.at[:, pl.ds(pl.multiple_of(row, block), block), :],
            held.at[i],
            arrived.at[i],
        )

    fetch(0).start()
    if count > 1:
        fetch(1).start()

    piece = width // chan_count
    for j in range(chan_count):
        at = pl.multiple_of(place[1 + j] * piece, piece)
        high, low = split_parts(key_refs[j][...], 2)
        keys[:, pl.ds(at, piece)] = jnp.concatenate([high, low], axis=0)
    raw = lax.dot_general(keys[...], added[...], NT, preferred_element_type=F32)
    raw = raw[:heads] + raw[heads:]
    lane = lax.broadcasted_iota(jnp.int32, (padded, lanes), 1)
    slot = lax.broadcasted_iota(jnp.int32, (padded, lanes), 0)
    expand = jnp.where(lane // block == slot, 1.0, 0.0).astype(BF16)
    total = jnp.zeros((heads, lanes), F32)
    for part in split_parts(raw, 3):
        total = total + jnp.dot(part, expand, preferred_element_type=F32)
    add_scores[...] = total
    scores[...] = jnp.zeros_like(scores)

    def fold(x, combine):
        out = x[:, :LANES]
        for g in range(1, groups):
            out = combine(out, x[:, g * LANES : (g + 1) * LANES])
        shift = LANES // 2
        while shift >= block:
            out = combine(out, pltpu.roll(out, shift, 1))
            shift //= 2
        return out

    def store(i):
        return pltpu.make_async_copy(
            pooled.at[i], pooled_out.at[:, pl.ds(i * block, block), :], stored.at[i]
        )

    step = min(width, 512)
    by_slot = None
    for i in range(count + 1):
        if i < count:
            fetch(i).wait()
            if i + 2 < count:
                fetch(i + 2).start()
        raw = None
        for at in range(0, width, step):
            if i < count:
                part = held[i, :, :, at : at + step].reshape(rows, step)
                got = lax.dot_general(
                    keys[:, at : at + step], part, NT, preferred_element_type=F32
                )
                raw = got if raw is None else raw + got
            if i > 0:
                part = held[i - 1, :, :, at : at + step].reshape(rows, step)
                got = jnp.dot(spreads[:, :rows], part, preferred_element_type=F32)
                got = got + jnp.dot(
                    by_slot, added[:, at : at + step], preferred_element_type=F32
                )
                pooled[i - 1, :, :, at : at + step] = got.reshape(heads, block, step).astype(BF16)
        if i > 0:
            store(i - 1).start()
        if i == 1 and taken is not None:
            copy_in.start()
        if i == count - 1 and taken is not None:
            copy_in.wait()
            copy_out.start()
        if i == count:
            break
        scores[:, :rows] = raw[:heads] + raw[heads:]
        alive = live[...] > 0.0
        masked = jnp.where(alive, scores[...] + add_scores[...], NEG)
        top = fold(masked, jnp.maximum)
        wide_top = jnp.concatenate([top] * groups, axis=1)
        weights = jnp.where(alive, jnp.exp(masked - wide_top), 0.0)
        weights = weights.astype(BF16).astype(F32)
        top_out[i] = top
        sum_out[i] = fold(weights, jnp.add)
        patch = lax.broadcasted_iota(jnp.int32, (heads, block, lanes), 1)
        column = lax.broadcasted_iota(jnp.int32, (heads, block, lanes), 2)
        spread = jnp.where(
            column % block == patch, jnp.broadcast_to(weights[:, None, :], patch.shape), 0.0
        )
        spread = spread.reshape(heads * block, lanes).astype(BF16)
        spreads[...] = spread
        pick = jnp.where(
            lax.broadcasted_iota(jnp.int32, (lanes, padded), 0) // block
            == lax.broadcasted_iota(jnp.int32, (lanes, padded), 1),
            1.0,
            0.0,
        ).astype(BF16)
        by_slot = jnp.dot(spread, pick, preferred_element_type=F32).astype(BF16)
    for i in range(count):
        store(i).wait()
    if taken is not None:
        copy_out.wait()


def pool_tokens(tokens, added, live, key_parts, place, heads, rows_own, first, count, take=None):
    slots, _, width = tokens.shape
    lanes = live.shape[1]
    vmem, hbm = (pl.BlockSpec(memory_space=m) for m in (pltpu.VMEM, pltpu.HBM))
    extra_in, extra_out, extra_scratch, taken = [], [], [], None
    if take is not None:
        whole, taken = take
        extra_in = [pltpu.with_memory_space_constraint(whole, pltpu.HBM)]
        extra = (whole.shape[0] - taken, whole.shape[1])
        extra_out = [pltpu.HBM(extra, whole.dtype)]
        extra_scratch = [pltpu.VMEM(extra, whole.dtype)] + [pltpu.SemaphoreType.DMA] * 2
    return pl.pallas_call(
        functools.partial(
            pool_kernel, heads, len(key_parts), first, count, max(rows_own // BLOCK, 1), taken
        ),
        out_shape=[
            pltpu.HBM((heads, count * BLOCK, width), BF16),
            jax.ShapeDtypeStruct((count, heads, LANES), F32),
            jax.ShapeDtypeStruct((count, heads, LANES), F32),
        ]
        + extra_out,
        in_specs=[pl.BlockSpec(memory_space=pltpu.SMEM), hbm]
        + [hbm] * len(extra_in)
        + [vmem] * (2 + len(key_parts)),
        out_specs=[hbm, vmem, vmem] + [hbm] * len(extra_out),
        scratch_shapes=[
            pltpu.VMEM((count, slots, BLOCK, width), BF16),
            pltpu.SemaphoreType.DMA((count,)),
            pltpu.VMEM((count, heads, BLOCK, width), BF16),
            pltpu.SemaphoreType.DMA((count,)),
            pltpu.VMEM((2 * heads, width), BF16),
            pltpu.VMEM((heads, lanes), F32),
            pltpu.VMEM((heads, lanes), F32),
            pltpu.VMEM((heads * BLOCK, lanes), BF16),
        ]
        + extra_scratch,
        compiler_params=pltpu.CompilerParams(
            vmem_limit_bytes=3 * MIB + count * (slots + heads) * BLOCK * width * 2
        ),
        cost_estimate=cost(
            count * slots * BLOCK * width * 1024, count * (slots + heads) * BLOCK * width * 2
        ),
        name="pool_tokens",
    )(
        place,
        pltpu.with_memory_space_constraint(tokens, pltpu.HBM),
        *extra_in,
        added,
        live,
        *key_parts,
    )


def value_kernel(together, pool_count, piece_count, has_start, has_factor, offsets, *rest):
    pooled, rest = rest[:pool_count], rest[pool_count:]
    pieces, rest = rest[:piece_count], rest[piece_count:]
    total = None
    for n, piece in enumerate(pieces):
        depth = piece.shape[0]
        at = pl.multiple_of(offsets[1 + n], LANES)
        stacked = jnp.concatenate(
            [part[h, :, pl.ds(at, depth)] for h in range(together) for part in pooled],
            axis=0,
        )
        got = jnp.dot(stacked, piece[...], preferred_element_type=F32)
        total = got if total is None else total + got
    patches = total.shape[0] // together
    out = rest[-1]
    for h in range(together):
        columns = slice(h * HEAD_DIM, (h + 1) * HEAD_DIM)
        got = total[h * patches : (h + 1) * patches, columns]
        if has_start:
            got = got + rest[0][:, columns]
        if has_factor:
            got = got * rest[-2][h]
        out[:, columns] = got.astype(out.dtype)


def value_products(pooled, window, pieces, offsets, first_head, head_count, start, factor, kind):
    patches, width = sum(part.shape[1] for part in pooled), pooled[0].shape[2]
    together = 2 if head_count % 2 == 0 else 1
    wide = together * HEAD_DIM
    first = first_head // together
    specs = [
        pl.BlockSpec((together, part.shape[1], window), lambda h, o: (first + h, 0, o[0]))
        for part in pooled
    ]
    operands = [pltpu.with_memory_space_constraint(part, pltpu.HBM) for part in pooled]
    for piece in pieces:
        specs.append(pl.BlockSpec((piece.shape[0], wide), lambda h, o: (0, first + h)))
        operands.append(piece)
    if start is not None:
        specs.append(pl.BlockSpec((patches, wide), lambda h, o: (0, first + h)))
        operands.append(start)
    if factor is not None:
        specs.append(pl.BlockSpec((together, patches, HEAD_DIM), lambda h, o: (first + h, 0, 0)))
        operands.append(factor)
    return pl.pallas_call(
        functools.partial(
            value_kernel,
            together,
            len(pooled),
            len(pieces),
            start is not None,
            factor is not None,
        ),
        out_shape=jax.ShapeDtypeStruct((patches, head_count * HEAD_DIM), kind),
        grid_spec=pltpu.PrefetchScalarGridSpec(
            num_scalar_prefetch=1,
            grid=(head_count // together,),
            in_specs=specs,
            out_specs=pl.BlockSpec((patches, wide), lambda h, o: (0, h)),
        ),
        compiler_params=pltpu.CompilerParams(vmem_limit_bytes=14 * MIB),
        cost_estimate=cost(
            4 * patches * width * head_count * HEAD_DIM, sum(x.size * 2 for x in operands)
        ),
        name="value_products",
    )(offsets, *operands)


def take_kernel(at, whole, out, held, arrived, left):
    rows = pl.ds(pl.multiple_of(at[0], 16), out.shape[0])
    copy = pltpu.make_async_copy(whole.at[rows, :], held, arrived)
    copy.start()
    copy.wait()
    copy = pltpu.make_async_copy(held, out, left)
    copy.start()
    copy.wait()


def take_rows(whole, at, count):
    return pl.pallas_call(
        take_kernel,
        out_shape=pltpu.HBM((count, whole.shape[1]), whole.dtype),
        in_specs=[pl.BlockSpec(memory_space=pltpu.SMEM), pl.BlockSpec(memory_space=pltpu.HBM)],
        out_specs=pl.BlockSpec(memory_space=pltpu.HBM),
        scratch_shapes=[
            pltpu.VMEM((count, whole.shape[1]), whole.dtype),
            pltpu.SemaphoreType.DMA,
            pltpu.SemaphoreType.DMA,
        ],
        compiler_params=pltpu.CompilerParams(vmem_limit_bytes=2 * MIB),
        name="take_rows",
    )(jnp.reshape(at, (1,)), pltpu.with_memory_space_constraint(whole, pltpu.HBM))


def load_kernel(*refs):
    half = len(refs) // 2
    arrived = refs[-1]
    copies = [
        pltpu.make_async_copy(refs[i], refs[half + i], arrived.at[i]) for i in range(half)
    ]
    for copy in copies:
        copy.start()
    for copy in copies:
        copy.wait()


def load_weights(*weights):
    return pl.pallas_call(
        load_kernel,
        out_shape=[pltpu.VMEM(w.shape, w.dtype) for w in weights],
        in_specs=[pl.BlockSpec(memory_space=pl.ANY)] * len(weights),
        out_specs=[pl.BlockSpec(memory_space=pltpu.VMEM)] * len(weights),
        scratch_shapes=[pltpu.SemaphoreType.DMA((len(weights),))],
        cost_estimate=pl.CostEstimate(
            flops=0, transcendentals=0, bytes_accessed=sum(w.size * 2 for w in weights)
        ),
        compiler_params=pltpu.CompilerParams(vmem_limit_bytes=MIB),
        name="load_weights",
    )(*[pltpu.with_memory_space_constraint(w, pltpu.HBM) for w in weights])


def window_kernel(count, at, *refs):
    parts, outs, arrived = refs[:count], refs[count : 2 * count], refs[-1]
    copies = []
    for n in range(count):
        columns = pl.ds(pl.multiple_of(at[0], outs[n].shape[2]), outs[n].shape[2])
        copies.append(
            pltpu.make_async_copy(parts[n].at[:, :, columns], outs[n], arrived.at[n])
        )
    for copy in copies:
        copy.start()
    for copy in copies:
        copy.wait()


def load_window(parts, at, window):
    size = sum(part.size // part.shape[2] * window * 2 for part in parts)
    return pl.pallas_call(
        functools.partial(window_kernel, len(parts)),
        out_shape=[pltpu.VMEM((*part.shape[:2], window), part.dtype) for part in parts],
        in_specs=[pl.BlockSpec(memory_space=pltpu.SMEM)]
        + [pl.BlockSpec(memory_space=pltpu.HBM)] * len(parts),
        out_specs=[pl.BlockSpec(memory_space=pltpu.VMEM)] * len(parts),
        scratch_shapes=[pltpu.SemaphoreType.DMA((len(parts),))],
        compiler_params=pltpu.CompilerParams(vmem_limit_bytes=MIB),
        cost_estimate=pl.CostEstimate(flops=0, transcendentals=0, bytes_accessed=size),
        name="load_window",
    )(jnp.reshape(at, (1,)), *[pltpu.with_memory_space_constraint(p, pltpu.HBM) for p in parts])


def late_kernel(pool_count, piece_count, offsets, *rest):
    pooled, rest = rest[:pool_count], rest[pool_count:]
    pieces, (start, factor, out) = rest[:piece_count], rest[piece_count:]
    patches = out.shape[0]
    heads = out.shape[1] // HEAD_DIM
    together = 2 if heads % 2 == 0 else 1
    wide = together * HEAD_DIM
    for head in range(0, heads, together):
        first = head * HEAD_DIM
        total = None
        for n, piece in enumerate(pieces):
            depth = piece.shape[0]
            at = pl.multiple_of(offsets[n], LANES)
            stacked = jnp.concatenate(
                [part[head + h, :, pl.ds(at, depth)] for h in range(together) for part in pooled],
                axis=0,
            )
            got = jnp.dot(stacked, piece[:, first : first + wide], preferred_element_type=F32)
            total = got if total is None else total + got
        for h in range(together):
            columns = slice(first + h * HEAD_DIM, first + (h + 1) * HEAD_DIM)
            got = total[h * patches : (h + 1) * patches, h * HEAD_DIM : (h + 1) * HEAD_DIM]
            got = (got + start[:, columns]) * factor[:, head + h : head + h + 1]
            out[:, columns] = got.astype(out.dtype)


def late_products(pooled, pieces, offsets, start, factor):
    patches = sum(part.shape[1] for part in pooled)
    heads = pooled[0].shape[0]
    vmem = pl.BlockSpec(memory_space=pltpu.VMEM)
    depth = sum(piece.shape[0] for piece in pieces)
    return pl.pallas_call(
        functools.partial(late_kernel, len(pooled), len(pieces)),
        out_shape=jax.ShapeDtypeStruct((patches, heads * HEAD_DIM), BF16),
        in_specs=[pl.BlockSpec(memory_space=pltpu.SMEM)]
        + [vmem] * (len(pooled) + len(pieces) + 2),
        out_specs=vmem,
        compiler_params=pltpu.CompilerParams(vmem_limit_bytes=8 * MIB),
        cost_estimate=cost(
            4 * patches * depth * heads * HEAD_DIM, sum(piece.size * 2 for piece in pieces)
        ),
        name="late_products",
    )(
        offsets,
        *[pltpu.with_memory_space_constraint(part, pltpu.VMEM) for part in pooled],
        *pieces,
        start,
        factor,
    )


def project_kernel(own, got, weights, out, sent):
    rows = (own[...].astype(F32) + got[...].astype(F32)).astype(BF16)
    found = jnp.dot(rows, weights[...], preferred_element_type=F32)
    out[...] = found
    sent[...] = found.astype(BF16)


def project(own, got, weights, guess):
    vmem = pl.BlockSpec(memory_space=pltpu.VMEM)
    shape = (own.shape[0], weights.shape[1])
    return pl.pallas_call(
        project_kernel,
        out_shape=[jax.ShapeDtypeStruct(shape, F32), jax.ShapeDtypeStruct(shape, BF16)],
        in_specs=[vmem] * 3,
        out_specs=[vmem] * 2,
        compiler_params=pltpu.CompilerParams(vmem_limit_bytes=4 * MIB),
        cost_estimate=cost(guess, own.size * 4),
        name="project",
    )(own, got, pltpu.with_memory_space_constraint(weights, pltpu.VMEM))


def add_kernel(left, right, out):
    out[...] = (left[...].astype(F32) + right[...].astype(F32)).astype(out.dtype)


def add_rows(left, right, guess):
    vmem = pl.BlockSpec(memory_space=pltpu.VMEM)
    return pl.pallas_call(
        add_kernel,
        out_shape=jax.ShapeDtypeStruct(left.shape, left.dtype),
        in_specs=[vmem] * 2,
        out_specs=vmem,
        compiler_params=pltpu.CompilerParams(vmem_limit_bytes=4 * MIB),
        cost_estimate=cost(guess, left.size * 6),
        name="add_rows",
    )(left, right)


def mlp_kernel(count, chunks, order, *refs):
    xs = refs[:chunks]
    gain, w_up, w_down, out, normed = refs[chunks:]
    piece = xs[0].shape[2]
    width = count * piece
    at_row = 0
    for x in xs:
        rows = x.shape[1]
        mean = jnp.zeros((rows, 1), F32)
        for j in range(count):
            mean = mean + jnp.sum(x[j].astype(F32), axis=1, keepdims=True)
        mean = mean / width
        variance = jnp.zeros((rows, 1), F32)
        for j in range(count):
            centered = x[j].astype(F32) - mean
            variance = variance + jnp.sum(centered * centered, axis=1, keepdims=True)
        scale = lax.rsqrt(variance / width + 1e-05)
        for j in range(count):
            got = ((x[j].astype(F32) - mean) * scale * gain[order[j]]).astype(BF16)
            normed[j, at_row : at_row + rows, :] = got
        at_row += rows
    total = None
    for j in range(count):
        at = pl.multiple_of(order[j] * piece, piece)
        got = jnp.dot(normed[j], w_up[pl.ds(at, piece), :], preferred_element_type=F32)
        total = got if total is None else total + got
    hidden = jax.nn.gelu(total).astype(BF16)
    for j in range(count):
        at = pl.multiple_of(order[j] * piece, piece)
        got = jnp.dot(hidden, w_down[:, pl.ds(at, piece)], preferred_element_type=F32)
        out[j] = got.astype(BF16)


def mlp(xs, order, ln_gain, w_up, w_down):
    count, _, piece = xs[0].shape
    patches = sum(x.shape[1] for x in xs)
    vmem = pl.BlockSpec(memory_space=pltpu.VMEM)
    w_up, w_down = (pltpu.with_memory_space_constraint(w, pltpu.VMEM) for w in (w_up, w_down))
    return pl.pallas_call(
        functools.partial(mlp_kernel, count, len(xs)),
        out_shape=jax.ShapeDtypeStruct((count, patches, piece), BF16),
        in_specs=[pl.BlockSpec(memory_space=pltpu.SMEM)] + [vmem] * (len(xs) + 3),
        out_specs=vmem,
        scratch_shapes=[pltpu.VMEM((count, patches, piece), BF16)],
        compiler_params=pltpu.CompilerParams(vmem_limit_bytes=8 * MIB),
        name="norm_mlp",
    )(order, *xs, ln_gain.reshape(count, 1, piece), w_up, w_down)


def key_vectors(query, w_key, heads):
    columns = query.shape[0]
    mine = jnp.arange(columns)[None, :] // HEAD_DIM == jnp.arange(heads)[:, None]
    rows = [jnp.where(mine, part[None, :], 0) for part in split_parts(query, 3)]
    stacked = jnp.concatenate(rows, axis=0).astype(BF16)
    got = lax.dot_general(stacked, w_key, NT, preferred_element_type=F32)
    scale = 1.0 / jnp.sqrt(F32(HEAD_DIM))
    return (got.reshape(3, heads, -1).sum(axis=0)) * scale


def add_up(*terms):
    total = terms[0].astype(F32)
    for term in terms[1:]:
        total = total + term.astype(F32)
    return total


def local(
    tokens, chan_table, chan_valid, chan_embed, query, w_key, w_value, w_out, ln_gain, w_up, w_down
):
    slots, patches, width = tokens.shape
    columns = query.shape[0]
    heads = columns // HEAD_DIM
    group, tensor = lax.axis_index("group"), lax.axis_index("tensor")
    tensors = lax.axis_size("tensor")
    chan = lax.axis_index(("y", "core"))
    chans = lax.axis_size("y") * lax.axis_size("core")
    chan_bits = [1] + [2 * b for b in bits_of("y")]
    tensor_bits = bits_of("tensor")
    rows_own = patches // tensors

    key_parts = key_vectors(query, w_key, heads)[None]
    key_order = [0]
    weights = w_value
    for bit in chan_bits:
        key_parts = jnp.concatenate([key_parts, chan_swap(key_parts, bit)], axis=0)
        key_order = key_order + [j ^ bit for j in key_order]
        if bit == 1:
            key_parts, weights = lax.optimization_barrier((key_parts, weights))
    key_place = chan ^ jnp.array(key_order, jnp.int32)
    place = jnp.concatenate([jnp.reshape(tensor, (1,)).astype(jnp.int32), key_place])

    padded = -(-slots // 16) * 16
    lanes = -(-(slots * BLOCK) // LANES) * LANES
    slot_ids = lax.dynamic_slice_in_dim(chan_table, chan * slots, slots)
    slot_ids = jnp.pad(slot_ids, (0, padded - slots), constant_values=-1)
    matches = slot_ids[:, None] == jnp.arange(chan_embed.shape[0], dtype=jnp.int32)[None, :]
    added = jnp.dot(matches.astype(BF16), chan_embed, preferred_element_type=F32).astype(BF16)
    live_slots = jnp.sum(matches.astype(jnp.int32) * chan_valid[None, :], axis=1) > 0
    live = jnp.repeat(live_slots.astype(F32), BLOCK)
    live = jnp.pad(live, (0, max(lanes - live.shape[0], 0)))[:lanes][None]

    blocks = patches // BLOCK
    spread_groups = lax.axis_size("y") == 2 and lax.axis_size("group") == 2
    cut = 3 * blocks // 4

    def pool(keys, added, where, first, count, take=None):
        keys = [keys[j] for j in range(chans)]
        return pool_tokens(
            tokens, added, live, keys, where, heads, rows_own, first, count, take
        )

    if spread_groups:
        rows = w_value.shape[0]
        share = 3 * rows // 8
        mine = take_rows(weights, group * share, share)
        key_parts, mine, added, live = lax.optimization_barrier((key_parts, mine, added, live))
        one = swap(mine, "y")
        near = swap(w_value, "core")
        *first_pool, straight = pool(key_parts, added, place, 0, cut, (weights, 2 * share))
        one, first_pool, late_place, straight = lax.optimization_barrier(
            (one, first_pool, place, straight)
        )
        two = swap(one, "group")
        three = swap(straight, "y")
        one_across = swap(one, "core")
        second_pool = pool(key_parts, added, late_place, cut, blocks - cut)
        found = (first_pool, second_pool)
    else:
        full = lax.all_gather(w_value, ("y", "core"), axis=0, tiled=True)
        found = [
            pool(key_parts, added, place, at, n) for at, n in ((0, cut), (cut, blocks - cut))
        ]

    pooled = [part[0] for part in found]
    tops = jnp.concatenate([part[1] for part in found])
    sums = jnp.concatenate([part[2] for part in found])
    top = tops[:, :, :BLOCK].transpose(1, 0, 2).reshape(heads, patches)
    weight_sum = sums[:, :, :BLOCK].transpose(1, 0, 2).reshape(heads, patches)
    stats = jnp.stack([top, weight_sum])[None]
    for bit in chan_bits:
        stats = jnp.concatenate([stats, chan_swap(stats, bit)], axis=0)
        if bit == 1:
            stats, pooled = lax.optimization_barrier((stats, pooled))
    def softmax_factor(stats):
        best = jnp.max(stats[:, 0], axis=0)
        total = jnp.sum(stats[:, 1] * jnp.exp(stats[:, 0] - best[None]), axis=0)
        return jnp.exp(top - best) / total

    if spread_groups:
        own_at, near_at, far, across = (jnp.int32(chan ^ j) * rows for j in range(4))
        starts = [jnp.int32(0), own_at, near_at, far + group * share, across + group * share]
        pieces = [w_value, near, one, one_across]
        start = value_products(
            pooled, width, pieces, jnp.stack(starts), 0, heads, None, None, F32
        )
        two, three, start = lax.optimization_barrier((two, three, start))
        pieces = [two, three, swap(two, "core"), swap(three, "core")]
        window, side = 2 * rows, jnp.int32(1 - chan // 2)
        starts = []
        for base in (far - side * window, across - side * window):
            starts += [base + (1 - group) * share, base + 2 * share]
        pooled, start = lax.optimization_barrier((pooled, start))
        loaded = load_window(pooled, side * window, window)
        factor = softmax_factor(stats).T
        pieces, loaded = lax.optimization_barrier((pieces, loaded))
        value = late_products(loaded, pieces, jnp.stack(starts), start, factor)
    else:
        value = value_products(
            pooled,
            width,
            [full],
            jnp.zeros((2,), jnp.int32),
            0,
            heads,
            None,
            jnp.broadcast_to(
                softmax_factor(stats)[:, :, None], (heads, patches, HEAD_DIM)
            ),
            BF16,
        )

    low = tensors // 2
    chunks = [list(range(low, tensors)), list(range(low))]
    split = lambda x: [x[ks[0] * rows_own : (ks[-1] + 1) * rows_own] for ks in chunks]
    value = add_up(value, swap(value, "core")).astype(BF16)
    value, w_out, w_up = lax.optimization_barrier((value, w_out, w_up))
    values = split(value)
    for bit in chan_bits[1:]:
        values = [(v, chan_swap(v, bit)) for v in values]
        (far_own, far_got), (low_own, low_got) = values
        last = bit == chan_bits[-1]
        if last:
            far_got, w_out, w_up = lax.optimization_barrier((far_got, *load_weights(w_out, w_up)))
        if last:
            _, far_out = project(far_own, far_got, w_out, 1e9)
            low_out, low_sent = project(low_own, low_got, w_out, LONG)
        else:
            values = [add_up(far_own, far_got).astype(BF16), add_up(low_own, low_got).astype(BF16)]
    sent = list(low_sent.reshape(low, rows_own, -1))
    sent += list(far_out.reshape(tensors - low, rows_own, -1))
    got = [swap(sent[k], "tensor", k) for k in range(1, tensors)]
    projected = add_up(low_out[:rows_own], *got)
    own = projected.astype(BF16)

    arrived = [own] + [swap(own, "tensor", k) for k in range(1, tensors)]
    low_rows, w_down = lax.optimization_barrier((arrived[:low], w_down))
    far_rows, w_down = lax.optimization_barrier((arrived[low:], *load_weights(w_down)))
    gathered = []
    for pieces in (low_rows, far_rows):
        rows, order = jnp.concatenate(pieces, axis=0)[None], [0]
        for bit in chan_bits[1:] + chan_bits[:1]:
            rows = jnp.concatenate([rows, chan_swap(rows, bit)], axis=0)
            order = order + [j ^ bit for j in order]
        gathered.append(rows)
    partial_out = mlp(gathered, chan ^ jnp.array(order, jnp.int32), ln_gain, w_up, w_down)

    held = {j: partial_out[n] for n, j in enumerate(order)}
    keep = [j for j in held if not j & 1]
    passed = swap(jnp.stack([held[j ^ 1] for j in keep]), "core")
    held = {j: add_up(held[j], passed[n]).astype(BF16) for n, j in enumerate(keep)}
    parts = {j: split(x) for j, x in held.items()}
    for bit in chan_bits[1:]:
        keep = sorted(j for j in parts if not j & bit)
        passed = [chan_swap(jnp.stack([parts[j ^ bit][n] for j in keep]), bit) for n in (0, 1)]
        far = [add_up(parts[j][0], passed[0][n]).astype(BF16) for n, j in enumerate(keep)]
        near = [add_rows(parts[j][1], passed[1][n], LONG) for n, j in enumerate(keep)]
        parts = {j: [far[n], near[n]] for n, j in enumerate(keep)}
    got = [
        swap(x, "tensor", k) for k, x in zip(chunks[0], parts[0][0].reshape(low, rows_own, -1))
    ]
    sent = parts[0][1].reshape(low, rows_own, -1)
    got += [swap(sent[k], "tensor", k) for k in range(1, low)]
    return add_up(projected, sent[0], *got).astype(BF16)


def solution(mesh):
    groups, chans, tensors = (mesh.shape[a] for a in ("group", "chan", "tensor"))
    split = Mesh(
        mesh.devices.reshape(groups, chans // 2, 2, tensors), ("group", "y", "core", "tensor")
    )
    chan = ("y", "core")
    in_specs = (
        P(chan, "group", None),
        P(),
        P(),
        P(),
        P("tensor"),
        P(chan, "tensor"),
        P(chan, "tensor"),
        P("tensor", chan),
        P(),
        P(None, (*chan, "tensor")),
        P((*chan, "tensor"), None),
    )
    out_specs = P(("group", "tensor"), chan)
    return jax.shard_map(
        local, mesh=split, in_specs=in_specs, out_specs=out_specs, check_vma=False
    )
```

```python
import functools

import jax
import jax.numpy as jnp
from jax import lax
from jax.experimental import pallas as pl
from jax.experimental.pallas import tpu as pltpu
from jax.sharding import Mesh, PartitionSpec as P

HEAD_DIM = 128
BLOCK = 16
LANES = 128
NEG = -1e30
F32 = jnp.float32
BF16 = jnp.bfloat16
NT = (((1,), (1,)), ((), ()))
MIB = 1 << 20
LONG = 1e10


def swap(x, axis, bit=1):
    size = lax.axis_size(axis)
    return lax.ppermute(x, axis, [(i, i ^ bit) for i in range(size)])


def cost(flops, size):
    return pl.CostEstimate(flops=int(flops), transcendentals=0, bytes_accessed=int(size))


def exact_parts(x):
    out, rest = [], x
    for _ in range(3):
        piece = lax.reduce_precision(rest, 8, 7)
        out.append(piece.astype(BF16))
        rest = rest - piece
    return out


def pack(value, stats):
    tail = jnp.concatenate(exact_parts(stats), axis=1)
    tail = jnp.pad(tail, ((0, 0), (0, -tail.shape[1] % LANES)))
    return jnp.concatenate([value, tail], axis=1)


def unpack_stats(packed, columns, count):
    tail = packed[:, columns:].astype(F32)
    return tail[:, :count] + tail[:, count : 2 * count] + tail[:, 2 * count : 3 * count]


def join_stats(own, got):
    heads = own.shape[1] // 2
    best = jnp.maximum(own[:, :heads], got[:, :heads])
    mine, theirs = jnp.exp(own[:, :heads] - best), jnp.exp(got[:, :heads] - best)
    return best, own[:, heads:] * mine + got[:, heads:] * theirs, mine, theirs


def bits_of(axis):
    size, bit, found = lax.axis_size(axis), 1, []
    while bit < size:
        found.append(bit)
        bit *= 2
    return found


def chan_swap(x, bit):
    return swap(x, "core", 1) if bit == 1 else swap(x, "y", bit // 2)


def split_parts(x, parts):
    out, rest = [], x
    for _ in range(parts):
        piece = rest.astype(BF16)
        out.append(piece)
        rest = rest - piece.astype(F32)
    return out


def pool_kernel(heads, chan_count, first, count, per_owner, taken, place, tokens, *rest):
    if taken is not None:
        whole, rest = rest[0], rest[1:]
    added, live, rest = rest[0], rest[1], rest[2:]
    key_refs = rest[:chan_count]
    pooled_out, top_out, sum_out = rest[chan_count : chan_count + 3]
    rest = rest[chan_count + 3 :]
    if taken is not None:
        out_rows, rest = rest[0], rest[1:]
    held, arrived, pooled, stored, keys, add_scores, scores, spreads = rest[:8]
    if taken is not None:
        held_rows, rows_in, rows_out = rest[8:]
        copy_in = pltpu.make_async_copy(
            whole.at[pl.ds(taken, out_rows.shape[0]), :], held_rows, rows_in
        )
        copy_out = pltpu.make_async_copy(held_rows, out_rows, rows_out)
    slots, _, width = tokens.shape
    block = held.shape[2]
    rows = slots * block
    lanes = scores.shape[1]
    groups = lanes // LANES
    padded = added.shape[0]

    def fetch(i):
        at = first + i
        row = (((at // per_owner) ^ place[0]) * per_owner + at % per_owner) * block
        return pltpu.make_async_copy(
            tokens.at[:, pl.ds(pl.multiple_of(row, block), block), :],
            held.at[i],
            arrived.at[i],
        )

    fetch(0).start()
    if count > 1:
        fetch(1).start()

    piece = width // chan_count
    for j in range(chan_count):
        at = pl.multiple_of(place[1 + j] * piece, piece)
        high, low = split_parts(key_refs[j][...], 2)
        keys[:, pl.ds(at, piece)] = jnp.concatenate([high, low], axis=0)
    raw = lax.dot_general(keys[...], added[...], NT, preferred_element_type=F32)
    raw = raw[:heads] + raw[heads:]
    lane = lax.broadcasted_iota(jnp.int32, (padded, lanes), 1)
    slot = lax.broadcasted_iota(jnp.int32, (padded, lanes), 0)
    expand = jnp.where(lane // block == slot, 1.0, 0.0).astype(BF16)
    total = jnp.zeros((heads, lanes), F32)
    for part in split_parts(raw, 3):
        total = total + jnp.dot(part, expand, preferred_element_type=F32)
    add_scores[...] = total
    scores[...] = jnp.zeros_like(scores)

    def fold(x, combine):
        out = x[:, :LANES]
        for g in range(1, groups):
            out = combine(out, x[:, g * LANES : (g + 1) * LANES])
        shift = LANES // 2
        while shift >= block:
            out = combine(out, pltpu.roll(out, shift, 1))
            shift //= 2
        return out

    def store(i):
        return pltpu.make_async_copy(
            pooled.at[i], pooled_out.at[:, pl.ds(i * block, block), :], stored.at[i]
        )

    step = min(width, 512)
    by_slot = None
    for i in range(count + 1):
        if i < count:
            fetch(i).wait()
            if i + 2 < count:
                fetch(i + 2).start()
        raw = None
        for at in range(0, width, step):
            if i < count:
                part = held[i, :, :, at : at + step].reshape(rows, step)
                got = lax.dot_general(
                    keys[:, at : at + step], part, NT, preferred_element_type=F32
                )
                raw = got if raw is None else raw + got
            if i > 0:
                part = held[i - 1, :, :, at : at + step].reshape(rows, step)
                got = jnp.dot(spreads[:, :rows], part, preferred_element_type=F32)
                got = got + jnp.dot(
                    by_slot, added[:, at : at + step], preferred_element_type=F32
                )
                pooled[i - 1, :, :, at : at + step] = got.reshape(heads, block, step).astype(BF16)
        if i > 0:
            store(i - 1).start()
        if i == 1 and taken is not None:
            copy_in.start()
        if i == count - 1 and taken is not None:
            copy_in.wait()
            copy_out.start()
        if i == count:
            break
        scores[:, :rows] = raw[:heads] + raw[heads:]
        alive = live[...] > 0.0
        masked = jnp.where(alive, scores[...] + add_scores[...], NEG)
        top = fold(masked, jnp.maximum)
        wide_top = jnp.concatenate([top] * groups, axis=1)
        weights = jnp.where(alive, jnp.exp(masked - wide_top), 0.0)
        weights = weights.astype(BF16).astype(F32)
        top_out[i] = top
        sum_out[i] = fold(weights, jnp.add)
        patch = lax.broadcasted_iota(jnp.int32, (heads, block, lanes), 1)
        column = lax.broadcasted_iota(jnp.int32, (heads, block, lanes), 2)
        spread = jnp.where(
            column % block == patch, jnp.broadcast_to(weights[:, None, :], patch.shape), 0.0
        )
        spread = spread.reshape(heads * block, lanes).astype(BF16)
        spreads[...] = spread
        pick = jnp.where(
            lax.broadcasted_iota(jnp.int32, (lanes, padded), 0) // block
            == lax.broadcasted_iota(jnp.int32, (lanes, padded), 1),
            1.0,
            0.0,
        ).astype(BF16)
        by_slot = jnp.dot(spread, pick, preferred_element_type=F32).astype(BF16)
    for i in range(count):
        store(i).wait()
    if taken is not None:
        copy_out.wait()


def pool_tokens(tokens, added, live, key_parts, place, heads, rows_own, first, count, take=None):
    slots, _, width = tokens.shape
    lanes = live.shape[1]
    vmem, hbm = (pl.BlockSpec(memory_space=m) for m in (pltpu.VMEM, pltpu.HBM))
    extra_in, extra_out, extra_scratch, taken = [], [], [], None
    if take is not None:
        whole, taken = take
        extra_in = [pltpu.with_memory_space_constraint(whole, pltpu.HBM)]
        extra = (whole.shape[0] - taken, whole.shape[1])
        extra_out = [pltpu.HBM(extra, whole.dtype)]
        extra_scratch = [pltpu.VMEM(extra, whole.dtype)] + [pltpu.SemaphoreType.DMA] * 2
    return pl.pallas_call(
        functools.partial(
            pool_kernel, heads, len(key_parts), first, count, max(rows_own // BLOCK, 1), taken
        ),
        out_shape=[
            pltpu.HBM((heads, count * BLOCK, width), BF16),
            jax.ShapeDtypeStruct((count, heads, LANES), F32),
            jax.ShapeDtypeStruct((count, heads, LANES), F32),
        ]
        + extra_out,
        in_specs=[pl.BlockSpec(memory_space=pltpu.SMEM), hbm]
        + [hbm] * len(extra_in)
        + [vmem] * (2 + len(key_parts)),
        out_specs=[hbm, vmem, vmem] + [hbm] * len(extra_out),
        scratch_shapes=[
            pltpu.VMEM((count, slots, BLOCK, width), BF16),
            pltpu.SemaphoreType.DMA((count,)),
            pltpu.VMEM((count, heads, BLOCK, width), BF16),
            pltpu.SemaphoreType.DMA((count,)),
            pltpu.VMEM((2 * heads, width), BF16),
            pltpu.VMEM((heads, lanes), F32),
            pltpu.VMEM((heads, lanes), F32),
            pltpu.VMEM((heads * BLOCK, lanes), BF16),
        ]
        + extra_scratch,
        compiler_params=pltpu.CompilerParams(
            vmem_limit_bytes=3 * MIB + count * (slots + heads) * BLOCK * width * 2
        ),
        cost_estimate=cost(
            count * slots * BLOCK * width * 1024, count * (slots + heads) * BLOCK * width * 2
        ),
        name="pool_tokens",
    )(
        place,
        pltpu.with_memory_space_constraint(tokens, pltpu.HBM),
        *extra_in,
        added,
        live,
        *key_parts,
    )


def value_kernel(together, pool_count, piece_count, has_start, has_factor, offsets, *rest):
    pooled, rest = rest[:pool_count], rest[pool_count:]
    pieces, rest = rest[:piece_count], rest[piece_count:]
    total = None
    for n, piece in enumerate(pieces):
        depth = piece.shape[0]
        at = pl.multiple_of(offsets[1 + n], LANES)
        stacked = jnp.concatenate(
            [part[h, :, pl.ds(at, depth)] for h in range(together) for part in pooled],
            axis=0,
        )
        got = jnp.dot(stacked, piece[...], preferred_element_type=F32)
        total = got if total is None else total + got
    patches = total.shape[0] // together
    out = rest[-1]
    for h in range(together):
        columns = slice(h * HEAD_DIM, (h + 1) * HEAD_DIM)
        got = total[h * patches : (h + 1) * patches, columns]
        if has_start:
            got = got + rest[0][:, columns]
        if has_factor:
            got = got * rest[-2][h]
        out[:, columns] = got.astype(out.dtype)


def value_products(pooled, window, pieces, offsets, first_head, head_count, start, factor, kind):
    patches, width = sum(part.shape[1] for part in pooled), pooled[0].shape[2]
    together = 2 if head_count % 2 == 0 else 1
    wide = together * HEAD_DIM
    first = first_head // together
    specs = [
        pl.BlockSpec((together, part.shape[1], window), lambda h, o: (first + h, 0, o[0]))
        for part in pooled
    ]
    operands = [pltpu.with_memory_space_constraint(part, pltpu.HBM) for part in pooled]
    for piece in pieces:
        specs.append(pl.BlockSpec((piece.shape[0], wide), lambda h, o: (0, first + h)))
        operands.append(piece)
    if start is not None:
        specs.append(pl.BlockSpec((patches, wide), lambda h, o: (0, first + h)))
        operands.append(start)
    if factor is not None:
        specs.append(pl.BlockSpec((together, patches, HEAD_DIM), lambda h, o: (first + h, 0, 0)))
        operands.append(factor)
    return pl.pallas_call(
        functools.partial(
            value_kernel,
            together,
            len(pooled),
            len(pieces),
            start is not None,
            factor is not None,
        ),
        out_shape=jax.ShapeDtypeStruct((patches, head_count * HEAD_DIM), kind),
        grid_spec=pltpu.PrefetchScalarGridSpec(
            num_scalar_prefetch=1,
            grid=(head_count // together,),
            in_specs=specs,
            out_specs=pl.BlockSpec((patches, wide), lambda h, o: (0, h)),
        ),
        compiler_params=pltpu.CompilerParams(vmem_limit_bytes=14 * MIB),
        cost_estimate=cost(
            4 * patches * width * head_count * HEAD_DIM, sum(x.size * 2 for x in operands)
        ),
        name="value_products",
    )(offsets, *operands)


def take_kernel(at, whole, out, held, arrived, left):
    rows = pl.ds(pl.multiple_of(at[0], 16), out.shape[0])
    copy = pltpu.make_async_copy(whole.at[rows, :], held, arrived)
    copy.start()
    copy.wait()
    copy = pltpu.make_async_copy(held, out, left)
    copy.start()
    copy.wait()


def take_rows(whole, at, count):
    return pl.pallas_call(
        take_kernel,
        out_shape=pltpu.HBM((count, whole.shape[1]), whole.dtype),
        in_specs=[pl.BlockSpec(memory_space=pltpu.SMEM), pl.BlockSpec(memory_space=pltpu.HBM)],
        out_specs=pl.BlockSpec(memory_space=pltpu.HBM),
        scratch_shapes=[
            pltpu.VMEM((count, whole.shape[1]), whole.dtype),
            pltpu.SemaphoreType.DMA,
            pltpu.SemaphoreType.DMA,
        ],
        compiler_params=pltpu.CompilerParams(vmem_limit_bytes=2 * MIB),
        name="take_rows",
    )(jnp.reshape(at, (1,)), pltpu.with_memory_space_constraint(whole, pltpu.HBM))


def load_kernel(*refs):
    half = len(refs) // 2
    arrived = refs[-1]
    copies = [
        pltpu.make_async_copy(refs[i], refs[half + i], arrived.at[i]) for i in range(half)
    ]
    for copy in copies:
        copy.start()
    for copy in copies:
        copy.wait()


def load_weights(*weights):
    return pl.pallas_call(
        load_kernel,
        out_shape=[pltpu.VMEM(w.shape, w.dtype) for w in weights],
        in_specs=[pl.BlockSpec(memory_space=pl.ANY)] * len(weights),
        out_specs=[pl.BlockSpec(memory_space=pltpu.VMEM)] * len(weights),
        scratch_shapes=[pltpu.SemaphoreType.DMA((len(weights),))],
        cost_estimate=pl.CostEstimate(
            flops=0, transcendentals=0, bytes_accessed=sum(w.size * 2 for w in weights)
        ),
        compiler_params=pltpu.CompilerParams(vmem_limit_bytes=MIB),
        name="load_weights",
    )(*[pltpu.with_memory_space_constraint(w, pltpu.HBM) for w in weights])


def window_kernel(count, at, *refs):
    parts, outs, arrived = refs[:count], refs[count : 2 * count], refs[-1]
    copies = []
    for n in range(count):
        columns = pl.ds(pl.multiple_of(at[0], outs[n].shape[2]), outs[n].shape[2])
        copies.append(
            pltpu.make_async_copy(parts[n].at[:, :, columns], outs[n], arrived.at[n])
        )
    for copy in copies:
        copy.start()
    for copy in copies:
        copy.wait()


def load_window(parts, at, window):
    size = sum(part.size // part.shape[2] * window * 2 for part in parts)
    return pl.pallas_call(
        functools.partial(window_kernel, len(parts)),
        out_shape=[pltpu.VMEM((*part.shape[:2], window), part.dtype) for part in parts],
        in_specs=[pl.BlockSpec(memory_space=pltpu.SMEM)]
        + [pl.BlockSpec(memory_space=pltpu.HBM)] * len(parts),
        out_specs=[pl.BlockSpec(memory_space=pltpu.VMEM)] * len(parts),
        scratch_shapes=[pltpu.SemaphoreType.DMA((len(parts),))],
        compiler_params=pltpu.CompilerParams(vmem_limit_bytes=MIB),
        cost_estimate=pl.CostEstimate(flops=0, transcendentals=0, bytes_accessed=size),
        name="load_window",
    )(jnp.reshape(at, (1,)), *[pltpu.with_memory_space_constraint(p, pltpu.HBM) for p in parts])


def late_kernel(pool_count, piece_count, offsets, *rest):
    pooled, rest = rest[:pool_count], rest[pool_count:]
    pieces, (start, factor, out) = rest[:piece_count], rest[piece_count:]
    patches = out.shape[0]
    heads = out.shape[1] // HEAD_DIM
    together = 2 if heads % 2 == 0 else 1
    wide = together * HEAD_DIM
    for head in range(0, heads, together):
        first = head * HEAD_DIM
        total = None
        for n, piece in enumerate(pieces):
            depth = piece.shape[0]
            at = pl.multiple_of(offsets[n], LANES)
            stacked = jnp.concatenate(
                [part[head + h, :, pl.ds(at, depth)] for h in range(together) for part in pooled],
                axis=0,
            )
            got = jnp.dot(stacked, piece[:, first : first + wide], preferred_element_type=F32)
            total = got if total is None else total + got
        for h in range(together):
            columns = slice(first + h * HEAD_DIM, first + (h + 1) * HEAD_DIM)
            got = total[h * patches : (h + 1) * patches, h * HEAD_DIM : (h + 1) * HEAD_DIM]
            got = (got + start[:, columns]) * factor[:, head + h : head + h + 1]
            out[:, columns] = got.astype(out.dtype)


def late_products(pooled, pieces, offsets, start, factor):
    patches = sum(part.shape[1] for part in pooled)
    heads = pooled[0].shape[0]
    vmem = pl.BlockSpec(memory_space=pltpu.VMEM)
    depth = sum(piece.shape[0] for piece in pieces)
    return pl.pallas_call(
        functools.partial(late_kernel, len(pooled), len(pieces)),
        out_shape=jax.ShapeDtypeStruct((patches, heads * HEAD_DIM), BF16),
        in_specs=[pl.BlockSpec(memory_space=pltpu.SMEM)]
        + [vmem] * (len(pooled) + len(pieces) + 2),
        out_specs=vmem,
        compiler_params=pltpu.CompilerParams(vmem_limit_bytes=8 * MIB),
        cost_estimate=cost(
            4 * patches * depth * heads * HEAD_DIM, sum(piece.size * 2 for piece in pieces)
        ),
        name="late_products",
    )(
        offsets,
        *[pltpu.with_memory_space_constraint(part, pltpu.VMEM) for part in pooled],
        *pieces,
        start,
        factor,
    )


def project_kernel(own, stats, got, weights, out, sent):
    columns, count = own.shape[1], stats.shape[1]
    _, total, mine, theirs = join_stats(stats[...], unpack_stats(got[...], columns, count))
    mine, theirs = mine / total, theirs / total
    rows = []
    for h in range(count // 2):
        at = slice(h * HEAD_DIM, (h + 1) * HEAD_DIM)
        row = own[:, at].astype(F32) * mine[:, h : h + 1]
        row = row + got[:, at].astype(F32) * theirs[:, h : h + 1]
        rows.append(row.astype(BF16))
    rows = jnp.concatenate(rows, axis=1)
    found = jnp.dot(rows, weights[...], preferred_element_type=F32)
    out[...] = found
    sent[...] = found.astype(BF16)


def project(own, stats, got, weights, guess):
    vmem = pl.BlockSpec(memory_space=pltpu.VMEM)
    shape = (own.shape[0], weights.shape[1])
    return pl.pallas_call(
        project_kernel,
        out_shape=[jax.ShapeDtypeStruct(shape, F32), jax.ShapeDtypeStruct(shape, BF16)],
        in_specs=[vmem] * 4,
        out_specs=[vmem] * 2,
        compiler_params=pltpu.CompilerParams(vmem_limit_bytes=4 * MIB),
        cost_estimate=cost(guess, own.size * 4),
        name="project",
    )(own, stats, got, pltpu.with_memory_space_constraint(weights, pltpu.VMEM))


def add_kernel(left, right, out):
    out[...] = (left[...].astype(F32) + right[...].astype(F32)).astype(out.dtype)


def add_rows(left, right, guess):
    vmem = pl.BlockSpec(memory_space=pltpu.VMEM)
    return pl.pallas_call(
        add_kernel,
        out_shape=jax.ShapeDtypeStruct(left.shape, left.dtype),
        in_specs=[vmem] * 2,
        out_specs=vmem,
        compiler_params=pltpu.CompilerParams(vmem_limit_bytes=4 * MIB),
        cost_estimate=cost(guess, left.size * 6),
        name="add_rows",
    )(left, right)


def down_columns(hidden, order, w_down, n):
    piece = w_down.shape[1] // order.shape[0]
    at = pl.multiple_of(order[n] * piece, piece)
    got = jnp.dot(hidden, w_down[:, pl.ds(at, piece)], preferred_element_type=F32)
    return got.astype(BF16)


def mlp_kernel(count, chunks, outs, order, *refs):
    xs = refs[: count * chunks]
    gain, w_up, w_down, *found, hidden, normed = refs[count * chunks :]
    piece = xs[0].shape[1]
    width = count * piece
    at_row = 0
    for chunk in range(chunks):
        x = xs[chunk * count : (chunk + 1) * count]
        rows = x[0].shape[0]
        mean = jnp.zeros((rows, 1), F32)
        for j in range(count):
            mean = mean + jnp.sum(x[j][...].astype(F32), axis=1, keepdims=True)
        mean = mean / width
        variance = jnp.zeros((rows, 1), F32)
        for j in range(count):
            centered = x[j][...].astype(F32) - mean
            variance = variance + jnp.sum(centered * centered, axis=1, keepdims=True)
        scale = lax.rsqrt(variance / width + 1e-05)
        for j in range(count):
            got = ((x[j][...].astype(F32) - mean) * scale * gain[order[j]]).astype(BF16)
            normed[j, at_row : at_row + rows, :] = got
        at_row += rows
    total = None
    for j in range(count):
        at = pl.multiple_of(order[j] * piece, piece)
        got = jnp.dot(normed[j], w_up[pl.ds(at, piece), :], preferred_element_type=F32)
        total = got if total is None else total + got
    active = jax.nn.gelu(total).astype(BF16)
    hidden[...] = active
    for n in range(outs):
        found[n][...] = down_columns(active, order, w_down, n)


def mlp(xs, order, ln_gain, w_up, w_down, outs):
    count, piece = len(xs[0]), xs[0][0].shape[1]
    patches = sum(x[0].shape[0] for x in xs)
    vmem = pl.BlockSpec(memory_space=pltpu.VMEM)
    w_up, w_down = (pltpu.with_memory_space_constraint(w, pltpu.VMEM) for w in (w_up, w_down))
    flat = [x for chunk in xs for x in chunk]
    *found, hidden = pl.pallas_call(
        functools.partial(mlp_kernel, count, len(xs), outs),
        out_shape=[jax.ShapeDtypeStruct((patches, piece), BF16)] * outs
        + [jax.ShapeDtypeStruct((patches, w_up.shape[1]), BF16)],
        in_specs=[pl.BlockSpec(memory_space=pltpu.SMEM)] + [vmem] * (len(flat) + 3),
        out_specs=[vmem] * (outs + 1),
        scratch_shapes=[pltpu.VMEM((count, patches, piece), BF16)],
        compiler_params=pltpu.CompilerParams(vmem_limit_bytes=8 * MIB),
        name="norm_mlp",
    )(order, *flat, ln_gain.reshape(count, 1, piece), w_up, w_down)
    return found, hidden


def down_kernel(first, order, hidden, w_down, *found):
    for n, out in enumerate(found):
        out[...] = down_columns(hidden[...], order, w_down, first + n)


def down(hidden, order, w_down, first, last):
    vmem = pl.BlockSpec(memory_space=pltpu.VMEM)
    shape = (hidden.shape[0], w_down.shape[1] // last)
    return pl.pallas_call(
        functools.partial(down_kernel, first),
        out_shape=[jax.ShapeDtypeStruct(shape, BF16)] * (last - first),
        in_specs=[pl.BlockSpec(memory_space=pltpu.SMEM), vmem, vmem],
        out_specs=[vmem] * (last - first),
        compiler_params=pltpu.CompilerParams(vmem_limit_bytes=4 * MIB),
        cost_estimate=cost(2e9, hidden.size * 2),
        name="down",
    )(order, hidden, pltpu.with_memory_space_constraint(w_down, pltpu.VMEM))


def key_vectors(query, w_key, heads):
    columns = query.shape[0]
    mine = jnp.arange(columns)[None, :] // HEAD_DIM == jnp.arange(heads)[:, None]
    rows = [jnp.where(mine, part[None, :], 0) for part in exact_parts(query)]
    stacked = jnp.concatenate(rows, axis=0).astype(BF16)
    got = lax.dot_general(stacked, w_key, NT, preferred_element_type=F32)
    scale = 1.0 / jnp.sqrt(F32(HEAD_DIM))
    return (got.reshape(3, heads, -1).sum(axis=0)) * scale


def add_up(*terms):
    total = terms[0].astype(F32)
    for term in terms[1:]:
        total = total + term.astype(F32)
    return total


def local(
    tokens, chan_table, chan_valid, chan_embed, query, w_key, w_value, w_out, ln_gain, w_up, w_down
):
    slots, patches, width = tokens.shape
    columns = query.shape[0]
    heads = columns // HEAD_DIM
    group, tensor = lax.axis_index("group"), lax.axis_index("tensor")
    tensors = lax.axis_size("tensor")
    chan = lax.axis_index(("y", "core"))
    chans = lax.axis_size("y") * lax.axis_size("core")
    chan_bits = [1] + [2 * b for b in bits_of("y")]
    tensor_bits = bits_of("tensor")
    rows_own = patches // tensors

    key_parts = key_vectors(query, w_key, heads)[None]
    key_order = [0]
    weights = w_value
    for bit in chan_bits:
        key_parts = jnp.concatenate([key_parts, chan_swap(key_parts, bit)], axis=0)
        key_order = key_order + [j ^ bit for j in key_order]
        if bit == 1:
            key_parts, weights = lax.optimization_barrier((key_parts, weights))
    key_place = chan ^ jnp.array(key_order, jnp.int32)
    place = jnp.concatenate([jnp.reshape(tensor, (1,)).astype(jnp.int32), key_place])

    padded = -(-slots // 16) * 16
    lanes = -(-(slots * BLOCK) // LANES) * LANES
    slot_ids = lax.dynamic_slice_in_dim(chan_table, chan * slots, slots)
    slot_ids = jnp.pad(slot_ids, (0, padded - slots), constant_values=-1)
    matches = slot_ids[:, None] == jnp.arange(chan_embed.shape[0], dtype=jnp.int32)[None, :]
    added = jnp.dot(matches.astype(BF16), chan_embed, preferred_element_type=F32).astype(BF16)
    live_slots = jnp.sum(matches.astype(jnp.int32) * chan_valid[None, :], axis=1) > 0
    live = jnp.repeat(live_slots.astype(F32), BLOCK)
    live = jnp.pad(live, (0, max(lanes - live.shape[0], 0)))[:lanes][None]

    blocks = patches // BLOCK
    spread_groups = lax.axis_size("y") == 2 and lax.axis_size("group") == 2
    cut = 3 * blocks // 4

    def pool(keys, added, where, first, count, take=None):
        keys = [keys[j] for j in range(chans)]
        return pool_tokens(
            tokens, added, live, keys, where, heads, rows_own, first, count, take
        )

    if spread_groups:
        rows = w_value.shape[0]
        share = 3 * rows // 8
        mine = take_rows(weights, group * share, share)
        key_parts, mine, added, live = lax.optimization_barrier((key_parts, mine, added, live))
        one = swap(mine, "y")
        near = swap(w_value, "core")
        *first_pool, straight = pool(key_parts, added, place, 0, cut, (weights, 2 * share))
        one, first_pool, late_place, straight = lax.optimization_barrier(
            (one, first_pool, place, straight)
        )
        two = swap(one, "group")
        three = swap(straight, "y")
        one_across = swap(one, "core")
        second_pool = pool(key_parts, added, late_place, cut, blocks - cut)
        found = (first_pool, second_pool)
    else:
        full = lax.all_gather(w_value, ("y", "core"), axis=0, tiled=True)
        found = [
            pool(key_parts, added, place, at, n) for at, n in ((0, cut), (cut, blocks - cut))
        ]

    pooled = [part[0] for part in found]
    tops = jnp.concatenate([part[1] for part in found])
    sums = jnp.concatenate([part[2] for part in found])
    top = tops[:, :, :BLOCK].transpose(1, 0, 2).reshape(heads, patches)
    weight_sum = sums[:, :, :BLOCK].transpose(1, 0, 2).reshape(heads, patches)
    stats = jnp.stack([top, weight_sum])
    other = swap(stats, "core")
    stats, other, pooled = lax.optimization_barrier((stats, other, pooled))
    best = jnp.maximum(stats[0], other[0])
    factor = jnp.exp(top - best)
    total = stats[1] * factor + other[1] * jnp.exp(other[0] - best)
    stats = jnp.concatenate([best, total], axis=0).T

    if spread_groups:
        own_at, near_at, far, across = (jnp.int32(chan ^ j) * rows for j in range(4))
        starts = [jnp.int32(0), own_at, near_at, far + group * share, across + group * share]
        pieces = [w_value, near, one, one_across]
        start = value_products(
            pooled, width, pieces, jnp.stack(starts), 0, heads, None, None, F32
        )
        two, three, start = lax.optimization_barrier((two, three, start))
        pieces = [two, three, swap(two, "core"), swap(three, "core")]
        window, side = 2 * rows, jnp.int32(1 - chan // 2)
        starts = []
        for base in (far - side * window, across - side * window):
            starts += [base + (1 - group) * share, base + 2 * share]
        pooled, start = lax.optimization_barrier((pooled, start))
        loaded = load_window(pooled, side * window, window)
        pieces, loaded = lax.optimization_barrier((pieces, loaded))
        value = late_products(loaded, pieces, jnp.stack(starts), start, factor.T)
    else:
        value = value_products(
            pooled,
            width,
            [full],
            jnp.zeros((2,), jnp.int32),
            0,
            heads,
            None,
            jnp.broadcast_to(factor[:, :, None], (heads, patches, HEAD_DIM)),
            BF16,
        )

    low = tensors // 2
    chunks = [list(range(low, tensors)), list(range(low))]
    split = lambda x: [x[ks[0] * rows_own : (ks[-1] + 1) * rows_own] for ks in chunks]
    value = add_up(value, swap(value, "core")).astype(BF16)
    value, w_out, w_up = lax.optimization_barrier((value, w_out, w_up))
    values, stats = split(value), split(stats)
    for bit in chan_bits[1:]:
        found = [chan_swap(pack(v, st), bit) for v, st in zip(values, stats)]
        if bit == chan_bits[-1]:
            found[0], w_out, w_up = lax.optimization_barrier(
                (found[0], *load_weights(w_out, w_up))
            )
            _, far_out = project(values[0], stats[0], found[0], w_out, 1e9)
            found[1], _ = lax.optimization_barrier((found[1], far_out))
            low_out, low_sent = project(values[1], stats[1], found[1], w_out, LONG)
            break
        for n in range(2):
            theirs = unpack_stats(found[n], columns, stats[n].shape[1])
            best, total, *scales = join_stats(stats[n], theirs)
            stats[n] = jnp.concatenate([best, total], axis=1)
            scales = [jnp.repeat(scale, HEAD_DIM, axis=1) for scale in scales]
            joined = values[n] * scales[0] + found[n][:, :columns] * scales[1]
            values[n] = joined.astype(BF16)
    sent = list(low_sent.reshape(low, rows_own, -1))
    sent += list(far_out.reshape(tensors - low, rows_own, -1))
    got = [swap(sent[k], "tensor", k) for k in range(1, tensors)]
    projected = add_up(low_out[:rows_own], *got)
    own = projected.astype(BF16)

    arrived = [own] + [swap(own, "tensor", k) for k in range(1, tensors)]
    low_rows, w_down = lax.optimization_barrier((arrived[:low], w_down))
    far_rows, w_down = lax.optimization_barrier((arrived[low:], *load_weights(w_down)))
    gathered = []
    for pieces in (low_rows, far_rows):
        found = {0: jnp.concatenate(pieces, axis=0)}
        for bit in chan_bits[1:] + chan_bits[:1]:
            found.update({j ^ bit: chan_swap(found[j], bit) for j in list(found)})
        gathered.append(found)
    order = list(gathered[0])
    first = [j for j in order if j & chan_bits[-1]]
    order = first + [j for j in order if j not in first]
    places = chan ^ jnp.array(order, jnp.int32)
    xs = [[found[j] for j in order] for found in gathered]
    parts, hidden = mlp(xs, places, ln_gain, w_up, w_down, len(first))
    parts += down(hidden, places, w_down, len(first), len(order))
    held = dict(zip(order, parts))
    keep = [j for j in order if not j & 1]
    passed = {j: swap(held[j ^ 1], "core") for j in keep}
    held = {j: add_up(held[j], passed[j]).astype(BF16) for j in keep}
    parts = {j: split(x) for j, x in held.items()}
    for bit in chan_bits[1:]:
        keep = sorted(j for j in parts if not j & bit)
        passed = [chan_swap(jnp.stack([parts[j ^ bit][n] for j in keep]), bit) for n in (0, 1)]
        far = [add_up(parts[j][0], passed[0][n]).astype(BF16) for n, j in enumerate(keep)]
        near = [add_rows(parts[j][1], passed[1][n], LONG) for n, j in enumerate(keep)]
        parts = {j: [far[n], near[n]] for n, j in enumerate(keep)}
    got = [
        swap(x, "tensor", k) for k, x in zip(chunks[0], parts[0][0].reshape(low, rows_own, -1))
    ]
    sent = parts[0][1].reshape(low, rows_own, -1)
    got += [swap(sent[k], "tensor", k) for k in range(1, low)]
    return add_up(projected, sent[0], *got).astype(BF16)


def solution(mesh):
    groups, chans, tensors = (mesh.shape[a] for a in ("group", "chan", "tensor"))
    split = Mesh(
        mesh.devices.reshape(groups, chans // 2, 2, tensors), ("group", "y", "core", "tensor")
    )
    chan = ("y", "core")
    in_specs = (
        P(chan, "group", None),
        P(),
        P(),
        P(),
        P("tensor"),
        P(chan, "tensor"),
        P(chan, "tensor"),
        P("tensor", chan),
        P(),
        P(None, (*chan, "tensor")),
        P((*chan, "tensor"), None),
    )
    out_specs = P(("group", "tensor"), chan)
    return jax.shard_map(
        local, mesh=split, in_specs=in_specs, out_specs=out_specs, check_vma=False
    )
```

```python
import functools

import jax
import jax.numpy as jnp
from jax import lax
from jax.experimental import pallas as pl
from jax.experimental.pallas import tpu as pltpu
from jax.sharding import Mesh, PartitionSpec as P

HEAD_DIM = 128
BLOCK = 16
LANES = 128
NEG = -1e30
F32 = jnp.float32
BF16 = jnp.bfloat16
NT = (((1,), (1,)), ((), ()))
MIB = 1 << 20
LONG = 1e10


def swap(x, axis, bit=1):
    size = lax.axis_size(axis)
    return lax.ppermute(x, axis, [(i, i ^ bit) for i in range(size)])


def cost(flops, size):
    return pl.CostEstimate(flops=int(flops), transcendentals=0, bytes_accessed=int(size))


def exact_parts(x):
    out, rest = [], x
    for _ in range(3):
        piece = lax.reduce_precision(rest, 8, 7)
        out.append(piece.astype(BF16))
        rest = rest - piece
    return out


def pack(value, stats):
    tail = jnp.concatenate(exact_parts(stats), axis=1)
    tail = jnp.pad(tail, ((0, 0), (0, -tail.shape[1] % LANES)))
    return jnp.concatenate([value, tail], axis=1)


def unpack_stats(packed, columns, count):
    tail = packed[:, columns:].astype(F32)
    return tail[:, :count] + tail[:, count : 2 * count] + tail[:, 2 * count : 3 * count]


def join_stats(own, got):
    heads = own.shape[1] // 2
    best = jnp.maximum(own[:, :heads], got[:, :heads])
    mine, theirs = jnp.exp(own[:, :heads] - best), jnp.exp(got[:, :heads] - best)
    return best, own[:, heads:] * mine + got[:, heads:] * theirs, mine, theirs


def bits_of(axis):
    size, bit, found = lax.axis_size(axis), 1, []
    while bit < size:
        found.append(bit)
        bit *= 2
    return found


def chan_swap(x, bit):
    return swap(x, "core", 1) if bit == 1 else swap(x, "y", bit // 2)


def split_parts(x, parts):
    out, rest = [], x
    for _ in range(parts):
        piece = rest.astype(BF16)
        out.append(piece)
        rest = rest - piece.astype(F32)
    return out


def pool_kernel(heads, chan_count, first, count, per_owner, taken, place, tokens, *rest):
    if taken is not None:
        whole, rest = rest[0], rest[1:]
    added, live, rest = rest[0], rest[1], rest[2:]
    key_refs = rest[:chan_count]
    pooled_out, top_out, sum_out = rest[chan_count : chan_count + 3]
    rest = rest[chan_count + 3 :]
    if taken is not None:
        out_rows, rest = rest[0], rest[1:]
    held, arrived, pooled, stored, keys, add_scores, scores, spreads = rest[:8]
    if taken is not None:
        held_rows, rows_in, rows_out = rest[8:]
        copy_in = pltpu.make_async_copy(
            whole.at[pl.ds(taken, out_rows.shape[0]), :], held_rows, rows_in
        )
        copy_out = pltpu.make_async_copy(held_rows, out_rows, rows_out)
    slots, _, width = tokens.shape
    block = held.shape[2]
    rows = slots * block
    lanes = scores.shape[1]
    groups = lanes // LANES
    padded = added.shape[0]

    def fetch(i):
        at = first + i
        row = (((at // per_owner) ^ place[0]) * per_owner + at % per_owner) * block
        return pltpu.make_async_copy(
            tokens.at[:, pl.ds(pl.multiple_of(row, block), block), :],
            held.at[i],
            arrived.at[i],
        )

    fetch(0).start()
    if count > 1:
        fetch(1).start()

    piece = width // chan_count
    for j in range(chan_count):
        at = pl.multiple_of(place[1 + j] * piece, piece)
        high, low = split_parts(key_refs[j][...], 2)
        keys[:, pl.ds(at, piece)] = jnp.concatenate([high, low], axis=0)
    raw = lax.dot_general(keys[...], added[...], NT, preferred_element_type=F32)
    raw = raw[:heads] + raw[heads:]
    lane = lax.broadcasted_iota(jnp.int32, (padded, lanes), 1)
    slot = lax.broadcasted_iota(jnp.int32, (padded, lanes), 0)
    expand = jnp.where(lane // block == slot, 1.0, 0.0).astype(BF16)
    total = jnp.zeros((heads, lanes), F32)
    for part in split_parts(raw, 3):
        total = total + jnp.dot(part, expand, preferred_element_type=F32)
    add_scores[...] = total
    scores[...] = jnp.zeros_like(scores)

    def fold(x, combine):
        out = x[:, :LANES]
        for g in range(1, groups):
            out = combine(out, x[:, g * LANES : (g + 1) * LANES])
        shift = LANES // 2
        while shift >= block:
            out = combine(out, pltpu.roll(out, shift, 1))
            shift //= 2
        return out

    def store(i):
        return pltpu.make_async_copy(
            pooled.at[i], pooled_out.at[:, pl.ds(i * block, block), :], stored.at[i]
        )

    step = min(width, 512)
    by_slot = None
    for i in range(count + 1):
        if i < count:
            fetch(i).wait()
            if i + 2 < count:
                fetch(i + 2).start()
        raw = None
        for at in range(0, width, step):
            if i < count:
                part = held[i, :, :, at : at + step].reshape(rows, step)
                got = lax.dot_general(
                    keys[:, at : at + step], part, NT, preferred_element_type=F32
                )
                raw = got if raw is None else raw + got
            if i > 0:
                part = held[i - 1, :, :, at : at + step].reshape(rows, step)
                got = jnp.dot(spreads[:, :rows], part, preferred_element_type=F32)
                got = got + jnp.dot(
                    by_slot, added[:, at : at + step], preferred_element_type=F32
                )
                pooled[i - 1, :, :, at : at + step] = got.reshape(heads, block, step).astype(BF16)
        if i > 0:
            store(i - 1).start()
        if i == 1 and taken is not None:
            copy_in.start()
        if i == count - 1 and taken is not None:
            copy_in.wait()
            copy_out.start()
        if i == count:
            break
        scores[:, :rows] = raw[:heads] + raw[heads:]
        alive = live[...] > 0.0
        masked = jnp.where(alive, scores[...] + add_scores[...], NEG)
        top = fold(masked, jnp.maximum)
        wide_top = jnp.concatenate([top] * groups, axis=1)
        weights = jnp.where(alive, jnp.exp(masked - wide_top), 0.0)
        weights = weights.astype(BF16).astype(F32)
        top_out[i] = top
        sum_out[i] = fold(weights, jnp.add)
        patch = lax.broadcasted_iota(jnp.int32, (heads, block, lanes), 1)
        column = lax.broadcasted_iota(jnp.int32, (heads, block, lanes), 2)
        spread = jnp.where(
            column % block == patch, jnp.broadcast_to(weights[:, None, :], patch.shape), 0.0
        )
        spread = spread.reshape(heads * block, lanes).astype(BF16)
        spreads[...] = spread
        pick = jnp.where(
            lax.broadcasted_iota(jnp.int32, (lanes, padded), 0) // block
            == lax.broadcasted_iota(jnp.int32, (lanes, padded), 1),
            1.0,
            0.0,
        ).astype(BF16)
        by_slot = jnp.dot(spread, pick, preferred_element_type=F32).astype(BF16)
    for i in range(count):
        store(i).wait()
    if taken is not None:
        copy_out.wait()


def pool_tokens(tokens, added, live, key_parts, place, heads, rows_own, first, count, take=None):
    slots, _, width = tokens.shape
    lanes = live.shape[1]
    vmem, hbm = (pl.BlockSpec(memory_space=m) for m in (pltpu.VMEM, pltpu.HBM))
    extra_in, extra_out, extra_scratch, taken = [], [], [], None
    if take is not None:
        whole, taken = take
        extra_in = [pltpu.with_memory_space_constraint(whole, pltpu.HBM)]
        extra = (whole.shape[0] - taken, whole.shape[1])
        extra_out = [pltpu.HBM(extra, whole.dtype)]
        extra_scratch = [pltpu.VMEM(extra, whole.dtype)] + [pltpu.SemaphoreType.DMA] * 2
    return pl.pallas_call(
        functools.partial(
            pool_kernel, heads, len(key_parts), first, count, max(rows_own // BLOCK, 1), taken
        ),
        out_shape=[
            pltpu.HBM((heads, count * BLOCK, width), BF16),
            jax.ShapeDtypeStruct((count, heads, LANES), F32),
            jax.ShapeDtypeStruct((count, heads, LANES), F32),
        ]
        + extra_out,
        in_specs=[pl.BlockSpec(memory_space=pltpu.SMEM), hbm]
        + [hbm] * len(extra_in)
        + [vmem] * (2 + len(key_parts)),
        out_specs=[hbm, vmem, vmem] + [hbm] * len(extra_out),
        scratch_shapes=[
            pltpu.VMEM((count, slots, BLOCK, width), BF16),
            pltpu.SemaphoreType.DMA((count,)),
            pltpu.VMEM((count, heads, BLOCK, width), BF16),
            pltpu.SemaphoreType.DMA((count,)),
            pltpu.VMEM((2 * heads, width), BF16),
            pltpu.VMEM((heads, lanes), F32),
            pltpu.VMEM((heads, lanes), F32),
            pltpu.VMEM((heads * BLOCK, lanes), BF16),
        ]
        + extra_scratch,
        compiler_params=pltpu.CompilerParams(
            vmem_limit_bytes=3 * MIB + count * (slots + heads) * BLOCK * width * 2
        ),
        cost_estimate=cost(
            count * slots * BLOCK * width * 1024, count * (slots + heads) * BLOCK * width * 2
        ),
        name="pool_tokens",
    )(
        place,
        pltpu.with_memory_space_constraint(tokens, pltpu.HBM),
        *extra_in,
        added,
        live,
        *key_parts,
    )


def value_kernel(together, pool_count, piece_count, has_start, has_factor, offsets, *rest):
    pooled, rest = rest[:pool_count], rest[pool_count:]
    pieces, rest = rest[:piece_count], rest[piece_count:]
    total = None
    for n, piece in enumerate(pieces):
        depth = piece.shape[0]
        at = pl.multiple_of(offsets[1 + n], LANES)
        stacked = jnp.concatenate(
            [part[h, :, pl.ds(at, depth)] for h in range(together) for part in pooled],
            axis=0,
        )
        got = jnp.dot(stacked, piece[...], preferred_element_type=F32)
        total = got if total is None else total + got
    patches = total.shape[0] // together
    out = rest[-1]
    for h in range(together):
        columns = slice(h * HEAD_DIM, (h + 1) * HEAD_DIM)
        got = total[h * patches : (h + 1) * patches, columns]
        if has_start:
            got = got + rest[0][:, columns]
        if has_factor:
            got = got * rest[-2][h]
        out[:, columns] = got.astype(out.dtype)


def value_products(pooled, window, pieces, offsets, first_head, head_count, start, factor, kind):
    patches, width = sum(part.shape[1] for part in pooled), pooled[0].shape[2]
    together = 2 if head_count % 2 == 0 else 1
    wide = together * HEAD_DIM
    first = first_head // together
    specs = [
        pl.BlockSpec((together, part.shape[1], window), lambda h, o: (first + h, 0, o[0]))
        for part in pooled
    ]
    operands = [pltpu.with_memory_space_constraint(part, pltpu.HBM) for part in pooled]
    for piece in pieces:
        specs.append(pl.BlockSpec((piece.shape[0], wide), lambda h, o: (0, first + h)))
        operands.append(piece)
    if start is not None:
        specs.append(pl.BlockSpec((patches, wide), lambda h, o: (0, first + h)))
        operands.append(start)
    if factor is not None:
        specs.append(pl.BlockSpec((together, patches, HEAD_DIM), lambda h, o: (first + h, 0, 0)))
        operands.append(factor)
    return pl.pallas_call(
        functools.partial(
            value_kernel,
            together,
            len(pooled),
            len(pieces),
            start is not None,
            factor is not None,
        ),
        out_shape=jax.ShapeDtypeStruct((patches, head_count * HEAD_DIM), kind),
        grid_spec=pltpu.PrefetchScalarGridSpec(
            num_scalar_prefetch=1,
            grid=(head_count // together,),
            in_specs=specs,
            out_specs=pl.BlockSpec((patches, wide), lambda h, o: (0, h)),
        ),
        compiler_params=pltpu.CompilerParams(vmem_limit_bytes=14 * MIB),
        cost_estimate=cost(
            4 * patches * width * head_count * HEAD_DIM, sum(x.size * 2 for x in operands)
        ),
        name="value_products",
    )(offsets, *operands)


def take_kernel(at, whole, out, held, arrived, left):
    rows = pl.ds(pl.multiple_of(at[0], 16), out.shape[0])
    copy = pltpu.make_async_copy(whole.at[rows, :], held, arrived)
    copy.start()
    copy.wait()
    copy = pltpu.make_async_copy(held, out, left)
    copy.start()
    copy.wait()


def take_rows(whole, at, count):
    return pl.pallas_call(
        take_kernel,
        out_shape=pltpu.HBM((count, whole.shape[1]), whole.dtype),
        in_specs=[pl.BlockSpec(memory_space=pltpu.SMEM), pl.BlockSpec(memory_space=pltpu.HBM)],
        out_specs=pl.BlockSpec(memory_space=pltpu.HBM),
        scratch_shapes=[
            pltpu.VMEM((count, whole.shape[1]), whole.dtype),
            pltpu.SemaphoreType.DMA,
            pltpu.SemaphoreType.DMA,
        ],
        compiler_params=pltpu.CompilerParams(vmem_limit_bytes=2 * MIB),
        name="take_rows",
    )(jnp.reshape(at, (1,)), pltpu.with_memory_space_constraint(whole, pltpu.HBM))


def load_kernel(firsts, *refs):
    half = len(refs) // 2
    arrived = refs[-1]
    copies = []
    for i in range(half):
        rows = pl.ds(firsts[i], refs[half + i].shape[0])
        copies.append(
            pltpu.make_async_copy(refs[i].at[rows, :], refs[half + i], arrived.at[i])
        )
    for copy in copies:
        copy.start()
    for copy in copies:
        copy.wait()


def load_rows(*ranges):
    weights = [w for w, _, _ in ranges]
    shapes = [(count, w.shape[1]) for w, _, count in ranges]
    return pl.pallas_call(
        functools.partial(load_kernel, [first for _, first, _ in ranges]),
        out_shape=[pltpu.VMEM(shape, w.dtype) for shape, w in zip(shapes, weights)],
        in_specs=[pl.BlockSpec(memory_space=pltpu.HBM)] * len(weights),
        out_specs=[pl.BlockSpec(memory_space=pltpu.VMEM)] * len(weights),
        scratch_shapes=[pltpu.SemaphoreType.DMA((len(weights),))],
        compiler_params=pltpu.CompilerParams(vmem_limit_bytes=MIB),
        cost_estimate=cost(0, sum(2 * r * c for r, c in shapes)),
        name="load_weights",
    )(*[pltpu.with_memory_space_constraint(w, pltpu.HBM) for w in weights])


def load_weights(*weights):
    return load_rows(*[(w, 0, w.shape[0]) for w in weights])


def window_kernel(count, at, *refs):
    parts, outs, arrived = refs[:count], refs[count : 2 * count], refs[-1]
    copies = []
    for n in range(count):
        columns = pl.ds(pl.multiple_of(at[0], outs[n].shape[2]), outs[n].shape[2])
        copies.append(
            pltpu.make_async_copy(parts[n].at[:, :, columns], outs[n], arrived.at[n])
        )
    for copy in copies:
        copy.start()
    for copy in copies:
        copy.wait()


def load_window(parts, at, window):
    size = sum(part.size // part.shape[2] * window * 2 for part in parts)
    return pl.pallas_call(
        functools.partial(window_kernel, len(parts)),
        out_shape=[pltpu.VMEM((*part.shape[:2], window), part.dtype) for part in parts],
        in_specs=[pl.BlockSpec(memory_space=pltpu.SMEM)]
        + [pl.BlockSpec(memory_space=pltpu.HBM)] * len(parts),
        out_specs=[pl.BlockSpec(memory_space=pltpu.VMEM)] * len(parts),
        scratch_shapes=[pltpu.SemaphoreType.DMA((len(parts),))],
        compiler_params=pltpu.CompilerParams(vmem_limit_bytes=MIB),
        cost_estimate=pl.CostEstimate(flops=0, transcendentals=0, bytes_accessed=size),
        name="load_window",
    )(jnp.reshape(at, (1,)), *[pltpu.with_memory_space_constraint(p, pltpu.HBM) for p in parts])


def late_kernel(pool_count, piece_count, offsets, *rest):
    pooled, rest = rest[:pool_count], rest[pool_count:]
    pieces, (start, factor, out) = rest[:piece_count], rest[piece_count:]
    patches = out.shape[0]
    heads = out.shape[1] // HEAD_DIM
    together = 2 if heads % 2 == 0 else 1
    wide = together * HEAD_DIM
    for head in range(0, heads, together):
        first = head * HEAD_DIM
        total = None
        for n, piece in enumerate(pieces):
            depth = piece.shape[0]
            at = pl.multiple_of(offsets[n], LANES)
            stacked = jnp.concatenate(
                [part[head + h, :, pl.ds(at, depth)] for h in range(together) for part in pooled],
                axis=0,
            )
            got = jnp.dot(stacked, piece[:, first : first + wide], preferred_element_type=F32)
            total = got if total is None else total + got
        for h in range(together):
            columns = slice(first + h * HEAD_DIM, first + (h + 1) * HEAD_DIM)
            got = total[h * patches : (h + 1) * patches, h * HEAD_DIM : (h + 1) * HEAD_DIM]
            got = (got + start[:, columns]) * factor[:, head + h : head + h + 1]
            out[:, columns] = got.astype(out.dtype)


def late_products(pooled, pieces, offsets, start, factor):
    patches = sum(part.shape[1] for part in pooled)
    heads = pooled[0].shape[0]
    vmem = pl.BlockSpec(memory_space=pltpu.VMEM)
    depth = sum(piece.shape[0] for piece in pieces)
    return pl.pallas_call(
        functools.partial(late_kernel, len(pooled), len(pieces)),
        out_shape=jax.ShapeDtypeStruct((patches, heads * HEAD_DIM), BF16),
        in_specs=[pl.BlockSpec(memory_space=pltpu.SMEM)]
        + [vmem] * (len(pooled) + len(pieces) + 2),
        out_specs=vmem,
        compiler_params=pltpu.CompilerParams(vmem_limit_bytes=8 * MIB),
        cost_estimate=cost(
            4 * patches * depth * heads * HEAD_DIM, sum(piece.size * 2 for piece in pieces)
        ),
        name="late_products",
    )(
        offsets,
        *[pltpu.with_memory_space_constraint(part, pltpu.VMEM) for part in pooled],
        *pieces,
        start,
        factor,
    )


def project_kernel(own, stats, got, weights, out, sent):
    columns, count = own.shape[1], stats.shape[1]
    _, total, mine, theirs = join_stats(stats[...], unpack_stats(got[...], columns, count))
    mine, theirs = mine / total, theirs / total
    rows = []
    for h in range(count // 2):
        at = slice(h * HEAD_DIM, (h + 1) * HEAD_DIM)
        row = own[:, at].astype(F32) * mine[:, h : h + 1]
        row = row + got[:, at].astype(F32) * theirs[:, h : h + 1]
        rows.append(row.astype(BF16))
    rows = jnp.concatenate(rows, axis=1)
    found = jnp.dot(rows, weights[...], preferred_element_type=F32)
    out[...] = found
    sent[...] = found.astype(BF16)


def project(own, stats, got, weights, guess):
    vmem = pl.BlockSpec(memory_space=pltpu.VMEM)
    shape = (own.shape[0], weights.shape[1])
    return pl.pallas_call(
        project_kernel,
        out_shape=[jax.ShapeDtypeStruct(shape, F32), jax.ShapeDtypeStruct(shape, BF16)],
        in_specs=[vmem] * 4,
        out_specs=[vmem] * 2,
        compiler_params=pltpu.CompilerParams(vmem_limit_bytes=4 * MIB),
        cost_estimate=cost(guess, own.size * 4),
        name="project",
    )(own, stats, got, pltpu.with_memory_space_constraint(weights, pltpu.VMEM))


def add_kernel(left, right, out):
    out[...] = (left[...].astype(F32) + right[...].astype(F32)).astype(out.dtype)


def add_rows(left, right, guess):
    vmem = pl.BlockSpec(memory_space=pltpu.VMEM)
    return pl.pallas_call(
        add_kernel,
        out_shape=jax.ShapeDtypeStruct(left.shape, left.dtype),
        in_specs=[vmem] * 2,
        out_specs=vmem,
        compiler_params=pltpu.CompilerParams(vmem_limit_bytes=4 * MIB),
        cost_estimate=cost(guess, left.size * 6),
        name="add_rows",
    )(left, right)


def down_columns(hidden, order, parts, n):
    piece = parts[0].shape[1] // order.shape[0]
    at = pl.multiple_of(order[n] * piece, piece)
    total, row = None, 0
    for part in parts:
        depth = part.shape[0]
        mine = hidden[:, row : row + depth]
        got = jnp.dot(mine, part[:, pl.ds(at, piece)], preferred_element_type=F32)
        total, row = got if total is None else total + got, row + depth
    return total.astype(BF16)


def mlp_kernel(count, chunks, outs, downs, order, *refs):
    xs = refs[: count * chunks]
    gain, w_up, *rest = refs[count * chunks :]
    w_down, (*found, hidden, normed) = rest[:downs], rest[downs:]
    piece = xs[0].shape[1]
    width = count * piece
    at_row = 0
    for chunk in range(chunks):
        x = xs[chunk * count : (chunk + 1) * count]
        rows = x[0].shape[0]
        mean = jnp.zeros((rows, 1), F32)
        for j in range(count):
            mean = mean + jnp.sum(x[j][...].astype(F32), axis=1, keepdims=True)
        mean = mean / width
        variance = jnp.zeros((rows, 1), F32)
        for j in range(count):
            centered = x[j][...].astype(F32) - mean
            variance = variance + jnp.sum(centered * centered, axis=1, keepdims=True)
        scale = lax.rsqrt(variance / width + 1e-05)
        for j in range(count):
            got = ((x[j][...].astype(F32) - mean) * scale * gain[order[j]]).astype(BF16)
            normed[j, at_row : at_row + rows, :] = got
        at_row += rows
    total = None
    for j in range(count):
        at = pl.multiple_of(order[j] * piece, piece)
        got = jnp.dot(normed[j], w_up[pl.ds(at, piece), :], preferred_element_type=F32)
        total = got if total is None else total + got
    active = jax.nn.gelu(total).astype(BF16)
    hidden[...] = active
    for n in range(outs):
        found[n][...] = down_columns(active, order, w_down, n)


def mlp(xs, order, ln_gain, w_up, w_down, outs):
    count, piece = len(xs[0]), xs[0][0].shape[1]
    patches = sum(x[0].shape[0] for x in xs)
    vmem = pl.BlockSpec(memory_space=pltpu.VMEM)
    w_up, *w_down = (pltpu.with_memory_space_constraint(w, pltpu.VMEM) for w in (w_up, *w_down))
    flat = [x for chunk in xs for x in chunk]
    *found, hidden = pl.pallas_call(
        functools.partial(mlp_kernel, count, len(xs), outs, len(w_down)),
        out_shape=[jax.ShapeDtypeStruct((patches, piece), BF16)] * outs
        + [jax.ShapeDtypeStruct((patches, w_up.shape[1]), BF16)],
        in_specs=[pl.BlockSpec(memory_space=pltpu.SMEM)] + [vmem] * (len(flat) + 2 + len(w_down)),
        out_specs=[vmem] * (outs + 1),
        scratch_shapes=[pltpu.VMEM((count, patches, piece), BF16)],
        compiler_params=pltpu.CompilerParams(vmem_limit_bytes=8 * MIB),
        name="norm_mlp",
    )(order, *flat, ln_gain.reshape(count, 1, piece), w_up, *w_down)
    return found, hidden


def down_kernel(first, downs, order, hidden, *refs):
    for n, out in enumerate(refs[downs:]):
        out[...] = down_columns(hidden[...], order, refs[:downs], first + n)


def down(hidden, order, w_down, first, last):
    vmem = pl.BlockSpec(memory_space=pltpu.VMEM)
    shape = (hidden.shape[0], w_down[0].shape[1] // last)
    return pl.pallas_call(
        functools.partial(down_kernel, first, len(w_down)),
        out_shape=[jax.ShapeDtypeStruct(shape, BF16)] * (last - first),
        in_specs=[pl.BlockSpec(memory_space=pltpu.SMEM)] + [vmem] * (1 + len(w_down)),
        out_specs=[vmem] * (last - first),
        compiler_params=pltpu.CompilerParams(vmem_limit_bytes=4 * MIB),
        cost_estimate=cost(2e9, hidden.size * 2),
        name="down",
    )(order, hidden, *[pltpu.with_memory_space_constraint(w, pltpu.VMEM) for w in w_down])


def key_vectors(query, w_key, heads):
    columns = query.shape[0]
    mine = jnp.arange(columns)[None, :] // HEAD_DIM == jnp.arange(heads)[:, None]
    rows = [jnp.where(mine, part[None, :], 0) for part in exact_parts(query)]
    stacked = jnp.concatenate(rows, axis=0).astype(BF16)
    got = lax.dot_general(stacked, w_key, NT, preferred_element_type=F32)
    scale = 1.0 / jnp.sqrt(F32(HEAD_DIM))
    return (got.reshape(3, heads, -1).sum(axis=0)) * scale


def add_up(*terms):
    total = terms[0].astype(F32)
    for term in terms[1:]:
        total = total + term.astype(F32)
    return total


def local(
    tokens, chan_table, chan_valid, chan_embed, query, w_key, w_value, w_out, ln_gain, w_up, w_down
):
    slots, patches, width = tokens.shape
    columns = query.shape[0]
    heads = columns // HEAD_DIM
    group, tensor = lax.axis_index("group"), lax.axis_index("tensor")
    tensors = lax.axis_size("tensor")
    chan = lax.axis_index(("y", "core"))
    chans = lax.axis_size("y") * lax.axis_size("core")
    chan_bits = [1] + [2 * b for b in bits_of("y")]
    tensor_bits = bits_of("tensor")
    rows_own = patches // tensors

    key_parts = key_vectors(query, w_key, heads)[None]
    key_order = [0]
    weights = w_value
    for bit in chan_bits:
        key_parts = jnp.concatenate([key_parts, chan_swap(key_parts, bit)], axis=0)
        key_order = key_order + [j ^ bit for j in key_order]
        if bit == 1:
            key_parts, weights = lax.optimization_barrier((key_parts, weights))
    key_place = chan ^ jnp.array(key_order, jnp.int32)
    place = jnp.concatenate([jnp.reshape(tensor, (1,)).astype(jnp.int32), key_place])

    padded = -(-slots // 16) * 16
    lanes = -(-(slots * BLOCK) // LANES) * LANES
    slot_ids = lax.dynamic_slice_in_dim(chan_table, chan * slots, slots)
    slot_ids = jnp.pad(slot_ids, (0, padded - slots), constant_values=-1)
    matches = slot_ids[:, None] == jnp.arange(chan_embed.shape[0], dtype=jnp.int32)[None, :]
    added = jnp.dot(matches.astype(BF16), chan_embed, preferred_element_type=F32).astype(BF16)
    live_slots = jnp.sum(matches.astype(jnp.int32) * chan_valid[None, :], axis=1) > 0
    live = jnp.repeat(live_slots.astype(F32), BLOCK)
    live = jnp.pad(live, (0, max(lanes - live.shape[0], 0)))[:lanes][None]

    blocks = patches // BLOCK
    spread_groups = lax.axis_size("y") == 2 and lax.axis_size("group") == 2
    cut = 3 * blocks // 4

    def pool(keys, added, where, first, count, take=None):
        keys = [keys[j] for j in range(chans)]
        return pool_tokens(
            tokens, added, live, keys, where, heads, rows_own, first, count, take
        )

    if spread_groups:
        rows = w_value.shape[0]
        share = 3 * rows // 8
        mine = take_rows(weights, group * share, share)
        key_parts, mine, added, live = lax.optimization_barrier((key_parts, mine, added, live))
        one = swap(mine, "y")
        near = swap(w_value, "core")
        *first_pool, straight = pool(key_parts, added, place, 0, cut, (weights, 2 * share))
        one, first_pool, late_place, straight = lax.optimization_barrier(
            (one, first_pool, place, straight)
        )
        two = swap(one, "group")
        three = swap(straight, "y")
        one_across = swap(one, "core")
        second_pool = pool(key_parts, added, late_place, cut, blocks - cut)
        found = (first_pool, second_pool)
    else:
        full = lax.all_gather(w_value, ("y", "core"), axis=0, tiled=True)
        found = [
            pool(key_parts, added, place, at, n) for at, n in ((0, cut), (cut, blocks - cut))
        ]

    pooled = [part[0] for part in found]
    tops = jnp.concatenate([part[1] for part in found])
    sums = jnp.concatenate([part[2] for part in found])
    top = tops[:, :, :BLOCK].transpose(1, 0, 2).reshape(heads, patches)
    weight_sum = sums[:, :, :BLOCK].transpose(1, 0, 2).reshape(heads, patches)
    stats = jnp.stack([top, weight_sum])
    other = swap(stats, "core")
    stats, other, pooled = lax.optimization_barrier((stats, other, pooled))
    best = jnp.maximum(stats[0], other[0])
    factor = jnp.exp(top - best)
    total = stats[1] * factor + other[1] * jnp.exp(other[0] - best)
    stats = jnp.concatenate([best, total], axis=0).T

    if spread_groups:
        own_at, near_at, far, across = (jnp.int32(chan ^ j) * rows for j in range(4))
        starts = [jnp.int32(0), own_at, near_at, far + group * share, across + group * share]
        pieces = [w_value, near, one, one_across]
        start = value_products(
            pooled, width, pieces, jnp.stack(starts), 0, heads, None, None, F32
        )
        two, three, start = lax.optimization_barrier((two, three, start))
        pieces = [two, three, swap(two, "core"), swap(three, "core")]
        window, side = 2 * rows, jnp.int32(1 - chan // 2)
        starts = []
        for base in (far - side * window, across - side * window):
            starts += [base + (1 - group) * share, base + 2 * share]
        pooled, start = lax.optimization_barrier((pooled, start))
        loaded = load_window(pooled, side * window, window)
        pieces, loaded = lax.optimization_barrier((pieces, loaded))
        value = late_products(loaded, pieces, jnp.stack(starts), start, factor.T)
    else:
        value = value_products(
            pooled,
            width,
            [full],
            jnp.zeros((2,), jnp.int32),
            0,
            heads,
            None,
            jnp.broadcast_to(factor[:, :, None], (heads, patches, HEAD_DIM)),
            BF16,
        )

    low = tensors // 2
    chunks = [list(range(low, tensors)), list(range(low))]
    split = lambda x: [x[ks[0] * rows_own : (ks[-1] + 1) * rows_own] for ks in chunks]
    value = add_up(value, swap(value, "core")).astype(BF16)
    value, w_out, w_up = lax.optimization_barrier((value, w_out, w_up))
    values, stats = split(value), split(stats)
    for bit in chan_bits[1:]:
        found = [chan_swap(pack(v, st), bit) for v, st in zip(values, stats)]
        if bit == chan_bits[-1]:
            found[0], w_out, w_up = lax.optimization_barrier(
                (found[0], *load_weights(w_out, w_up))
            )
            _, far_out = project(values[0], stats[0], found[0], w_out, 1e9)
            _, w_down = lax.optimization_barrier((far_out, w_down))
            cut = w_down.shape[0] // 4
            (w_first,) = load_rows((w_down, 0, cut))
            found[1], w_first = lax.optimization_barrier((found[1], w_first))
            low_out, low_sent = project(values[1], stats[1], found[1], w_out, LONG)
            break
        for n in range(2):
            theirs = unpack_stats(found[n], columns, stats[n].shape[1])
            best, total, *scales = join_stats(stats[n], theirs)
            stats[n] = jnp.concatenate([best, total], axis=1)
            scales = [jnp.repeat(scale, HEAD_DIM, axis=1) for scale in scales]
            joined = values[n] * scales[0] + found[n][:, :columns] * scales[1]
            values[n] = joined.astype(BF16)
    sent = list(low_sent.reshape(low, rows_own, -1))
    sent += list(far_out.reshape(tensors - low, rows_own, -1))
    got = [swap(sent[k], "tensor", k) for k in range(1, tensors)]
    projected = add_up(low_out[:rows_own], *got)
    own = projected.astype(BF16)

    arrived = [own] + [swap(own, "tensor", k) for k in range(1, tensors)]
    low_rows, w_down = lax.optimization_barrier((arrived[:low], w_down))
    far_rows, w_rest = lax.optimization_barrier(
        (arrived[low:], *load_rows((w_down, cut, w_down.shape[0] - cut)))
    )
    w_down = [w_first, w_rest]
    gathered = []
    for pieces in (low_rows, far_rows):
        found = {0: jnp.concatenate(pieces, axis=0)}
        for bit in chan_bits[1:] + chan_bits[:1]:
            found.update({j ^ bit: chan_swap(found[j], bit) for j in list(found)})
        gathered.append(found)
    order = list(gathered[0])
    first = [j for j in order if j & chan_bits[-1]]
    order = first + [j for j in order if j not in first]
    places = chan ^ jnp.array(order, jnp.int32)
    xs = [[found[j] for j in order] for found in gathered]
    parts, hidden = mlp(xs, places, ln_gain, w_up, w_down, len(first))
    parts += down(hidden, places, w_down, len(first), len(order))
    held = dict(zip(order, parts))
    keep = [j for j in order if not j & 1]
    passed = {j: swap(held[j ^ 1], "core") for j in keep}
    held = {j: add_up(held[j], passed[j]).astype(BF16) for j in keep}
    parts = {j: split(x) for j, x in held.items()}
    for bit in chan_bits[1:]:
        keep = sorted(j for j in parts if not j & bit)
        passed = [chan_swap(jnp.stack([parts[j ^ bit][n] for j in keep]), bit) for n in (0, 1)]
        far = [add_up(parts[j][0], passed[0][n]).astype(BF16) for n, j in enumerate(keep)]
        near = [add_rows(parts[j][1], passed[1][n], LONG) for n, j in enumerate(keep)]
        parts = {j: [far[n], near[n]] for n, j in enumerate(keep)}
    got = [
        swap(x, "tensor", k) for k, x in zip(chunks[0], parts[0][0].reshape(low, rows_own, -1))
    ]
    sent = parts[0][1].reshape(low, rows_own, -1)
    got += [swap(sent[k], "tensor", k) for k in range(1, low)]
    return add_up(projected, sent[0], *got).astype(BF16)


def solution(mesh):
    groups, chans, tensors = (mesh.shape[a] for a in ("group", "chan", "tensor"))
    split = Mesh(
        mesh.devices.reshape(groups, chans // 2, 2, tensors), ("group", "y", "core", "tensor")
    )
    chan = ("y", "core")
    in_specs = (
        P(chan, "group", None),
        P(),
        P(),
        P(),
        P("tensor"),
        P(chan, "tensor"),
        P(chan, "tensor"),
        P("tensor", chan),
        P(),
        P(None, (*chan, "tensor")),
        P((*chan, "tensor"), None),
    )
    out_specs = P(("group", "tensor"), chan)
    return jax.shard_map(
        local, mesh=split, in_specs=in_specs, out_specs=out_specs, check_vma=False
    )
```

```python
import functools

import jax
import jax.numpy as jnp
from jax import lax
from jax.experimental import pallas as pl
from jax.experimental.pallas import tpu as pltpu
from jax.sharding import Mesh, PartitionSpec as P

HEAD_DIM = 128
BLOCK = 16
LANES = 128
NEG = -1e30
F32 = jnp.float32
BF16 = jnp.bfloat16
NT = (((1,), (1,)), ((), ()))
MIB = 1 << 20
LONG = 1e10


def swap(x, axis, bit=1):
    size = lax.axis_size(axis)
    return lax.ppermute(x, axis, [(i, i ^ bit) for i in range(size)])


def cost(flops, size):
    return pl.CostEstimate(flops=int(flops), transcendentals=0, bytes_accessed=int(size))


def exact_parts(x):
    out, rest = [], x
    for _ in range(3):
        piece = lax.reduce_precision(rest, 8, 7)
        out.append(piece.astype(BF16))
        rest = rest - piece
    return out


def pack(value, stats):
    tail = jnp.concatenate(exact_parts(stats), axis=1)
    tail = jnp.pad(tail, ((0, 0), (0, -tail.shape[1] % LANES)))
    return jnp.concatenate([value, tail], axis=1)


def unpack_stats(packed, columns, count):
    tail = packed[:, columns:].astype(F32)
    return tail[:, :count] + tail[:, count : 2 * count] + tail[:, 2 * count : 3 * count]


def join_stats(own, got):
    heads = own.shape[1] // 2
    best = jnp.maximum(own[:, :heads], got[:, :heads])
    mine, theirs = jnp.exp(own[:, :heads] - best), jnp.exp(got[:, :heads] - best)
    return best, own[:, heads:] * mine + got[:, heads:] * theirs, mine, theirs


def bits_of(axis):
    size, bit, found = lax.axis_size(axis), 1, []
    while bit < size:
        found.append(bit)
        bit *= 2
    return found


def chan_swap(x, bit):
    return swap(x, "core", 1) if bit == 1 else swap(x, "y", bit // 2)


def split_parts(x, parts):
    out, rest = [], x
    for _ in range(parts):
        piece = rest.astype(BF16)
        out.append(piece)
        rest = rest - piece.astype(F32)
    return out


def pool_kernel(heads, chan_count, first, count, per_owner, taken, place, tokens, *rest):
    if taken is not None:
        whole, rest = rest[0], rest[1:]
    added, live, rest = rest[0], rest[1], rest[2:]
    key_refs = rest[:chan_count]
    pooled_out, top_out, sum_out = rest[chan_count : chan_count + 3]
    rest = rest[chan_count + 3 :]
    if taken is not None:
        out_rows, rest = rest[0], rest[1:]
    held, arrived, pooled, stored, keys, add_scores, scores, spreads = rest[:8]
    if taken is not None:
        held_rows, rows_in, rows_out = rest[8:]
        copy_in = pltpu.make_async_copy(
            whole.at[pl.ds(taken, out_rows.shape[0]), :], held_rows, rows_in
        )
        copy_out = pltpu.make_async_copy(held_rows, out_rows, rows_out)
    slots, _, width = tokens.shape
    block = held.shape[2]
    rows = slots * block
    lanes = scores.shape[1]
    groups = lanes // LANES
    padded = added.shape[0]

    def fetch(i):
        at = first + i
        row = (((at // per_owner) ^ place[0]) * per_owner + at % per_owner) * block
        return pltpu.make_async_copy(
            tokens.at[:, pl.ds(pl.multiple_of(row, block), block), :],
            held.at[i],
            arrived.at[i],
        )

    fetch(0).start()
    if count > 1:
        fetch(1).start()

    piece = width // chan_count
    for j in range(chan_count):
        at = pl.multiple_of(place[1 + j] * piece, piece)
        high, low = split_parts(key_refs[j][...], 2)
        keys[:, pl.ds(at, piece)] = jnp.concatenate([high, low], axis=0)
    raw = lax.dot_general(keys[...], added[...], NT, preferred_element_type=F32)
    raw = raw[:heads] + raw[heads:]
    lane = lax.broadcasted_iota(jnp.int32, (padded, lanes), 1)
    slot = lax.broadcasted_iota(jnp.int32, (padded, lanes), 0)
    expand = jnp.where(lane // block == slot, 1.0, 0.0).astype(BF16)
    total = jnp.zeros((heads, lanes), F32)
    for part in split_parts(raw, 3):
        total = total + jnp.dot(part, expand, preferred_element_type=F32)
    add_scores[...] = total
    scores[...] = jnp.zeros_like(scores)

    def fold(x, combine):
        out = x[:, :LANES]
        for g in range(1, groups):
            out = combine(out, x[:, g * LANES : (g + 1) * LANES])
        shift = LANES // 2
        while shift >= block:
            out = combine(out, pltpu.roll(out, shift, 1))
            shift //= 2
        return out

    def store(i):
        return pltpu.make_async_copy(
            pooled.at[i], pooled_out.at[:, pl.ds(i * block, block), :], stored.at[i]
        )

    step = min(width, 512)
    by_slot = None
    for i in range(count + 1):
        if i < count:
            fetch(i).wait()
            if i + 2 < count:
                fetch(i + 2).start()
        raw = None
        for at in range(0, width, step):
            if i < count:
                part = held[i, :, :, at : at + step].reshape(rows, step)
                got = lax.dot_general(
                    keys[:, at : at + step], part, NT, preferred_element_type=F32
                )
                raw = got if raw is None else raw + got
            if i > 0:
                part = held[i - 1, :, :, at : at + step].reshape(rows, step)
                got = jnp.dot(spreads[:, :rows], part, preferred_element_type=F32)
                got = got + jnp.dot(
                    by_slot, added[:, at : at + step], preferred_element_type=F32
                )
                pooled[i - 1, :, :, at : at + step] = got.reshape(heads, block, step).astype(BF16)
        if i > 0:
            store(i - 1).start()
        if i == 1 and taken is not None:
            copy_in.start()
        if i == count - 1 and taken is not None:
            copy_in.wait()
            copy_out.start()
        if i == count:
            break
        scores[:, :rows] = raw[:heads] + raw[heads:]
        alive = live[...] > 0.0
        masked = jnp.where(alive, scores[...] + add_scores[...], NEG)
        top = fold(masked, jnp.maximum)
        wide_top = jnp.concatenate([top] * groups, axis=1)
        weights = jnp.where(alive, jnp.exp(masked - wide_top), 0.0)
        weights = weights.astype(BF16).astype(F32)
        top_out[i] = top
        sum_out[i] = fold(weights, jnp.add)
        patch = lax.broadcasted_iota(jnp.int32, (heads, block, lanes), 1)
        column = lax.broadcasted_iota(jnp.int32, (heads, block, lanes), 2)
        spread = jnp.where(
            column % block == patch, jnp.broadcast_to(weights[:, None, :], patch.shape), 0.0
        )
        spread = spread.reshape(heads * block, lanes).astype(BF16)
        spreads[...] = spread
        pick = jnp.where(
            lax.broadcasted_iota(jnp.int32, (lanes, padded), 0) // block
            == lax.broadcasted_iota(jnp.int32, (lanes, padded), 1),
            1.0,
            0.0,
        ).astype(BF16)
        by_slot = jnp.dot(spread, pick, preferred_element_type=F32).astype(BF16)
    for i in range(count):
        store(i).wait()
    if taken is not None:
        copy_out.wait()


def pool_tokens(tokens, added, live, key_parts, place, heads, rows_own, first, count, take=None):
    slots, _, width = tokens.shape
    lanes = live.shape[1]
    vmem, hbm = (pl.BlockSpec(memory_space=m) for m in (pltpu.VMEM, pltpu.HBM))
    extra_in, extra_out, extra_scratch, taken = [], [], [], None
    if take is not None:
        whole, taken = take
        extra_in = [pltpu.with_memory_space_constraint(whole, pltpu.HBM)]
        extra = (whole.shape[0] - taken, whole.shape[1])
        extra_out = [pltpu.HBM(extra, whole.dtype)]
        extra_scratch = [pltpu.VMEM(extra, whole.dtype)] + [pltpu.SemaphoreType.DMA] * 2
    return pl.pallas_call(
        functools.partial(
            pool_kernel, heads, len(key_parts), first, count, max(rows_own // BLOCK, 1), taken
        ),
        out_shape=[
            pltpu.HBM((heads, count * BLOCK, width), BF16),
            jax.ShapeDtypeStruct((count, heads, LANES), F32),
            jax.ShapeDtypeStruct((count, heads, LANES), F32),
        ]
        + extra_out,
        in_specs=[pl.BlockSpec(memory_space=pltpu.SMEM), hbm]
        + [hbm] * len(extra_in)
        + [vmem] * (2 + len(key_parts)),
        out_specs=[hbm, vmem, vmem] + [hbm] * len(extra_out),
        scratch_shapes=[
            pltpu.VMEM((count, slots, BLOCK, width), BF16),
            pltpu.SemaphoreType.DMA((count,)),
            pltpu.VMEM((count, heads, BLOCK, width), BF16),
            pltpu.SemaphoreType.DMA((count,)),
            pltpu.VMEM((2 * heads, width), BF16),
            pltpu.VMEM((heads, lanes), F32),
            pltpu.VMEM((heads, lanes), F32),
            pltpu.VMEM((heads * BLOCK, lanes), BF16),
        ]
        + extra_scratch,
        compiler_params=pltpu.CompilerParams(
            vmem_limit_bytes=3 * MIB + count * (slots + heads) * BLOCK * width * 2
        ),
        cost_estimate=cost(
            count * slots * BLOCK * width * 1024, count * (slots + heads) * BLOCK * width * 2
        ),
        name="pool_tokens",
    )(
        place,
        pltpu.with_memory_space_constraint(tokens, pltpu.HBM),
        *extra_in,
        added,
        live,
        *key_parts,
    )


def value_kernel(together, pool_count, piece_count, has_start, has_factor, offsets, *rest):
    pooled, rest = rest[:pool_count], rest[pool_count:]
    pieces, rest = rest[:piece_count], rest[piece_count:]
    total = None
    for n, piece in enumerate(pieces):
        depth = piece.shape[0]
        at = pl.multiple_of(offsets[1 + n], LANES)
        stacked = jnp.concatenate(
            [part[h, :, pl.ds(at, depth)] for h in range(together) for part in pooled],
            axis=0,
        )
        got = jnp.dot(stacked, piece[...], preferred_element_type=F32)
        total = got if total is None else total + got
    patches = total.shape[0] // together
    out = rest[-1]
    for h in range(together):
        columns = slice(h * HEAD_DIM, (h + 1) * HEAD_DIM)
        got = total[h * patches : (h + 1) * patches, columns]
        if has_start:
            got = got + rest[0][:, columns]
        if has_factor:
            got = got * rest[-2][h]
        out[:, columns] = got.astype(out.dtype)


def value_products(pooled, window, pieces, offsets, first_head, head_count, start, factor, kind):
    patches, width = sum(part.shape[1] for part in pooled), pooled[0].shape[2]
    together = 2 if head_count % 2 == 0 else 1
    wide = together * HEAD_DIM
    first = first_head // together
    specs = [
        pl.BlockSpec((together, part.shape[1], window), lambda h, o: (first + h, 0, o[0]))
        for part in pooled
    ]
    operands = [pltpu.with_memory_space_constraint(part, pltpu.HBM) for part in pooled]
    for piece in pieces:
        specs.append(pl.BlockSpec((piece.shape[0], wide), lambda h, o: (0, first + h)))
        operands.append(piece)
    if start is not None:
        specs.append(pl.BlockSpec((patches, wide), lambda h, o: (0, first + h)))
        operands.append(start)
    if factor is not None:
        specs.append(pl.BlockSpec((together, patches, HEAD_DIM), lambda h, o: (first + h, 0, 0)))
        operands.append(factor)
    return pl.pallas_call(
        functools.partial(
            value_kernel,
            together,
            len(pooled),
            len(pieces),
            start is not None,
            factor is not None,
        ),
        out_shape=jax.ShapeDtypeStruct((patches, head_count * HEAD_DIM), kind),
        grid_spec=pltpu.PrefetchScalarGridSpec(
            num_scalar_prefetch=1,
            grid=(head_count // together,),
            in_specs=specs,
            out_specs=pl.BlockSpec((patches, wide), lambda h, o: (0, h)),
        ),
        compiler_params=pltpu.CompilerParams(vmem_limit_bytes=14 * MIB),
        cost_estimate=cost(
            4 * patches * width * head_count * HEAD_DIM, sum(x.size * 2 for x in operands)
        ),
        name="value_products",
    )(offsets, *operands)


def take_kernel(at, whole, out, held, arrived, left):
    rows = pl.ds(pl.multiple_of(at[0], 16), out.shape[0])
    copy = pltpu.make_async_copy(whole.at[rows, :], held, arrived)
    copy.start()
    copy.wait()
    copy = pltpu.make_async_copy(held, out, left)
    copy.start()
    copy.wait()


def take_rows(whole, at, count):
    return pl.pallas_call(
        take_kernel,
        out_shape=pltpu.HBM((count, whole.shape[1]), whole.dtype),
        in_specs=[pl.BlockSpec(memory_space=pltpu.SMEM), pl.BlockSpec(memory_space=pltpu.HBM)],
        out_specs=pl.BlockSpec(memory_space=pltpu.HBM),
        scratch_shapes=[
            pltpu.VMEM((count, whole.shape[1]), whole.dtype),
            pltpu.SemaphoreType.DMA,
            pltpu.SemaphoreType.DMA,
        ],
        compiler_params=pltpu.CompilerParams(vmem_limit_bytes=2 * MIB),
        name="take_rows",
    )(jnp.reshape(at, (1,)), pltpu.with_memory_space_constraint(whole, pltpu.HBM))


def load_kernel(firsts, *refs):
    half = len(refs) // 2
    arrived = refs[-1]
    copies = []
    for i in range(half):
        rows = pl.ds(firsts[i], refs[half + i].shape[0])
        copies.append(
            pltpu.make_async_copy(refs[i].at[rows, :], refs[half + i], arrived.at[i])
        )
    for copy in copies:
        copy.start()
    for copy in copies:
        copy.wait()


def load_rows(*ranges):
    weights = [w for w, _, _ in ranges]
    shapes = [(count, w.shape[1]) for w, _, count in ranges]
    return pl.pallas_call(
        functools.partial(load_kernel, [first for _, first, _ in ranges]),
        out_shape=[pltpu.VMEM(shape, w.dtype) for shape, w in zip(shapes, weights)],
        in_specs=[pl.BlockSpec(memory_space=pltpu.HBM)] * len(weights),
        out_specs=[pl.BlockSpec(memory_space=pltpu.VMEM)] * len(weights),
        scratch_shapes=[pltpu.SemaphoreType.DMA((len(weights),))],
        compiler_params=pltpu.CompilerParams(vmem_limit_bytes=MIB),
        cost_estimate=cost(0, sum(2 * r * c for r, c in shapes)),
        name="load_weights",
    )(*[pltpu.with_memory_space_constraint(w, pltpu.HBM) for w in weights])


def load_weights(*weights):
    return load_rows(*[(w, 0, w.shape[0]) for w in weights])


def window_kernel(count, at, *refs):
    parts, outs, arrived = refs[:count], refs[count : 2 * count], refs[-1]
    copies = []
    for n in range(count):
        columns = pl.ds(pl.multiple_of(at[0], outs[n].shape[2]), outs[n].shape[2])
        copies.append(
            pltpu.make_async_copy(parts[n].at[:, :, columns], outs[n], arrived.at[n])
        )
    for copy in copies:
        copy.start()
    for copy in copies:
        copy.wait()


def load_window(parts, at, window):
    size = sum(part.size // part.shape[2] * window * 2 for part in parts)
    return pl.pallas_call(
        functools.partial(window_kernel, len(parts)),
        out_shape=[pltpu.VMEM((*part.shape[:2], window), part.dtype) for part in parts],
        in_specs=[pl.BlockSpec(memory_space=pltpu.SMEM)]
        + [pl.BlockSpec(memory_space=pltpu.HBM)] * len(parts),
        out_specs=[pl.BlockSpec(memory_space=pltpu.VMEM)] * len(parts),
        scratch_shapes=[pltpu.SemaphoreType.DMA((len(parts),))],
        compiler_params=pltpu.CompilerParams(vmem_limit_bytes=MIB),
        cost_estimate=pl.CostEstimate(flops=0, transcendentals=0, bytes_accessed=size),
        name="load_window",
    )(jnp.reshape(at, (1,)), *[pltpu.with_memory_space_constraint(p, pltpu.HBM) for p in parts])


def late_kernel(pool_count, piece_count, offsets, *rest):
    pooled, rest = rest[:pool_count], rest[pool_count:]
    pieces, (start, factor, out) = rest[:piece_count], rest[piece_count:]
    patches = out.shape[0]
    heads = out.shape[1] // HEAD_DIM
    together = 2 if heads % 2 == 0 else 1
    wide = together * HEAD_DIM
    for head in range(0, heads, together):
        first = head * HEAD_DIM
        total = None
        for n, piece in enumerate(pieces):
            depth = piece.shape[0]
            at = pl.multiple_of(offsets[n], LANES)
            stacked = jnp.concatenate(
                [part[head + h, :, pl.ds(at, depth)] for h in range(together) for part in pooled],
                axis=0,
            )
            got = jnp.dot(stacked, piece[:, first : first + wide], preferred_element_type=F32)
            total = got if total is None else total + got
        for h in range(together):
            columns = slice(first + h * HEAD_DIM, first + (h + 1) * HEAD_DIM)
            got = total[h * patches : (h + 1) * patches, h * HEAD_DIM : (h + 1) * HEAD_DIM]
            got = (got + start[:, columns]) * factor[:, head + h : head + h + 1]
            out[:, columns] = got.astype(out.dtype)


def late_products(pooled, pieces, offsets, start, factor):
    patches = sum(part.shape[1] for part in pooled)
    heads = pooled[0].shape[0]
    vmem = pl.BlockSpec(memory_space=pltpu.VMEM)
    depth = sum(piece.shape[0] for piece in pieces)
    return pl.pallas_call(
        functools.partial(late_kernel, len(pooled), len(pieces)),
        out_shape=jax.ShapeDtypeStruct((patches, heads * HEAD_DIM), BF16),
        in_specs=[pl.BlockSpec(memory_space=pltpu.SMEM)]
        + [vmem] * (len(pooled) + len(pieces) + 2),
        out_specs=vmem,
        compiler_params=pltpu.CompilerParams(vmem_limit_bytes=8 * MIB),
        cost_estimate=cost(
            4 * patches * depth * heads * HEAD_DIM, sum(piece.size * 2 for piece in pieces)
        ),
        name="late_products",
    )(
        offsets,
        *[pltpu.with_memory_space_constraint(part, pltpu.VMEM) for part in pooled],
        *pieces,
        start,
        factor,
    )


def project_kernel(own, stats, got, weights, *outs):
    columns, count = own.shape[1], stats.shape[1]
    _, total, mine, theirs = join_stats(stats[...], unpack_stats(got[...], columns, count))
    mine, theirs = mine / total, theirs / total
    rows = []
    for h in range(count // 2):
        at = slice(h * HEAD_DIM, (h + 1) * HEAD_DIM)
        row = own[:, at].astype(F32) * mine[:, h : h + 1]
        row = row + got[:, at].astype(F32) * theirs[:, h : h + 1]
        rows.append(row.astype(BF16))
    rows = jnp.concatenate(rows, axis=1)
    found = jnp.dot(rows, weights[...], preferred_element_type=F32)
    for out in outs:
        out[...] = found.astype(out.dtype)


def project(own, stats, got, weights, guess, kinds):
    vmem = pl.BlockSpec(memory_space=pltpu.VMEM)
    shape = (own.shape[0], weights.shape[1])
    return pl.pallas_call(
        project_kernel,
        out_shape=[jax.ShapeDtypeStruct(shape, kind) for kind in kinds],
        in_specs=[vmem] * 4,
        out_specs=[vmem] * len(kinds),
        compiler_params=pltpu.CompilerParams(vmem_limit_bytes=4 * MIB),
        cost_estimate=cost(guess, own.size * 4),
        name="project",
    )(own, stats, got, pltpu.with_memory_space_constraint(weights, pltpu.VMEM))


def add_kernel(left, right, out):
    out[...] = (left[...].astype(F32) + right[...].astype(F32)).astype(out.dtype)


def add_rows(left, right, guess):
    vmem = pl.BlockSpec(memory_space=pltpu.VMEM)
    return pl.pallas_call(
        add_kernel,
        out_shape=jax.ShapeDtypeStruct(left.shape, left.dtype),
        in_specs=[vmem] * 2,
        out_specs=vmem,
        compiler_params=pltpu.CompilerParams(vmem_limit_bytes=4 * MIB),
        cost_estimate=cost(guess, left.size * 6),
        name="add_rows",
    )(left, right)


def down_columns(hidden, order, parts, n):
    piece = parts[0].shape[1] // order.shape[0]
    at = pl.multiple_of(order[n] * piece, piece)
    total, row = None, 0
    for part in parts:
        depth = part.shape[0]
        mine = hidden[:, row : row + depth]
        got = jnp.dot(mine, part[:, pl.ds(at, piece)], preferred_element_type=F32)
        total, row = got if total is None else total + got, row + depth
    return total.astype(BF16)


def mlp_kernel(count, chunks, outs, downs, order, *refs):
    xs = refs[: count * chunks]
    gain, w_up, *rest = refs[count * chunks :]
    w_down, (*found, hidden, normed) = rest[:downs], rest[downs:]
    piece = xs[0].shape[1]
    width = count * piece
    at_row = 0
    for chunk in range(chunks):
        x = xs[chunk * count : (chunk + 1) * count]
        rows = x[0].shape[0]
        mean = jnp.zeros((rows, 1), F32)
        for j in range(count):
            mean = mean + jnp.sum(x[j][...].astype(F32), axis=1, keepdims=True)
        mean = mean / width
        variance = jnp.zeros((rows, 1), F32)
        for j in range(count):
            centered = x[j][...].astype(F32) - mean
            variance = variance + jnp.sum(centered * centered, axis=1, keepdims=True)
        scale = lax.rsqrt(variance / width + 1e-05)
        for j in range(count):
            got = ((x[j][...].astype(F32) - mean) * scale * gain[order[j]]).astype(BF16)
            normed[j, at_row : at_row + rows, :] = got
        at_row += rows
    total = None
    for j in range(count):
        at = pl.multiple_of(order[j] * piece, piece)
        got = jnp.dot(normed[j], w_up[pl.ds(at, piece), :], preferred_element_type=F32)
        total = got if total is None else total + got
    active = jax.nn.gelu(total).astype(BF16)
    hidden[...] = active
    for n in range(outs):
        found[n][...] = down_columns(active, order, w_down, n)


def mlp(xs, order, ln_gain, w_up, w_down, outs):
    count, piece = len(xs[0]), xs[0][0].shape[1]
    patches = sum(x[0].shape[0] for x in xs)
    vmem = pl.BlockSpec(memory_space=pltpu.VMEM)
    w_up, *w_down = (pltpu.with_memory_space_constraint(w, pltpu.VMEM) for w in (w_up, *w_down))
    flat = [x for chunk in xs for x in chunk]
    *found, hidden = pl.pallas_call(
        functools.partial(mlp_kernel, count, len(xs), outs, len(w_down)),
        out_shape=[jax.ShapeDtypeStruct((patches, piece), BF16)] * outs
        + [jax.ShapeDtypeStruct((patches, w_up.shape[1]), BF16)],
        in_specs=[pl.BlockSpec(memory_space=pltpu.SMEM)] + [vmem] * (len(flat) + 2 + len(w_down)),
        out_specs=[vmem] * (outs + 1),
        scratch_shapes=[pltpu.VMEM((count, patches, piece), BF16)],
        compiler_params=pltpu.CompilerParams(vmem_limit_bytes=8 * MIB),
        name="norm_mlp",
    )(order, *flat, ln_gain.reshape(count, 1, piece), w_up, *w_down)
    return found, hidden


def down_kernel(first, downs, order, hidden, *refs):
    for n, out in enumerate(refs[downs:]):
        out[...] = down_columns(hidden[...], order, refs[:downs], first + n)


def down(hidden, order, w_down, first, last):
    vmem = pl.BlockSpec(memory_space=pltpu.VMEM)
    shape = (hidden.shape[0], w_down[0].shape[1] // last)
    return pl.pallas_call(
        functools.partial(down_kernel, first, len(w_down)),
        out_shape=[jax.ShapeDtypeStruct(shape, BF16)] * (last - first),
        in_specs=[pl.BlockSpec(memory_space=pltpu.SMEM)] + [vmem] * (1 + len(w_down)),
        out_specs=[vmem] * (last - first),
        compiler_params=pltpu.CompilerParams(vmem_limit_bytes=4 * MIB),
        cost_estimate=cost(2e9, hidden.size * 2),
        name="down",
    )(order, hidden, *[pltpu.with_memory_space_constraint(w, pltpu.VMEM) for w in w_down])


def key_vectors(query, w_key, heads):
    columns = query.shape[0]
    mine = jnp.arange(columns)[None, :] // HEAD_DIM == jnp.arange(heads)[:, None]
    rows = [jnp.where(mine, part[None, :], 0) for part in exact_parts(query)]
    stacked = jnp.concatenate(rows, axis=0).astype(BF16)
    got = lax.dot_general(stacked, w_key, NT, preferred_element_type=F32)
    scale = 1.0 / jnp.sqrt(F32(HEAD_DIM))
    return (got.reshape(3, heads, -1).sum(axis=0)) * scale


def add_up(*terms):
    total = terms[0].astype(F32)
    for term in terms[1:]:
        total = total + term.astype(F32)
    return total


def local(
    tokens, chan_table, chan_valid, chan_embed, query, w_key, w_value, w_out, ln_gain, w_up, w_down
):
    slots, patches, width = tokens.shape
    columns = query.shape[0]
    heads = columns // HEAD_DIM
    group, tensor = lax.axis_index("group"), lax.axis_index("tensor")
    tensors = lax.axis_size("tensor")
    chan = lax.axis_index(("y", "core"))
    chans = lax.axis_size("y") * lax.axis_size("core")
    chan_bits = [1] + [2 * b for b in bits_of("y")]
    tensor_bits = bits_of("tensor")
    rows_own = patches // tensors

    key_parts = key_vectors(query, w_key, heads)[None]
    key_order = [0]
    weights = w_value
    for bit in chan_bits:
        key_parts = jnp.concatenate([key_parts, chan_swap(key_parts, bit)], axis=0)
        key_order = key_order + [j ^ bit for j in key_order]
        if bit == 1:
            key_parts, weights = lax.optimization_barrier((key_parts, weights))
    key_place = chan ^ jnp.array(key_order, jnp.int32)
    place = jnp.concatenate([jnp.reshape(tensor, (1,)).astype(jnp.int32), key_place])

    padded = -(-slots // 16) * 16
    lanes = -(-(slots * BLOCK) // LANES) * LANES
    slot_ids = lax.dynamic_slice_in_dim(chan_table, chan * slots, slots)
    slot_ids = jnp.pad(slot_ids, (0, padded - slots), constant_values=-1)
    matches = slot_ids[:, None] == jnp.arange(chan_embed.shape[0], dtype=jnp.int32)[None, :]
    added = jnp.dot(matches.astype(BF16), chan_embed, preferred_element_type=F32).astype(BF16)
    live_slots = jnp.sum(matches.astype(jnp.int32) * chan_valid[None, :], axis=1) > 0
    live = jnp.repeat(live_slots.astype(F32), BLOCK)
    live = jnp.pad(live, (0, max(lanes - live.shape[0], 0)))[:lanes][None]

    blocks = patches // BLOCK
    spread_groups = lax.axis_size("y") == 2 and lax.axis_size("group") == 2
    cut = 3 * blocks // 4

    def pool(keys, added, where, first, count, take=None):
        keys = [keys[j] for j in range(chans)]
        return pool_tokens(
            tokens, added, live, keys, where, heads, rows_own, first, count, take
        )

    if spread_groups:
        rows = w_value.shape[0]
        share = 3 * rows // 8
        mine = take_rows(weights, group * share, share)
        key_parts, mine, added, live = lax.optimization_barrier((key_parts, mine, added, live))
        one = swap(mine, "y")
        near = swap(w_value, "core")
        *first_pool, straight = pool(key_parts, added, place, 0, cut, (weights, 2 * share))
        one, first_pool, late_place, straight = lax.optimization_barrier(
            (one, first_pool, place, straight)
        )
        two = swap(one, "group")
        three = swap(straight, "y")
        one_across = swap(one, "core")
        second_pool = pool(key_parts, added, late_place, cut, blocks - cut)
        found = (first_pool, second_pool)
    else:
        full = lax.all_gather(w_value, ("y", "core"), axis=0, tiled=True)
        found = [
            pool(key_parts, added, place, at, n) for at, n in ((0, cut), (cut, blocks - cut))
        ]

    pooled = [part[0] for part in found]
    tops = jnp.concatenate([part[1] for part in found])
    sums = jnp.concatenate([part[2] for part in found])
    top = tops[:, :, :BLOCK].transpose(1, 0, 2).reshape(heads, patches)
    weight_sum = sums[:, :, :BLOCK].transpose(1, 0, 2).reshape(heads, patches)
    stats = jnp.stack([top, weight_sum])
    other = swap(stats, "core")
    stats, other, pooled = lax.optimization_barrier((stats, other, pooled))
    best = jnp.maximum(stats[0], other[0])
    factor = jnp.exp(top - best)
    total = stats[1] * factor + other[1] * jnp.exp(other[0] - best)
    stats = jnp.concatenate([best, total], axis=0).T

    if spread_groups:
        own_at, near_at, far, across = (jnp.int32(chan ^ j) * rows for j in range(4))
        starts = [jnp.int32(0), own_at, near_at, far + group * share, across + group * share]
        pieces = [w_value, near, one, one_across]
        start = value_products(
            pooled, width, pieces, jnp.stack(starts), 0, heads, None, None, F32
        )
        two, three, start = lax.optimization_barrier((two, three, start))
        pieces = [two, three, swap(two, "core"), swap(three, "core")]
        window, side = 2 * rows, jnp.int32(1 - chan // 2)
        starts = []
        for base in (far - side * window, across - side * window):
            starts += [base + (1 - group) * share, base + 2 * share]
        pooled, start = lax.optimization_barrier((pooled, start))
        loaded = load_window(pooled, side * window, window)
        pieces, loaded = lax.optimization_barrier((pieces, loaded))
        value = late_products(loaded, pieces, jnp.stack(starts), start, factor.T)
    else:
        value = value_products(
            pooled,
            width,
            [full],
            jnp.zeros((2,), jnp.int32),
            0,
            heads,
            None,
            jnp.broadcast_to(factor[:, :, None], (heads, patches, HEAD_DIM)),
            BF16,
        )

    low = tensors // 2
    chunks = [list(range(low, tensors)), list(range(low))]
    split = lambda x: [x[ks[0] * rows_own : (ks[-1] + 1) * rows_own] for ks in chunks]
    value = add_up(value, swap(value, "core")).astype(BF16)
    value, w_out, w_up = lax.optimization_barrier((value, w_out, w_up))
    values, stats = split(value), split(stats)
    for bit in chan_bits[1:]:
        found = [chan_swap(pack(v, st), bit) for v, st in zip(values, stats)]
        if bit == chan_bits[-1]:
            found[0], w_out, w_up = lax.optimization_barrier(
                (found[0], *load_weights(w_out, w_up))
            )
            (far_out,) = project(values[0], stats[0], found[0], w_out, 1e9, (BF16,))
            _, w_down = lax.optimization_barrier((far_out, w_down))
            cut = w_down.shape[0] // 4
            (w_first,) = load_rows((w_down, 0, cut))
            found[1], w_first = lax.optimization_barrier((found[1], w_first))
            low_out, low_sent = project(
                values[1], stats[1], found[1], w_out, LONG, (F32, BF16)
            )
            break
        for n in range(2):
            theirs = unpack_stats(found[n], columns, stats[n].shape[1])
            best, total, *scales = join_stats(stats[n], theirs)
            stats[n] = jnp.concatenate([best, total], axis=1)
            scales = [jnp.repeat(scale, HEAD_DIM, axis=1) for scale in scales]
            joined = values[n] * scales[0] + found[n][:, :columns] * scales[1]
            values[n] = joined.astype(BF16)
    sent = list(low_sent.reshape(low, rows_own, -1))
    sent += list(far_out.reshape(tensors - low, rows_own, -1))
    got = [swap(sent[k], "tensor", k) for k in range(1, tensors)]
    projected = add_up(low_out[:rows_own], *got)
    own = projected.astype(BF16)

    arrived = [own] + [swap(own, "tensor", k) for k in range(1, tensors)]
    low_rows, w_down = lax.optimization_barrier((arrived[:low], w_down))
    far_rows, w_rest = lax.optimization_barrier(
        (arrived[low:], *load_rows((w_down, cut, w_down.shape[0] - cut)))
    )
    w_down = [w_first, w_rest]
    gathered = []
    for pieces in (low_rows, far_rows):
        found = {0: jnp.concatenate(pieces, axis=0)}
        for bit in chan_bits[1:] + chan_bits[:1]:
            found.update({j ^ bit: chan_swap(found[j], bit) for j in list(found)})
        gathered.append(found)
    order = list(gathered[0])
    first = [j for j in order if j & chan_bits[-1]]
    order = first + [j for j in order if j not in first]
    places = chan ^ jnp.array(order, jnp.int32)
    xs = [[found[j] for j in order] for found in gathered]
    parts, hidden = mlp(xs, places, ln_gain, w_up, w_down, len(first))
    parts += down(hidden, places, w_down, len(first), len(order))
    held = dict(zip(order, parts))
    keep = [j for j in order if not j & 1]
    passed = {j: swap(held[j ^ 1], "core") for j in keep}
    held = {j: add_up(held[j], passed[j]).astype(BF16) for j in keep}
    parts = {j: split(x) for j, x in held.items()}
    for bit in chan_bits[1:]:
        keep = sorted(j for j in parts if not j & bit)
        passed = [chan_swap(jnp.stack([parts[j ^ bit][n] for j in keep]), bit) for n in (0, 1)]
        far = [add_up(parts[j][0], passed[0][n]).astype(BF16) for n, j in enumerate(keep)]
        near = [add_rows(parts[j][1], passed[1][n], LONG) for n, j in enumerate(keep)]
        parts = {j: [far[n], near[n]] for n, j in enumerate(keep)}
    got = [
        swap(x, "tensor", k) for k, x in zip(chunks[0], parts[0][0].reshape(low, rows_own, -1))
    ]
    sent = parts[0][1].reshape(low, rows_own, -1)
    got += [swap(sent[k], "tensor", k) for k in range(1, low)]
    return add_up(projected, sent[0], *got).astype(BF16)


def solution(mesh):
    groups, chans, tensors = (mesh.shape[a] for a in ("group", "chan", "tensor"))
    split = Mesh(
        mesh.devices.reshape(groups, chans // 2, 2, tensors), ("group", "y", "core", "tensor")
    )
    chan = ("y", "core")
    in_specs = (
        P(chan, "group", None),
        P(),
        P(),
        P(),
        P("tensor"),
        P(chan, "tensor"),
        P(chan, "tensor"),
        P("tensor", chan),
        P(),
        P(None, (*chan, "tensor")),
        P((*chan, "tensor"), None),
    )
    out_specs = P(("group", "tensor"), chan)
    return jax.shard_map(
        local, mesh=split, in_specs=in_specs, out_specs=out_specs, check_vma=False
    )
```
